32 devices in a mesh: dp: 4 (over y, x), expert: 8 (over z, core).
Axes of the slice: x: 2, y: 2, z: 4, core: 2. Of those that a mesh axis runs over, the one named last changes fastest.
Arguments:
- tokens: bfloat16 [8192, 768], P(('dp', 'expert')), may hold values from -6 to 6
- cotangent: float32 [8192, 768], P(('dp', 'expert')), may hold values from -6 to 6
- buckets: int32 [256, 256], replicated, may hold values from 0 to 31
- routes: int32 [8192, 2], P(('dp', 'expert')), may hold values from 0 to 15, all different within a row; in each aligned block of 256 rows (0 to 255, 256 to 511, ...) at most 36 rows name the same one
- gain_attn: bfloat16 [768], P(('dp', 'expert')), may hold values from 0.5 to 1.5
- gain_moe: bfloat16 [768], P(('dp', 'expert')), may hold values from 0.5 to 1.5
- rel_bias: bfloat16 [384], P(('dp', 'expert')), may hold values from -6 to 256
- w_query: bfloat16 [768, 768], P(('dp', 'expert')), may hold values from -0.21875 to 0.21875
- w_key: bfloat16 [768, 768], P(('dp', 'expert')), may hold values from -0.21875 to 0.21875
- w_value: bfloat16 [768, 768], P(('dp', 'expert')), may hold values from -0.21875 to 0.21875
- w_out: bfloat16 [768, 768], P(('dp', 'expert')), may hold values from -0.625 to 0.625
- w_router: bfloat16 [768, 16], P(('dp', 'expert')), may hold values from -18 to 18
- w_gate: bfloat16 [16, 768, 3072], P('expert', None, 'dp'), may hold values from -0.21875 to 0.21875
- w_up: bfloat16 [16, 768, 3072], P('expert', None, 'dp'), may hold values from -0.21875 to 0.21875
- w_down: bfloat16 [16, 768, 3072], P('expert', None, 'dp'), may hold values from -0.15625 to 0.15625
Outputs:
- layer_out: float32 [8192, 768], P(('dp', 'expert'))
- tokens_grad: float32 [8192, 768], P(('dp', 'expert'))
- gain_attn_grad: float32 [768], P(('dp', 'expert'))
- gain_moe_grad: float32 [768], P(('dp', 'expert'))
- rel_bias_grad: float32 [384], P(('dp', 'expert'))
- query_weight_grad: float32 [768, 768], P(('dp', 'expert'))
- key_weight_grad: float32 [768, 768], P(('dp', 'expert'))
- value_weight_grad: float32 [768, 768], P(('dp', 'expert'))
- out_weight_grad: float32 [768, 768], P(('dp', 'expert'))
- router_grad: float32 [768, 16], P(('dp', 'expert'))
- gate_grad: float32 [16, 768, 3072], P('expert', None, 'dp')
- up_grad: float32 [16, 768, 3072], P('expert', None, 'dp')
- down_grad: float32 [16, 768, 3072], P('expert', None, 'dp')
The draws below stay inside these ranges and needn't reach their ends.
Inputs may be any that keep to these rules, and one draw needn't show every extreme that they name: `routes`: in each aligned block of 256 rows (the rows of one device) no expert is named by more than 36 rows, a bound that some block reaches; the two experts of a row differ.
All inputs are finite; a program needn't handle non-finite values.
Results may differ from the reference program's by a relative error of at most 0.015.
The reference program's roundings to bfloat16 on the way count: a program that leaves them out, or rounds other values in their place, can miss the bound.
Values may be sent and summed in bfloat16 or wider, within the bound.
No kernel may reach another device: no remote copies, remote signals or barrier semaphores. Data moves between devices by JAX's collectives and lax.ppermute only.
A program may use at most 192 MiB of HBM per device.

```python
import math
import jax
import jax.numpy as jnp
import numpy as np
from jax import lax

D = 768
H = 12
DH = 64
FF = 3072
NB = 32
SEQ = 256
TOK_DEV = 256
TOKENS = 8192
EXPERTS = 16
CAP = 36
DEVICES = 32


def draw_rel_bias(key, part):
    base = jnp.clip(jax.random.normal(key, (NB * H,), jnp.float32), -6.0, 6.0)
    return base.astype(jnp.bfloat16)


def draw_w_router(key, part):
    first = jax.random.fold_in(key, 0)
    weight = jnp.clip(jax.random.normal(first, (D, EXPERTS), jnp.float32), -4.0, 4.0) * D ** (-0.5)
    return weight.astype(jnp.bfloat16)


def set_ends(array, own_key, least, high):
    extent = array.shape
    index_at = [jax.random.randint(jax.random.fold_in(own_key, axis), (), 0, extent[axis]) for axis in range(len(extent))]
    array = array.at[tuple(index_at)].set(least)
    longest = extent.index(max(extent))
    index_at[longest] = (index_at[longest] + 1) % extent[longest]
    return array.at[tuple(index_at)].set(high)


def block_levels(stream_key, shape, cuts, smallest, top_value):
    factor_of = 1.0
    for dim, blocks in cuts:
        heights = jax.random.uniform(jax.random.fold_in(jax.random.fold_in(stream_key, 6), dim), (blocks,), jnp.float32, smallest / len(cuts), top_value / len(cuts))
        factor_of = factor_of * jnp.repeat(jnp.exp(heights), shape[dim] // blocks).reshape((-1,) + (1,) * (len(shape) - 1 - dim))
    return factor_of


def assign_block(own_key, own, number, rows, count, top, limit, slope):
    order = jax.random.permutation(own_key, count)
    packed, usual = load_shares(count, rows * top, limit, slope, True), load_shares(count, rows * top, limit, slope, False)
    places = jnp.arange(count)

    def named(sizes, turn):
        used = int((sizes > 0).sum())
        fixed = max(1, used // 4)
        passed = fixed + (places - fixed + turn * (used - fixed)) % max(1, count - fixed)
        return jnp.zeros((count,), jnp.int32).at[order[jnp.where(places < fixed, places, passed)]].set(jnp.asarray(sizes, jnp.int32))

    sizes = jnp.where(number % 4 == 0, named(packed, number // 4), named(usual, number - number // 4 - 1))
    mixed = jax.random.permutation(jax.random.fold_in(own, 3), count)
    donor, receiver = mixed[0:count // 2 * 2:2], mixed[1:count // 2 * 2:2]
    slack = jnp.minimum(sizes[donor] - 1, limit - sizes[receiver]) // 2
    slack = jnp.where((donor == order[0]) | (receiver == order[0]) | (sizes[receiver] == 0), 0, jnp.maximum(slack, 0))
    passed = jax.random.randint(jax.random.fold_in(own, 4), (count // 2,), 0, 1 << 20) % (slack + 1)
    sizes = sizes.at[donor].add(-passed).at[receiver].add(passed)
    members = jnp.searchsorted(jnp.cumsum(sizes), jnp.arange(rows * top), side="right").astype(jnp.int32)
    table = members.reshape(top, rows).T
    table = table[jax.random.permutation(jax.random.fold_in(own, 1), rows)]
    turn = jax.random.randint(jax.random.fold_in(own, 2), (rows, 1), 0, top)
    return jnp.take_along_axis(table, (jnp.arange(top)[None, :] + turn) % top, axis=1)


def load_shares(number_of, total, limit, lean, full):
    weights = [(1 << 20) // math.isqrt(standing ** lean) + 1 for standing in range(1, number_of + 1)]
    largest = limit if full else min(limit, max(-(-total // number_of), total * weights[0] // sum(weights)))
    least = 1 if total - largest >= number_of - 1 else 0
    counts, surplus = [largest] + [least] * (number_of - 1), total - largest - least * (number_of - 1)
    while surplus > 0:
        candidates = [i for i in range(1, number_of) if counts[i] < largest] or [i for i in range(1, number_of) if counts[i] < limit]
        whole, remaining = sum([weights[i] for i in candidates]), surplus
        for i in candidates:
            extra = min(limit - counts[i], max(1, remaining * weights[i] // whole), surplus)
            counts[i] = counts[i] + extra
            surplus = surplus - extra
    return np.array(counts)


def centred(key, dims, deviation, limit, cuts=(), held_as=jnp.bfloat16):
    array = deviation * jax.random.normal(key, dims, jnp.float32)
    if cuts:
        array = array * block_levels(key, dims, cuts, -0.22, 0.18)
    return jnp.clip(array, -limit, limit).astype(held_as)


def setup_inputs(seed: int = 0) -> dict:
    key_list = jax.random.split(jax.random.key(seed), 16)
    tokens = centred(key_list[0], (TOKENS, D), 1.0, 6.0, ((0, 32),))
    cotangent = centred(key_list[1], (TOKENS, D), 1.0, 6.0, ((0, 32),), jnp.float32)
    buckets = set_ends(jax.random.randint(key_list[2], (SEQ, SEQ), 0, NB), jax.random.fold_in(key_list[2], 1), 0, NB - 1).astype(jnp.int32)
    routes_keys = jax.random.split(jax.random.fold_in(key_list[3], 1), TOKENS // TOK_DEV)
    routes_turns = jax.random.permutation(jax.random.fold_in(key_list[3], 3), TOKENS // TOK_DEV)
    routes = jax.vmap(lambda own, number: assign_block(jax.random.fold_in(key_list[3], 2), own, number, TOK_DEV, EXPERTS, 2, CAP, 2))(routes_keys, routes_turns).reshape((TOKENS, 2))
    gain_attn = jnp.clip(1.0 + 0.1 * jax.random.normal(key_list[4], (D,), jnp.float32), 0.5, 1.5).astype(jnp.bfloat16)
    gain_moe = jnp.clip(1.0 + 0.1 * jax.random.normal(key_list[5], (D,), jnp.float32), 0.5, 1.5).astype(jnp.bfloat16)
    rel_bias = draw_rel_bias(jax.random.fold_in(key_list[15], 71), 0)
    w_query = centred(key_list[7], (D, D), D ** -0.5, 0.21875, ((0, 32),))
    w_key = centred(key_list[8], (D, D), D ** -0.5, 0.21875, ((0, 32),))
    w_value = centred(key_list[9], (D, D), D ** -0.5, 0.21875, ((0, 32),))
    w_out = centred(key_list[10], (D, D), (D // 8) ** -0.5, 0.625, ((0, 32),))
    w_router = draw_w_router(jax.random.fold_in(key_list[15], 71), 0)
    w_gate = centred(key_list[12], (EXPERTS, D, FF), D ** -0.5, 0.21875, ((0, 8), (2, 4)))
    w_up = centred(key_list[13], (EXPERTS, D, FF), D ** -0.5, 0.21875, ((0, 8), (2, 4)))
    w_down = centred(key_list[14], (EXPERTS, D, FF), (FF // 2) ** -0.5, 0.15625, ((0, 8), (2, 4)))
    return {"tokens": tokens, "cotangent": cotangent, "buckets": buckets, "routes": routes, "gain_attn": gain_attn, "gain_moe": gain_moe, "rel_bias": rel_bias, "w_query": w_query, "w_key": w_key, "w_value": w_value, "w_out": w_out, "w_router": w_router, "w_gate": w_gate, "w_up": w_up, "w_down": w_down}


EPSILON = 1e-06

def rms_apply(hidden, gain):
    factor = lax.rsqrt(lax.optimization_barrier(jnp.mean(hidden * hidden, axis=-1, keepdims=True)) + EPSILON)
    return hidden * factor * gain

def geglu(gate_pre, up_pre):
    return jax.nn.gelu(gate_pre, approximate=True) * up_pre

def rounded(value):
    return lax.optimization_barrier(value.astype(jnp.bfloat16))

def matmul(left, right):
    return jnp.dot(left, right, preferred_element_type=jnp.float32)

def reference(tokens, cotangent, buckets, routes, gain_attn, gain_moe, rel_bias, w_query, w_key, w_value, w_out, w_router, w_gate, w_up, w_down):
    sequences = TOKENS // SEQ
    tokens_f = tokens.astype(jnp.float32)
    gain_one = gain_attn.astype(jnp.float32)
    gain_two = gain_moe.astype(jnp.float32)
    normed_one = rms_apply(tokens_f, gain_one).astype(jnp.bfloat16)

    def heads_of(flat):
        return flat.reshape(sequences, SEQ, H, DH)
    query4 = heads_of(matmul(normed_one, w_query).astype(jnp.bfloat16))
    key4 = heads_of(matmul(normed_one, w_key).astype(jnp.bfloat16))
    value4 = heads_of(matmul(normed_one, w_value).astype(jnp.bfloat16))
    bias_table = rel_bias.astype(jnp.float32).reshape(NB, H)
    bias_grid = jnp.transpose(bias_table[buckets], (2, 0, 1))
    causal = jnp.arange(SEQ)[:, None] >= jnp.arange(SEQ)[None, :]
    score_scale = 1.0 / math.sqrt(DH)

    def scores_of(query3, keys3):
        raw = jnp.einsum('qhd,khd->hqk', query3.astype(jnp.float32), keys3.astype(jnp.float32)) * score_scale + bias_grid
        return jnp.where(causal[None], raw, -1e+30)

    def forward_step(carry, items):
        query3, keys3, values3 = items
        scores = scores_of(query3, keys3)
        row_peak = lax.optimization_barrier(jnp.max(scores, axis=-1, keepdims=True))
        log_total = row_peak + jnp.log(lax.optimization_barrier(jnp.sum(jnp.exp(scores - row_peak), axis=-1, keepdims=True)))
        attn_weights = rounded(jnp.exp(scores - log_total))
        attended = jnp.einsum('hqk,khd->qhd', attn_weights.astype(jnp.float32), values3.astype(jnp.float32)).astype(jnp.bfloat16)
        return (carry, (attended, log_total))
    _, (attended4, log_totals) = lax.scan(forward_step, jnp.zeros((), jnp.float32), (query4, key4, value4))
    attended_flat = attended4.reshape(TOKENS, D)
    hidden_one = tokens_f + matmul(attended_flat, w_out)
    normed_two = rms_apply(hidden_one, gain_two).astype(jnp.bfloat16)
    logits = matmul(normed_two, w_router)
    chosen = jnp.take_along_axis(logits, routes, axis=1)
    gates = jax.nn.softmax(chosen, axis=-1)
    blocks = routes.reshape(DEVICES, TOK_DEV * 2)
    expert_hot = (blocks[:, :, None] == jnp.arange(EXPERTS, dtype=jnp.int32)[None, None, :]).astype(jnp.int32)
    earlier = jnp.cumsum(expert_hot, axis=1) - expert_hot
    position = lax.optimization_barrier(jnp.sum(earlier * expert_hot, axis=2))
    targets = (blocks * CAP + position).reshape(TOKENS, 2).astype(jnp.int32)
    device_of = (jnp.arange(TOKENS, dtype=jnp.int32) // TOK_DEV)[:, None]

    def to_experts(buffer):
        return buffer.reshape(DEVICES, EXPERTS, CAP, D).transpose(1, 0, 2, 3).reshape(EXPERTS, DEVICES * CAP, D)

    def to_devices(stack):
        return stack.reshape(EXPERTS, DEVICES, CAP, D).transpose(1, 0, 2, 3).reshape(DEVICES, EXPERTS * CAP, D)
    buffer = jnp.zeros((DEVICES, EXPERTS * CAP, D), jnp.bfloat16)
    buffer = buffer.at[device_of, targets].set(jnp.broadcast_to(normed_two[:, None, :], (TOKENS, 2, D)))
    expert_rows = to_experts(buffer)

    def expert_forward(items):
        rows, gate_w, up_w, down_w = items
        hidden_act = rounded(geglu(matmul(rows, gate_w), matmul(rows, up_w)))
        return matmul(hidden_act, down_w.T).astype(jnp.bfloat16)
    expert_out = to_devices(lax.map(expert_forward, (expert_rows, w_gate, w_up, w_down)))
    picked = expert_out[device_of, targets].astype(jnp.float32)
    layer_out = hidden_one + lax.optimization_barrier(jnp.sum(gates[:, :, None] * picked, axis=1))
    upstream = cotangent
    gate_back = lax.optimization_barrier(jnp.sum(upstream[:, None, :] * picked, axis=-1))
    chosen_back = gates * (gate_back - lax.optimization_barrier(jnp.sum(gates * gate_back, axis=-1, keepdims=True)))
    route_hot = (routes[:, :, None] == jnp.arange(EXPERTS, dtype=jnp.int32)[None, None, :]).astype(jnp.float32)
    logit_back = rounded(lax.optimization_barrier(jnp.sum(route_hot * chosen_back[:, :, None], axis=1)))
    router_grad = matmul(normed_two.T, logit_back)
    normed_two_back = matmul(logit_back, w_router.T)
    out_back = rounded(gates[:, :, None] * upstream[:, None, :])
    grad_buffer = jnp.zeros((DEVICES, EXPERTS * CAP, D), jnp.bfloat16).at[device_of, targets].set(out_back)
    grad_rows = to_experts(grad_buffer)

    def expert_backward(items):
        rows, grads, gate_w, up_w, down_w = items
        gate_pre = matmul(rows, gate_w)
        up_pre = matmul(rows, up_w)
        hidden_act = rounded(geglu(gate_pre, up_pre))
        hidden_back = matmul(grads, down_w)
        down_part = matmul(grads.T, hidden_act)
        _, geglu_back = jax.vjp(geglu, gate_pre, up_pre)
        gate_back_pre, up_back_pre = geglu_back(hidden_back)
        gate_back_pre = rounded(gate_back_pre)
        up_back_pre = rounded(up_back_pre)
        gate_part = matmul(rows.T, gate_back_pre)
        up_part = matmul(rows.T, up_back_pre)
        rows_back = (matmul(gate_back_pre, gate_w.T) + matmul(up_back_pre, up_w.T)).astype(jnp.bfloat16)
        return (rows_back, gate_part, up_part, down_part)
    rows_back, gate_grad, up_grad, down_grad = lax.map(expert_backward, (expert_rows, grad_rows, w_gate, w_up, w_down))
    rows_back = to_devices(rows_back)
    normed_two_back = normed_two_back + lax.optimization_barrier(jnp.sum(rows_back[device_of, targets].astype(jnp.float32), axis=1))
    _, norm_two_back = jax.vjp(rms_apply, hidden_one, gain_two)
    hidden_norm_back, gain_moe_grad = norm_two_back(normed_two_back)
    hidden_one_back = upstream + hidden_norm_back
    residual_back = hidden_one_back.astype(jnp.bfloat16)
    out_weight_grad = matmul(attended_flat.T, residual_back)
    attended_back4 = heads_of(matmul(residual_back, w_out.T).astype(jnp.bfloat16))

    def backward_step(bias_sum, items):
        query3, keys3, values3, attended3, attended_back3, log3 = items
        scores = scores_of(query3, keys3)
        weights_f = jnp.exp(scores - log3)
        weights_b = rounded(weights_f)
        value_back = jnp.einsum('hqk,qhd->khd', weights_b.astype(jnp.float32), attended_back3.astype(jnp.float32)).astype(jnp.bfloat16)
        weight_back = jnp.einsum('qhd,khd->hqk', attended_back3.astype(jnp.float32), values3.astype(jnp.float32))
        row_delta = jnp.einsum('qhd,qhd->hq', attended_back3.astype(jnp.float32), attended3.astype(jnp.float32))[:, :, None]
        score_back = weights_f * (weight_back - row_delta)
        score_round = rounded(score_back).astype(jnp.float32)
        query_back = (jnp.einsum('hqk,khd->qhd', score_round, keys3.astype(jnp.float32)) * score_scale).astype(jnp.bfloat16)
        key_back = (jnp.einsum('hqk,qhd->khd', score_round, query3.astype(jnp.float32)) * score_scale).astype(jnp.bfloat16)
        return (bias_sum + score_back, (query_back, key_back, value_back))
    bias_sum, (query_back, key_back, value_back) = lax.scan(backward_step, jnp.zeros((H, SEQ, SEQ), jnp.float32), (query4, key4, value4, attended4, attended_back4, log_totals))
    rel_bias_grad = jax.ops.segment_sum(jnp.transpose(bias_sum, (1, 2, 0)).reshape(SEQ * SEQ, H), buckets.reshape(-1), num_segments=NB).reshape(NB * H)
    query_back = query_back.reshape(TOKENS, D)
    key_back = key_back.reshape(TOKENS, D)
    value_back = value_back.reshape(TOKENS, D)
    query_weight_grad = matmul(normed_one.T, query_back)
    key_weight_grad = matmul(normed_one.T, key_back)
    value_weight_grad = matmul(normed_one.T, value_back)
    normed_one_back = matmul(query_back, w_query.T) + matmul(key_back, w_key.T) + matmul(value_back, w_value.T)
    _, norm_one_back = jax.vjp(rms_apply, tokens_f, gain_one)
    tokens_norm_back, gain_attn_grad = norm_one_back(normed_one_back)
    tokens_grad = hidden_one_back + tokens_norm_back
    return (layer_out, tokens_grad, gain_attn_grad, gain_moe_grad, rel_bias_grad, query_weight_grad, key_weight_grad, value_weight_grad, out_weight_grad, router_grad, gate_grad, up_grad, down_grad)
```

```python
import math

import jax
import jax.numpy as jnp
from jax import lax
from jax.sharding import PartitionSpec as P

H = 12
DH = 64
NB = 32
SEQ = 256
LANES = 128

EPSILON = 1e-06


def rms_apply(hidden, gain):
    factor = lax.rsqrt(jnp.mean(hidden * hidden, axis=-1, keepdims=True) + EPSILON)
    return hidden * factor * gain


def geglu(gate_pre, up_pre):
    return jax.nn.gelu(gate_pre, approximate=True) * up_pre


def matmul(left, right):
    return jnp.dot(left, right, preferred_element_type=jnp.float32)


def matmul_nt(left, right):
    return lax.dot_general(left, right, (((1,), (1,)), ((), ())), preferred_element_type=jnp.float32)


def matmul_tn(left, right):
    return lax.dot_general(left, right, (((0,), (0,)), ((), ())), preferred_element_type=jnp.float32)


def bf(value):
    return value.astype(jnp.bfloat16)


def swap(value, axis, distance):
    size = lax.axis_size(axis)
    return lax.ppermute(value, axis, [(i, i ^ distance) for i in range(size)])


def xor_order(blocks, index, axis):
    size = blocks.shape[axis]
    bit = 1
    while bit < size:
        shape = blocks.shape
        split = shape[:axis] + (size // (2 * bit), 2, bit) + shape[axis + 1 :]
        view = blocks.reshape(split)
        blocks = jnp.where((index & bit) != 0, jnp.flip(view, axis + 1), view).reshape(shape)
        bit *= 2
    return blocks


def dp_steps(parity):
    return (1, 2) if parity == 0 else (2, 1)


def dp_gather(block, parity):
    first, second = dp_steps(parity)
    near = swap(block, "dp", first)
    pair = jnp.stack([block, near])
    far = swap(pair, "dp", second)
    found = {0: block, first: near, second: far[0], first | second: far[1]}
    return [found[k] for k in range(4)]


def dp_reduce(parts, parity):
    second, first = dp_steps(parity)
    got = swap(jnp.stack([bf(parts[first]), bf(parts[first | second])]), "dp", first)
    mine = parts[0] + got[0].astype(jnp.float32)
    other = parts[second] + got[1].astype(jnp.float32)
    last = swap(bf(other), "dp", second)
    return mine + last.astype(jnp.float32)


def chip_gather(block, chips):
    return [block] + [swap(block, "expert", 2 * k) for k in range(1, chips)]


def gather_rows(parts, small, chips, core, chip_index, dp_index):
    rows = parts[0].shape[0]
    half = parts[0].shape[1] // 2
    keep = [jnp.where(core == 0, p[:, :half], p[:, half:]) for p in parts]
    send = [jnp.where(core == 0, p[:, half:], p[:, :half]) for p in parts]
    if small is not None:
        keep, send = keep + [small], send + [small]
    keep, send = jnp.concatenate(keep, 1), jnp.concatenate(send, 1)
    got = swap(send, "expert", 1)
    block = jnp.concatenate([jnp.where(core == 0, keep, got), jnp.where(core == 0, got, keep)], 0)
    width = block.shape[1]
    found = chip_gather(block, chips)
    lower = jnp.stack(found[: chips // 2])
    upper = jnp.stack(found[chips // 2 :])
    full = jnp.concatenate(
        [jnp.stack(dp_gather(lower, 0)), jnp.stack(dp_gather(upper, 1))], axis=1
    )
    payload = full[..., : half * len(parts)]
    other = swap(payload, "expert", 1)

    def ordered(value):
        value = xor_order(xor_order(value, dp_index, 0), chip_index, 1)
        return value.reshape(-1, value.shape[-1])

    mine, other = ordered(payload), ordered(other)
    left, right = jnp.where(core == 0, mine, other), jnp.where(core == 0, other, mine)
    result = [
        jnp.concatenate([left[:, i * half : (i + 1) * half], right[:, i * half : (i + 1) * half]], 1)
        for i in range(len(parts))
    ]
    if small is None:
        return result, None
    return result, ordered(full[..., half * len(parts) :])


def scatter_rows(parts, small, chips, core, chip_index, dp_index):
    half = parts[0].shape[1] // 2
    replicas = lax.axis_size("dp")
    keep = [jnp.where(core == 0, p[:, :half], p[:, half:]) for p in parts]
    send = [bf(jnp.where(core == 0, p[:, half:], p[:, :half])) for p in parts]
    if small is not None:
        keep, send = keep + [small], send + [bf(small)]
    got = swap(jnp.concatenate(send, 1), "expert", 1)
    total = jnp.concatenate(keep, 1) + got.astype(jnp.float32)
    width = total.shape[1]
    blocks = total.reshape(replicas, chips, -1, width)
    blocks = xor_order(xor_order(blocks, dp_index, 0), chip_index, 1)
    lower, upper = blocks[:, : chips // 2], blocks[:, chips // 2 :]
    lower = dp_reduce([lower[k] for k in range(replicas)], 0)
    upper = dp_reduce([upper[k] for k in range(replicas)], 1)
    chip_blocks = [lower[k] for k in range(chips // 2)] + [upper[k] for k in range(chips // 2)]
    arrived = [swap(bf(chip_blocks[k]), "expert", 2 * k) for k in range(1, chips)]
    block = chip_blocks[0]
    for piece in arrived:
        block = block + piece.astype(jnp.float32)
    rows = block.shape[0] // 2
    mine = jnp.where(core == 0, block[:rows], block[rows:])
    theirs = jnp.where(core == 0, block[rows:], block[:rows])
    payload = half * len(parts)
    got = swap(bf(theirs[:, :payload]), "expert", 1).astype(jnp.float32)
    left = jnp.where(core == 0, mine[:, :payload], got)
    right = jnp.where(core == 0, got, mine[:, :payload])
    result = [
        jnp.concatenate([left[:, i * half : (i + 1) * half], right[:, i * half : (i + 1) * half]], 1)
        for i in range(len(parts))
    ]
    return result, (None if small is None else mine[:, payload:])


def slot_positions(routes, experts):
    flat = routes.reshape(-1)
    expert_hot = (flat[:, None] == jnp.arange(experts, dtype=jnp.int32)[None, :]).astype(jnp.int32)
    earlier = jnp.cumsum(expert_hot, axis=0) - expert_hot
    return jnp.sum(earlier * expert_hot, axis=1).reshape(routes.shape)


def per_device(
    tokens,
    cotangent,
    buckets,
    routes,
    gain_attn,
    gain_moe,
    rel_bias,
    w_query,
    w_key,
    w_value,
    w_out,
    w_router,
    w_gate,
    w_up,
    w_down,
):
    f32 = jnp.float32
    groups = lax.axis_size("expert")
    chips = groups // 2
    replicas = lax.axis_size("dp")
    expert_index, dp_index = lax.axis_index("expert"), lax.axis_index("dp")
    core, chip_index = expert_index & 1, expert_index >> 1

    shard_rows = w_query.shape[0]
    experts = w_router.shape[1]
    n_bias = rel_bias.shape[0]
    small = jnp.concatenate(
        [
            w_router,
            gain_attn[:, None],
            gain_moe[:, None],
            jnp.pad(rel_bias, (0, shard_rows - n_bias))[:, None],
            jnp.zeros((shard_rows, LANES - experts - 3), jnp.bfloat16),
        ],
        axis=1,
    )
    (query_w, key_w, value_w), small_full = gather_rows(
        [w_query, w_key, w_value], small, chips, core, chip_index, dp_index
    )
    (out_w,), _ = gather_rows([w_out], None, chips, core, chip_index, dp_index)
    router_w = small_full[:, :experts]
    gain_one = small_full[:, experts].astype(f32)
    gain_two = small_full[:, experts + 1].astype(f32)
    bias_table = (
        small_full[:, experts + 2].reshape(-1, shard_rows)[:, :n_bias].reshape(NB, H)
    )

    tok_count, model_width = tokens.shape
    local_experts = w_gate.shape[0]
    capacity = max(2, 9 * tok_count // (4 * experts))
    unit = 2 * capacity
    expert_rows_n = chips * unit
    n_rows = local_experts * expert_rows_n
    group = routes // local_experts
    rel_core = (group & 1) ^ core
    rel_chip = (group >> 1) ^ chip_index
    targets = (
        rel_core * n_rows
        + (routes % local_experts) * expert_rows_n
        + rel_chip * unit
        + rel_core * capacity
        + slot_positions(routes, experts)
    )
    partner_targets = swap(targets, "expert", 1)
    partner_cot = swap(cotangent, "expert", 1)
    row_ids = jnp.arange(n_rows, dtype=jnp.int32)
    pick_own = [bf(row_ids[:, None] == targets[None, :, k]) for k in range(2)]
    pick_partner = [bf(row_ids[:, None] + n_rows == partner_targets[None, :, k]) for k in range(2)]
    return_ids = jnp.arange(2 * n_rows, dtype=jnp.int32)
    unpick = [bf(targets[:, k][:, None] == return_ids[None, :]) for k in range(2)]

    sequences = tok_count // SEQ
    score_scale = 1.0 / math.sqrt(DH)
    tokens_f = tokens.astype(f32)
    normed_one = bf(rms_apply(tokens_f, gain_one))
    query4 = bf(matmul(normed_one, query_w)).reshape(sequences, SEQ, H, DH)
    key4 = bf(matmul(normed_one, key_w)).reshape(sequences, SEQ, H, DH)
    value4 = bf(matmul(normed_one, value_w)).reshape(sequences, SEQ, H, DH)
    bucket_hot = bf(buckets.reshape(-1)[None, :] == jnp.arange(NB, dtype=jnp.int32)[:, None])
    bias_grid = matmul_tn(bias_table, bucket_hot).reshape(H, SEQ, SEQ)
    causal = jnp.arange(SEQ)[:, None] >= jnp.arange(SEQ)[None, :]

    def scores_of():
        raw = (
            jnp.einsum("bqhd,bkhd->bhqk", query4, key4, preferred_element_type=f32) * score_scale
            + bias_grid[None]
        )
        return jnp.where(causal[None, None], raw, -1e30)

    scores = scores_of()
    row_peak = jnp.max(scores, axis=-1, keepdims=True)
    log_total = row_peak + jnp.log(jnp.sum(jnp.exp(scores - row_peak), axis=-1, keepdims=True))
    weights_f = jnp.exp(scores - log_total)
    attn_weights = bf(weights_f)
    attended4 = bf(jnp.einsum("bhqk,bkhd->bqhd", attn_weights, value4, preferred_element_type=f32))
    attended_flat = attended4.reshape(tok_count, model_width)
    hidden_one = tokens_f + matmul(attended_flat, out_w)
    normed_two = bf(rms_apply(hidden_one, gain_two))

    partner_normed = swap(normed_two, "expert", 1)
    logits = matmul(normed_two, router_w)
    route_hot = (routes[:, :, None] == jnp.arange(experts, dtype=jnp.int32)[None, None, :]).astype(f32)
    chosen = jnp.sum(route_hot * logits[:, None, :], axis=2)
    gates = jax.nn.softmax(chosen, axis=-1)
    partner_gates = swap(gates, "expert", 1)

    def dispatch(rows):
        gathered = []
        for e in range(local_experts):
            own = rows[e * expert_rows_n : (e + 1) * expert_rows_n]
            found = [own[:unit]] + [
                swap(own[k * unit : (k + 1) * unit], "expert", 2 * k) for k in range(1, chips)
            ]
            gathered.append(dp_gather(jnp.concatenate(found, 0), e % 2))
        return gathered

    picks = jnp.concatenate([pick_own[0] + pick_own[1], pick_partner[0] + pick_partner[1]], 1)
    rows = dispatch(bf(matmul(picks, jnp.concatenate([normed_two, partner_normed], 0))))
    grad_picks = jnp.concatenate(pick_own + pick_partner, 1)
    grads = dispatch(
        bf(
            matmul(
                grad_picks,
                jnp.concatenate(
                    [bf(gates[:, k : k + 1] * cotangent) for k in range(2)]
                    + [bf(partner_gates[:, k : k + 1] * partner_cot) for k in range(2)],
                    0,
                ),
            )
        )
    )

    def combine(parts, e):
        split = parts.reshape(replicas, expert_rows_n, model_width)
        total = bf(dp_reduce([split[k] for k in range(replicas)], e % 2))
        found = [total[:unit]] + [
            swap(total[k * unit : (k + 1) * unit], "expert", 2 * k) for k in range(1, chips)
        ]
        mine = jnp.concatenate(found, 0)
        return mine, swap(mine, "expert", 1)

    rows_e = [jnp.concatenate(rows[e], 0) for e in range(local_experts)]
    grads_e = [jnp.concatenate(grads[e], 0) for e in range(local_experts)]
    acts, vjps, out_back = [], [], []
    for e in range(local_experts):
        gate_pre = matmul(rows_e[e], w_gate[e])
        up_pre = matmul(rows_e[e], w_up[e])
        act, vjp = jax.vjp(geglu, gate_pre, up_pre)
        acts.append(bf(act))
        vjps.append(vjp)
        out_back.append(combine(matmul_nt(acts[e], w_down[e]), e))
    rows_grad, pres = [], []
    for e in range(local_experts):
        gate_back_pre, up_back_pre = vjps[e](matmul(grads_e[e], w_down[e]))
        gate_back_pre, up_back_pre = bf(gate_back_pre), bf(up_back_pre)
        pres.append((gate_back_pre, up_back_pre))
        rows_grad.append(
            combine(matmul_nt(gate_back_pre, w_gate[e]) + matmul_nt(up_back_pre, w_up[e]), e)
        )
    down_grad = jnp.stack([matmul_tn(grads_e[e], acts[e]) for e in range(local_experts)])
    gate_grad = jnp.stack([matmul_tn(rows_e[e], pres[e][0]) for e in range(local_experts)])
    up_grad = jnp.stack([matmul_tn(rows_e[e], pres[e][1]) for e in range(local_experts)])

    returned = jnp.concatenate([m for m, _ in out_back] + [o for _, o in out_back], 0)
    first_out, second_out = matmul(unpick[0], returned), matmul(unpick[1], returned)
    layer_out = hidden_one + gates[:, 0:1] * first_out + gates[:, 1:2] * second_out
    gate_back = jnp.stack(
        [jnp.sum(cotangent * first_out, axis=-1), jnp.sum(cotangent * second_out, axis=-1)], axis=1
    )
    chosen_back = gates * (gate_back - jnp.sum(gates * gate_back, axis=-1, keepdims=True))
    logit_back = bf(jnp.sum(route_hot * chosen_back[:, :, None], axis=1))
    router_grad = matmul_tn(normed_two, logit_back)
    back_rows = jnp.concatenate([m for m, _ in rows_grad] + [o for _, o in rows_grad], 0)
    normed_two_back = matmul_nt(logit_back, router_w) + matmul(unpick[0] + unpick[1], back_rows)
    _, norm_two_back = jax.vjp(rms_apply, hidden_one, gain_two)
    hidden_norm_back, gain_moe_grad = norm_two_back(normed_two_back)
    hidden_one_back = cotangent + hidden_norm_back
    residual_back = bf(hidden_one_back)
    out_weight_grad = matmul_tn(attended_flat, residual_back)
    (out_total,), _ = scatter_rows([out_weight_grad], None, chips, core, chip_index, dp_index)
    attended_back4 = bf(matmul_nt(residual_back, out_w)).reshape(sequences, SEQ, H, DH)
    value_back = bf(
        jnp.einsum("bhqk,bqhd->bkhd", attn_weights, attended_back4, preferred_element_type=f32)
    )
    weight_back = jnp.einsum("bqhd,bkhd->bhqk", attended_back4, value4, preferred_element_type=f32)
    row_delta = jnp.einsum("bqhd,bqhd->bhq", attended_back4, attended4, preferred_element_type=f32)
    score_back = weights_f * (weight_back - row_delta[..., None])
    summed_back = jnp.sum(score_back, axis=0).reshape(H, SEQ * SEQ)
    summed_high = bf(summed_back)
    summed_low = bf(summed_back - summed_high.astype(f32))
    rel_bias_grad = (matmul_nt(bucket_hot, summed_high) + matmul_nt(bucket_hot, summed_low)).reshape(-1)
    score_round = bf(score_back)
    query_back = bf(
        jnp.einsum("bhqk,bkhd->bqhd", score_round, key4, preferred_element_type=f32) * score_scale
    ).reshape(tok_count, model_width)
    key_back = bf(
        jnp.einsum("bhqk,bqhd->bkhd", score_round, query4, preferred_element_type=f32) * score_scale
    ).reshape(tok_count, model_width)
    value_back = value_back.reshape(tok_count, model_width)
    query_weight_grad = matmul_tn(normed_one, query_back)
    key_weight_grad = matmul_tn(normed_one, key_back)
    value_weight_grad = matmul_tn(normed_one, value_back)
    normed_one_back = (
        matmul_nt(query_back, query_w) + matmul_nt(key_back, key_w) + matmul_nt(value_back, value_w)
    )
    _, norm_one_back = jax.vjp(rms_apply, tokens_f, gain_one)
    tokens_norm_back, gain_attn_grad = norm_one_back(normed_one_back)
    tokens_grad = hidden_one_back + tokens_norm_back

    devices = replicas * groups
    bias_rows = jnp.pad(rel_bias_grad.reshape(devices, n_bias), ((0, 0), (0, shard_rows - n_bias)))
    small_grad = jnp.concatenate(
        [
            router_grad,
            gain_attn_grad[:, None],
            gain_moe_grad[:, None],
            bias_rows.reshape(-1, 1),
            jnp.zeros((model_width, LANES - experts - 3), f32),
        ],
        axis=1,
    )
    (query_total, key_total, value_total), small_total = scatter_rows(
        [query_weight_grad, key_weight_grad, value_weight_grad],
        small_grad,
        chips,
        core,
        chip_index,
        dp_index,
    )
    return (
        layer_out,
        tokens_grad,
        small_total[:, experts],
        small_total[:, experts + 1],
        small_total[:n_bias, experts + 2],
        query_total,
        key_total,
        value_total,
        out_total,
        small_total[:, :experts],
        gate_grad,
        up_grad,
        down_grad,
    )


def solution(mesh):
    both = ("dp", "expert")
    row = P(both, None)
    return jax.shard_map(
        per_device,
        mesh=mesh,
        in_specs=(row, row, P(), row, P(both), P(both), P(both), row, row, row, row, row)
        + (P("expert", None, "dp"),) * 3,
        out_specs=(row, row, P(both), P(both), P(both), row, row, row, row, row)
        + (P("expert", None, "dp"),) * 3,
        check_vma=False,
    )
```

```python
import math

import jax
import jax.numpy as jnp
from jax import lax
from jax.experimental import pallas as pl
from jax.experimental.pallas import tpu as pltpu
from jax.sharding import PartitionSpec as P


H = 12
DH = 64
NB = 32
SEQ = 256
LANES = 128

EPSILON = 1e-06


def rms_apply(hidden, gain):
    factor = lax.rsqrt(jnp.mean(hidden * hidden, axis=-1, keepdims=True) + EPSILON)
    return hidden * factor * gain


def geglu(gate_pre, up_pre):
    return jax.nn.gelu(gate_pre, approximate=True) * up_pre


def matmul(left, right):
    return jnp.dot(left, right, preferred_element_type=jnp.float32)


def matmul_nt(left, right):
    return lax.dot_general(left, right, (((1,), (1,)), ((), ())), preferred_element_type=jnp.float32)


def matmul_tn(left, right):
    return lax.dot_general(left, right, (((0,), (0,)), ((), ())), preferred_element_type=jnp.float32)


def bf(value):
    return value.astype(jnp.bfloat16)


def swap(value, axis, distance):
    size = lax.axis_size(axis)
    return lax.ppermute(value, axis, [(i, i ^ distance) for i in range(size)])


def dp_steps(parity):
    return (1, 2) if parity == 0 else (2, 1)


def dp_gather(block, parity):
    first, second = dp_steps(parity)
    near = swap(block, "dp", first)
    pair = jnp.stack([block, near])
    far = swap(pair, "dp", second)
    found = {0: block, first: near, second: far[0], first | second: far[1]}
    return [found[k] for k in range(4)]


def dp_reduce(parts, parity):
    second, first = dp_steps(parity)
    got = swap(jnp.stack([bf(parts[first]), bf(parts[first | second])]), "dp", first)
    mine = parts[0] + got[0].astype(jnp.float32)
    other = parts[second] + got[1].astype(jnp.float32)
    last = swap(bf(other), "dp", second)
    return mine + last.astype(jnp.float32)


def chip_gather(block, chips):
    return [block] + [swap(block, "expert", 2 * k) for k in range(1, chips)]


SMEM = pl.BlockSpec(memory_space=pltpu.SMEM)
VMEM = pl.BlockSpec(memory_space=pltpu.VMEM)


def place_kernel(index_ref, near_low, far_low, near_up, far_up, out_ref):
    dp_index, chip_index = index_ref[0], index_ref[1]
    half = near_low.shape[1]
    for pieces, parity, base in (((near_low, far_low), 0, 0), ((near_up, far_up), 1, half)):
        first, second = dp_steps(parity)
        for far in range(2):
            for i in range(2):
                step = first * i + second * far
                for j in range(half):
                    out_ref[dp_index ^ step, chip_index ^ (base + j)] = pieces[far][i, j]


def place(index, pieces):
    _, half, rows, width = pieces[0].shape
    return pl.pallas_call(
        place_kernel,
        out_shape=jax.ShapeDtypeStruct((4, 2 * half, rows, width), pieces[0].dtype),
        in_specs=[SMEM] + [VMEM] * 4,
        out_specs=VMEM,
        name="place_weights",
    )(index, *pieces).reshape(-1, width)


def attn_fwd_kernel(
    tok_ref, gain_ref, bias_ref, bucket_ref, mine_ref, other_ref,
    n_ref, q_ref, k_ref, v_ref, low_ref, high_ref, att_ref,
):
    f32 = jnp.float32
    half_seq = SEQ // 2
    hidden = tok_ref[...].astype(f32)
    normed = bf(rms_apply(hidden, gain_ref[...]))
    n_ref[...] = normed
    half = other_ref.shape[1] // 3
    for part, out in enumerate((q_ref, k_ref, v_ref)):
        cut = slice(part * half, (part + 1) * half)
        out[:, :half] = bf(matmul(normed, mine_ref[:, cut]))
        out[:, half:] = bf(matmul(normed, other_ref[:, cut]))
    scale = 1.0 / math.sqrt(DH)
    row_ids = lax.broadcasted_iota(jnp.int32, (half_seq, half_seq), 0)
    col_ids = lax.broadcasted_iota(jnp.int32, (half_seq, half_seq), 1)
    causal = row_ids >= col_ids

    def biased(raw, head, rows, cols):
        table = jnp.broadcast_to(bias_ref[pl.ds(head, 1), :], (half_seq, LANES))
        return raw * scale + jnp.take_along_axis(table, bucket_ref[rows, cols], axis=1)

    def softmax(blocks):
        peak = blocks[0].max(-1, keepdims=True)
        for b in blocks[1:]:
            peak = jnp.maximum(peak, b.max(-1, keepdims=True))
        exps = [jnp.exp(b - peak) for b in blocks]
        total = sum(x.sum(-1, keepdims=True) for x in exps)
        inverse = 1.0 / total
        return [x * inverse for x in exps]

    first, second = slice(0, half_seq), slice(half_seq, SEQ)

    def pair_step(pair, carry):
        lanes = pl.ds(pl.multiple_of(pair * 2 * DH, 2 * DH), 2 * DH)
        qp, kp, vp = q_ref[:, lanes], k_ref[:, lanes], v_ref[:, lanes]
        outs_low, outs_high = [], []
        for sub in range(2):
            head = pair * 2 + sub
            cut = slice(sub * DH, (sub + 1) * DH)
            q, k, v = qp[:, cut], kp[:, cut], vp[:, cut]
            s00 = biased(matmul_nt(q[first], k[first]), head, first, first)
            s1 = matmul_nt(q[second], k)
            s10 = biased(s1[:, first], head, second, first)
            s11 = biased(s1[:, second], head, second, second)
            (p00,) = softmax([jnp.where(causal, s00, -1e30)])
            p10, p11 = softmax([s10, jnp.where(causal, s11, -1e30)])
            low_ref[head] = p00
            high_ref[head, :, first] = p10
            high_ref[head, :, second] = p11
            outs_low.append(matmul(bf(p00), v[first]))
            outs_high.append(matmul(bf(p10), v[first]) + matmul(bf(p11), v[second]))
        att_ref[first, lanes] = bf(jnp.concatenate(outs_low, 1))
        att_ref[second, lanes] = bf(jnp.concatenate(outs_high, 1))
        return carry

    lax.fori_loop(0, H // 2, pair_step, 0)


def attn_fwd(tokens, gain, bias_rows, buckets, mine, other):
    tok_count, width = tokens.shape
    b16, f32 = jnp.bfloat16, jnp.float32
    shaped = jax.ShapeDtypeStruct
    flat = shaped((tok_count, width), b16)
    return pl.pallas_call(
        attn_fwd_kernel,
        out_shape=(flat, flat, flat, flat)
        + (shaped((H, SEQ // 2, SEQ // 2), f32), shaped((H, SEQ // 2, SEQ), f32), flat),
        in_specs=[VMEM] * 6,
        out_specs=(VMEM,) * 7,
        name="attention_forward",
    )(tokens, gain, bias_rows, buckets, mine, other)


def attn_bwd_kernel(
    index_ref, ab_ref, att_ref, low_ref, high_ref, n_ref, q_ref, k_ref, v_ref, mine_ref, other_ref,
    tok_ref, gain_ref, base_ref, small_ref,
    keep_ref, send_ref, grad_ref, score_ref, qb_ref, kb_ref, vb_ref,
):
    f32 = jnp.float32
    half_seq = SEQ // 2
    scale = 1.0 / math.sqrt(DH)
    first, second = slice(0, half_seq), slice(half_seq, SEQ)

    def pair_step(pair, carry):
        lanes = pl.ds(pl.multiple_of(pair * 2 * DH, 2 * DH), 2 * DH)
        qp, kp, vp = q_ref[:, lanes], k_ref[:, lanes], v_ref[:, lanes]
        abp, attp = ab_ref[:, lanes], att_ref[:, lanes]
        found = [[], [], []]
        for sub in range(2):
            head = pair * 2 + sub
            cut = slice(sub * DH, (sub + 1) * DH)
            q, k, v, ab, att = qp[:, cut], kp[:, cut], vp[:, cut], abp[:, cut], attp[:, cut]
            delta = jnp.sum(ab.astype(f32) * att.astype(f32), axis=1, keepdims=True)
            low, high = low_ref[head], high_ref[head]
            low_b, high_b = bf(low), bf(high)
            value_low = matmul_tn(low_b, ab[first])
            value_high = matmul_tn(high_b, ab[second])
            found[2].append(
                jnp.concatenate([value_low + value_high[first], value_high[second]], 0)
            )
            back_low = low * (matmul_nt(ab[first], v[first]) - delta[first])
            back_high = high * (matmul_nt(ab[second], v) - delta[second])
            score_ref[head, first, first] = back_low
            score_ref[head, first, second] = jnp.zeros_like(back_low)
            score_ref[head, second, :] = back_high
            low_r, high_r = bf(back_low), bf(back_high)
            found[0].append(
                jnp.concatenate([matmul(low_r, k[first]), matmul(high_r, k)], 0) * scale
            )
            key_low = matmul_tn(low_r, q[first])
            key_high = matmul_tn(high_r, q[second])
            found[1].append(
                jnp.concatenate([key_low + key_high[first], key_high[second]], 0) * scale
            )
        for out, value in zip((qb_ref, kb_ref, vb_ref), found):
            out[:, lanes] = bf(jnp.concatenate(value, 1))
        return carry

    lax.fori_loop(0, H // 2, pair_step, 0)

    normed = n_ref[...]
    half = other_ref.shape[1] // 3
    replicas, chips, rows, width = keep_ref.shape
    dp_index, chip_index = index_ref[0], index_ref[1]
    payload = 3 * half

    def store(out, cut, value):
        for i in range(replicas):
            for j in range(chips):
                at = (i * chips + j) * rows
                out[dp_index ^ i, chip_index ^ j, :, cut] = value[at : at + rows]

    normed_back = jnp.zeros(tok_ref.shape, f32)
    for part, ref in enumerate((qb_ref, kb_ref, vb_ref)):
        cut = slice(part * half, (part + 1) * half)
        mine_b, other_b = ref[:, :half], ref[:, half:]
        store(keep_ref, cut, matmul_tn(normed, mine_b))
        store(send_ref, cut, bf(matmul_tn(normed, other_b)))
        normed_back += matmul_nt(mine_b, mine_ref[:, cut]) + matmul_nt(other_b, other_ref[:, cut])
    hidden = tok_ref[...].astype(f32)
    factor = lax.rsqrt(jnp.mean(hidden * hidden, axis=-1, keepdims=True) + EPSILON)
    scaled = normed_back * gain_ref[...]
    inner = jnp.mean(scaled * hidden, axis=-1, keepdims=True)
    grad_ref[...] = base_ref[...] + factor * (scaled - hidden * (factor * factor * inner))
    gain_back = jnp.sum(normed_back * (hidden * factor), axis=0, keepdims=True)
    wide = jnp.broadcast_to(gain_back, (LANES, gain_back.shape[1])).T
    lane = lax.broadcasted_iota(jnp.int32, wide.shape, 1)
    small = jnp.where(lane == index_ref[2], wide, small_ref[...])
    store(keep_ref, slice(payload, width), small)
    store(send_ref, slice(payload, width), bf(small))


def attn_bwd(index, ab, saved, mine, other, tokens, gain, base, small, chips, replicas):
    normed, q, k, v, low, high, att = saved
    tok_count, width = tokens.shape
    b16, f32 = jnp.bfloat16, jnp.float32
    shaped = jax.ShapeDtypeStruct
    total = other.shape[1] + LANES
    blocks = (replicas, chips, width // (replicas * chips), total)
    return pl.pallas_call(
        attn_bwd_kernel,
        out_shape=(
            shaped(blocks, f32),
            shaped(blocks, b16),
            shaped((tok_count, width), f32),
            shaped((H, SEQ, SEQ), f32),
        ),
        in_specs=[SMEM] + [VMEM] * 14,
        out_specs=(VMEM,) * 4,
        scratch_shapes=[pltpu.VMEM((tok_count, width), b16)] * 3,
        name="attention_backward",
    )(index, ab, att, low, high, normed, q, k, v, mine, other, tokens, gain, base, small)


def out_grad_kernel(index_ref, att_ref, keep_in, send_in, keep_ref, send_ref):
    replicas, chips, rows, _ = keep_ref.shape
    dp_index, chip_index = index_ref[0], index_ref[1]
    kept = matmul_tn(att_ref[...], keep_in[...])
    sent = bf(matmul_tn(att_ref[...], send_in[...]))
    for i in range(replicas):
        for j in range(chips):
            at = (i * chips + j) * rows
            keep_ref[dp_index ^ i, chip_index ^ j] = kept[at : at + rows]
            send_ref[dp_index ^ i, chip_index ^ j] = sent[at : at + rows]


def out_grad(index, attended, res_keep, res_send, chips, replicas):
    width = attended.shape[1]
    blocks = (replicas, chips, width // (replicas * chips), res_keep.shape[1])
    shaped = jax.ShapeDtypeStruct
    return pl.pallas_call(
        out_grad_kernel,
        out_shape=(shaped(blocks, jnp.float32), shaped(blocks, jnp.bfloat16)),
        in_specs=[SMEM] + [VMEM] * 3,
        out_specs=(VMEM,) * 2,
        name="out_weight_grad",
    )(index, attended, res_keep, res_send)


def core_split(parts, core):
    half = parts[0].shape[1] // 2
    keep = [jnp.where(core == 0, p[:, :half], p[:, half:]) for p in parts]
    send = [jnp.where(core == 0, p[:, half:], p[:, :half]) for p in parts]
    return keep, send


def core_join(mine, other, core, axis=1):
    return jnp.concatenate(
        [jnp.where(core == 0, mine, other), jnp.where(core == 0, other, mine)], axis
    )


def gather_pieces(keep, send, chips, core):
    got = swap(send, "expert", 1)
    block = core_join(keep, got, core, 0)
    found = chip_gather(block, chips)
    pieces = []
    for parity, part in enumerate((found[: chips // 2], found[chips // 2 :])):
        first, second = dp_steps(parity)
        part = jnp.stack(part)
        near = jnp.stack([part, swap(part, "dp", first)])
        far = swap(near, "dp", second)
        pieces += [near, far]
    return pieces


def partner_pieces(pieces, width):
    return [swap(p[..., :width], "expert", 1) for p in pieces]


def scatter_blocks(keep, send, parts, chips, core):
    replicas = lax.axis_size("dp")
    got = swap(send, "expert", 1)
    blocks = keep + got.astype(jnp.float32)
    lower, upper = blocks[:, : chips // 2], blocks[:, chips // 2 :]
    lower = dp_reduce([lower[k] for k in range(replicas)], 0)
    upper = dp_reduce([upper[k] for k in range(replicas)], 1)
    chip_blocks = [lower[k] for k in range(chips // 2)] + [upper[k] for k in range(chips // 2)]
    arrived = [swap(bf(chip_blocks[k]), "expert", 2 * k) for k in range(1, chips)]
    block = chip_blocks[0]
    for piece in arrived:
        block = block + piece.astype(jnp.float32)
    rows = block.shape[0] // 2
    mine = jnp.where(core == 0, block[:rows], block[rows:])
    theirs = jnp.where(core == 0, block[rows:], block[:rows])
    payload = block.shape[1] // LANES * LANES if parts == 1 else block.shape[1] - LANES
    half = payload // parts
    got = swap(bf(theirs[:, :payload]), "expert", 1).astype(jnp.float32)
    result = [
        core_join(mine[:, i * half : (i + 1) * half], got[:, i * half : (i + 1) * half], core)
        for i in range(parts)
    ]
    return result, mine[:, payload:]


def slot_positions(routes, experts):
    flat = routes.reshape(-1)
    expert_hot = (flat[:, None] == jnp.arange(experts, dtype=jnp.int32)[None, :]).astype(jnp.int32)
    earlier = jnp.cumsum(expert_hot, axis=0) - expert_hot
    return jnp.sum(earlier * expert_hot, axis=1).reshape(routes.shape)


def per_device(
    tokens,
    cotangent,
    buckets,
    routes,
    gain_attn,
    gain_moe,
    rel_bias,
    w_query,
    w_key,
    w_value,
    w_out,
    w_router,
    w_gate,
    w_up,
    w_down,
):
    f32 = jnp.float32
    groups = lax.axis_size("expert")
    chips = groups // 2
    replicas = lax.axis_size("dp")
    expert_index, dp_index = lax.axis_index("expert"), lax.axis_index("dp")
    core, chip_index = expert_index & 1, expert_index >> 1

    shard_rows = w_query.shape[0]
    experts = w_router.shape[1]
    n_bias = rel_bias.shape[0]
    small = jnp.concatenate(
        [
            w_router,
            gain_attn[:, None],
            gain_moe[:, None],
            jnp.pad(rel_bias, (0, shard_rows - n_bias))[:, None],
            jnp.zeros((shard_rows, LANES - experts - 3), jnp.bfloat16),
        ],
        axis=1,
    )
    model_width = tokens.shape[1]
    half = model_width // 2
    index = jnp.stack([dp_index, chip_index, jnp.int32(experts)]).astype(jnp.int32)
    keep, send = core_split([w_query, w_key, w_value], core)
    pieces = gather_pieces(
        jnp.concatenate(keep + [small], 1), jnp.concatenate(send + [small], 1), chips, core
    )
    keep, send = core_split([w_out], core)
    out_pieces = gather_pieces(keep[0], send[0], chips, core)
    qkv_other = place(index, partner_pieces(pieces, 3 * half))
    qkv_mine = place(index, pieces)
    out_other = place(index, partner_pieces(out_pieces, half))
    out_w = core_join(place(index, out_pieces), out_other, core)
    small_full = qkv_mine[:, 3 * half :]
    router_w = small_full[:, :experts]
    gain_one = small_full[:, experts].astype(f32)[None, :]
    gain_two = small_full[:, experts + 1].astype(f32)
    bias_table = (
        small_full[:, experts + 2].reshape(-1, shard_rows)[:, :n_bias].reshape(NB, H)
    )

    tok_count = tokens.shape[0]
    local_experts = w_gate.shape[0]
    capacity = max(2, 9 * tok_count // (4 * experts))
    unit = 2 * capacity
    expert_rows_n = chips * unit
    n_rows = local_experts * expert_rows_n
    group = routes // local_experts
    rel_core = (group & 1) ^ core
    rel_chip = (group >> 1) ^ chip_index
    targets = (
        rel_core * n_rows
        + (routes % local_experts) * expert_rows_n
        + rel_chip * unit
        + rel_core * capacity
        + slot_positions(routes, experts)
    )
    partner_targets = swap(targets, "expert", 1)
    partner_cot = swap(cotangent, "expert", 1)
    row_ids = jnp.arange(n_rows, dtype=jnp.int32)
    pick_own = [bf(row_ids[:, None] == targets[None, :, k]) for k in range(2)]
    pick_partner = [bf(row_ids[:, None] + n_rows == partner_targets[None, :, k]) for k in range(2)]
    return_ids = jnp.arange(2 * n_rows, dtype=jnp.int32)
    unpick = [bf(targets[:, k][:, None] == return_ids[None, :]) for k in range(2)]

    tokens_f = tokens.astype(f32)
    bias_rows = bias_table.astype(f32).T
    bias_rows = core_join(bias_rows[: H // 2], bias_rows[H // 2 :], core, 0)
    bias_rows = jnp.pad(bias_rows, ((0, 0), (0, LANES - NB)))
    normed_one, query, keys, values, low, high, attended = attn_fwd(
        tokens, gain_one, bias_rows, buckets, qkv_mine, qkv_other
    )
    attended_flat = core_join(attended[:, :half], attended[:, half:], core)
    hidden_one = tokens_f + matmul(attended_flat, out_w)
    normed_two = bf(rms_apply(hidden_one, gain_two))

    partner_normed = swap(normed_two, "expert", 1)
    logits = matmul(normed_two, router_w)
    route_hot = (routes[:, :, None] == jnp.arange(experts, dtype=jnp.int32)[None, None, :]).astype(f32)
    chosen = jnp.sum(route_hot * logits[:, None, :], axis=2)
    gates = jax.nn.softmax(chosen, axis=-1)
    partner_gates = swap(gates, "expert", 1)

    def dispatch(rows):
        gathered = []
        for e in range(local_experts):
            own = rows[e * expert_rows_n : (e + 1) * expert_rows_n]
            found = [own[:unit]] + [
                swap(own[k * unit : (k + 1) * unit], "expert", 2 * k) for k in range(1, chips)
            ]
            gathered.append(dp_gather(jnp.concatenate(found, 0), e % 2))
        return gathered

    picks = jnp.concatenate([pick_own[0] + pick_own[1], pick_partner[0] + pick_partner[1]], 1)
    rows = dispatch(bf(matmul(picks, jnp.concatenate([normed_two, partner_normed], 0))))
    grad_picks = jnp.concatenate(pick_own + pick_partner, 1)
    grads = dispatch(
        bf(
            matmul(
                grad_picks,
                jnp.concatenate(
                    [bf(gates[:, k : k + 1] * cotangent) for k in range(2)]
                    + [bf(partner_gates[:, k : k + 1] * partner_cot) for k in range(2)],
                    0,
                ),
            )
        ),
    )

    def combine(parts, e):
        split = parts.reshape(replicas, expert_rows_n, model_width)
        total = bf(dp_reduce([split[k] for k in range(replicas)], e % 2))
        found = [total[:unit]] + [
            swap(total[k * unit : (k + 1) * unit], "expert", 2 * k) for k in range(1, chips)
        ]
        mine = jnp.concatenate(found, 0)
        return mine, swap(mine, "expert", 1)

    rows_e = [jnp.concatenate(rows[e], 0) for e in range(local_experts)]
    grads_e = [jnp.concatenate(grads[e], 0) for e in range(local_experts)]
    acts, vjps, out_back = [], [], []
    for e in range(local_experts):
        gate_pre = matmul(rows_e[e], w_gate[e])
        up_pre = matmul(rows_e[e], w_up[e])
        act, vjp = jax.vjp(geglu, gate_pre, up_pre)
        acts.append(bf(act))
        vjps.append(vjp)
        part = matmul_nt(acts[e], w_down[e])
        out_back.append(combine(part, e))
    rows_grad, pres = [], []
    for e in range(local_experts):
        gate_back_pre, up_back_pre = vjps[e](matmul(grads_e[e], w_down[e]))
        gate_back_pre, up_back_pre = bf(gate_back_pre), bf(up_back_pre)
        pres.append((gate_back_pre, up_back_pre))
        part = matmul_nt(gate_back_pre, w_gate[e]) + matmul_nt(up_back_pre, w_up[e])
        rows_grad.append(combine(part, e))
    down_grad = jnp.stack([matmul_tn(grads_e[e], acts[e]) for e in range(local_experts)])
    gate_grad = jnp.stack([matmul_tn(rows_e[e], pres[e][0]) for e in range(local_experts)])
    up_grad = jnp.stack([matmul_tn(rows_e[e], pres[e][1]) for e in range(local_experts)])

    returned = jnp.concatenate([m for m, _ in out_back] + [o for _, o in out_back], 0)
    late_cot, returned, late_gates = lax.optimization_barrier((cotangent, returned, gates))
    first_out, second_out = matmul(unpick[0], returned), matmul(unpick[1], returned)
    layer_out = hidden_one + late_gates[:, 0:1] * first_out + late_gates[:, 1:2] * second_out
    gate_back = jnp.stack(
        [jnp.sum(late_cot * first_out, axis=-1), jnp.sum(late_cot * second_out, axis=-1)], axis=1
    )
    chosen_back = late_gates * (gate_back - jnp.sum(late_gates * gate_back, axis=-1, keepdims=True))
    logit_back = bf(jnp.sum(route_hot * chosen_back[:, :, None], axis=1))
    router_grad = matmul_tn(normed_two, logit_back)
    back_rows = jnp.concatenate([m for m, _ in rows_grad] + [o for _, o in rows_grad], 0)
    normed_two_back = matmul_nt(logit_back, router_w) + matmul(unpick[0] + unpick[1], back_rows)
    _, norm_two_back = jax.vjp(rms_apply, hidden_one, gain_two)
    hidden_norm_back, gain_moe_grad = norm_two_back(normed_two_back)
    hidden_one_back = late_cot + hidden_norm_back
    residual_back = bf(hidden_one_back)
    res_keep, res_send = core_split([residual_back], core)
    keep, send = out_grad(index, attended_flat, res_keep[0], res_send[0], chips, replicas)
    (out_total,), _ = scatter_blocks(keep, send, 1, chips, core)
    attended_back = bf(matmul_nt(residual_back, out_w))
    attended_back = core_join(attended_back[:, :half], attended_back[:, half:], core)
    small_grad = jnp.concatenate(
        [
            router_grad,
            jnp.zeros((model_width, 1), f32),
            gain_moe_grad[:, None],
            jnp.zeros((model_width, LANES - experts - 2), f32),
        ],
        axis=1,
    )
    keep, send, tokens_grad, score_back = attn_bwd(
        index,
        attended_back,
        (normed_one, query, keys, values, low, high, attended),
        qkv_mine,
        qkv_other,
        tokens,
        gain_one,
        hidden_one_back,
        small_grad,
        chips,
        replicas,
    )
    (query_total, key_total, value_total), small_total = scatter_blocks(keep, send, 3, chips, core)
    bucket_hot = bf(buckets[None] == jnp.arange(NB, dtype=jnp.int32)[:, None, None])
    score_high = bf(score_back)
    score_low = bf(score_back - score_high.astype(f32))
    bias_grad = sum(
        lax.dot_general(bucket_hot, x, (((1, 2), (1, 2)), ((), ())), preferred_element_type=f32)
        for x in (score_high, score_low)
    )
    bias_grad = core_join(bias_grad[:, : H // 2], bias_grad[:, H // 2 :], core)
    bias_grad = jnp.pad(bias_grad, ((0, 0), (0, LANES - H)))
    for axis in ("expert", "dp"):
        distance = 1
        while distance < lax.axis_size(axis):
            bias_grad = bias_grad + swap(bias_grad, axis, distance)
            distance *= 2
    bias_total = lax.dynamic_slice(
        bias_grad[:, :H].reshape(-1), ((dp_index * groups + expert_index) * n_bias,), (n_bias,)
    )
    return (
        layer_out,
        tokens_grad,
        small_total[:, experts],
        small_total[:, experts + 1],
        bias_total,
        query_total,
        key_total,
        value_total,
        out_total,
        small_total[:, :experts],
        gate_grad,
        up_grad,
        down_grad,
    )


def solution(mesh):
    both = ("dp", "expert")
    row = P(both, None)

    return jax.shard_map(
        per_device,
        mesh=mesh,
        in_specs=(row, row, P(), row, P(both), P(both), P(both), row, row, row, row, row)
        + (P("expert", None, "dp"),) * 3,
        out_specs=(row, row, P(both), P(both), P(both), row, row, row, row, row)
        + (P("expert", None, "dp"),) * 3,
        check_vma=False,
    )
```

```python
import functools
import math

import jax
import jax.numpy as jnp
from jax import lax
from jax.experimental import pallas as pl
from jax.experimental.pallas import tpu as pltpu
from jax.sharding import PartitionSpec as P


H = 12
DH = 64
NB = 32
SEQ = 256
LANES = 128

EPSILON = 1e-06


def rms_apply(hidden, gain):
    factor = lax.rsqrt(jnp.mean(hidden * hidden, axis=-1, keepdims=True) + EPSILON)
    return hidden * factor * gain


def geglu(gate_pre, up_pre):
    return jax.nn.gelu(gate_pre, approximate=True) * up_pre


def matmul(left, right):
    return jnp.dot(left, right, preferred_element_type=jnp.float32)


def matmul_nt(left, right):
    return lax.dot_general(left, right, (((1,), (1,)), ((), ())), preferred_element_type=jnp.float32)


def matmul_tn(left, right):
    return lax.dot_general(left, right, (((0,), (0,)), ((), ())), preferred_element_type=jnp.float32)


def bf(value):
    return value.astype(jnp.bfloat16)


def swap(value, axis, distance):
    size = lax.axis_size(axis)
    return lax.ppermute(value, axis, [(i, i ^ distance) for i in range(size)])


def xor_order(blocks, index, axis):
    size = blocks.shape[axis]
    bit = 1
    while bit < size:
        shape = blocks.shape
        split = shape[:axis] + (size // (2 * bit), 2, bit) + shape[axis + 1 :]
        view = blocks.reshape(split)
        blocks = jnp.where((index & bit) != 0, jnp.flip(view, axis + 1), view).reshape(shape)
        bit *= 2
    return blocks


def dp_steps(parity):
    return (1, 2) if parity == 0 else (2, 1)


def dp_gather(block, parity):
    first, second = dp_steps(parity)
    near = swap(block, "dp", first)
    pair = jnp.stack([block, near])
    far = swap(pair, "dp", second)
    found = {0: block, first: near, second: far[0], first | second: far[1]}
    return [found[k] for k in range(4)]


def dp_reduce(parts, parity):
    second, first = dp_steps(parity)
    got = swap(jnp.stack([bf(parts[first]), bf(parts[first | second])]), "dp", first)
    mine = parts[0] + got[0].astype(jnp.float32)
    other = parts[second] + got[1].astype(jnp.float32)
    last = swap(bf(other), "dp", second)
    return mine + last.astype(jnp.float32)


def chip_gather(block, chips):
    return [block] + [swap(block, "expert", 2 * k) for k in range(1, chips)]


SMEM = pl.BlockSpec(memory_space=pltpu.SMEM)
VMEM = pl.BlockSpec(memory_space=pltpu.VMEM)


def place_kernel(index_ref, near_low, far_low, near_up, far_up, out_ref):
    dp_index, chip_index = index_ref[0], index_ref[1]
    half = near_low.shape[1]
    for pieces, parity, base in (((near_low, far_low), 0, 0), ((near_up, far_up), 1, half)):
        first, second = dp_steps(parity)
        for far in range(2):
            for i in range(2):
                step = first * i + second * far
                for j in range(half):
                    out_ref[dp_index ^ step, chip_index ^ (base + j)] = pieces[far][i, j]


def place(index, pieces):
    _, half, rows, width = pieces[0].shape
    return pl.pallas_call(
        place_kernel,
        out_shape=jax.ShapeDtypeStruct((4, 2 * half, rows, width), pieces[0].dtype),
        in_specs=[SMEM] + [VMEM] * 4,
        out_specs=VMEM,
        name="place_weights",
    )(index, *pieces).reshape(-1, width)


def core_pick(core, first, second):
    return jnp.where(jnp.broadcast_to(core, first.shape) == 0, first, second)


def forward_kernel(placed, experts, *refs):
    if placed:
        index_ref, *refs = refs
        pieces, refs = refs[:8], refs[8:]
        tok_ref, bucket_ref, route_ref, head_ref, hot_ref, mine_ref, other_ref, *refs = refs
        dp_index, chip_index = index_ref[0], index_ref[1]
        half_chips, rows = pieces[0].shape[1:3]
        for out, group in ((mine_ref, pieces[:4]), (other_ref, pieces[4:])):
            for parity in range(2):
                first, second = dp_steps(parity)
                for far in range(2):
                    for i in range(2):
                        dp_at = dp_index ^ (first * i + second * far)
                        for j in range(half_chips):
                            chip_at = chip_index ^ (half_chips * parity + j)
                            at = pl.multiple_of((dp_at * 2 * half_chips + chip_at) * rows, rows)
                            out[pl.ds(at, rows), :] = group[2 * parity + far][i, j]
    else:
        index_ref, mine_ref, other_ref, tok_ref, bucket_ref, route_ref, head_ref, hot_ref, *refs = refs
    n_ref, q_ref, k_ref, v_ref, low_ref, high_ref, att_ref, flat_ref = refs[:8]
    hidden_ref, second_ref, gate_ref, gain_ref, bias_ref = refs[8:]
    f32 = jnp.float32
    core = index_ref[3]
    half_seq = SEQ // 2
    half = q_ref.shape[1] // 2
    small = mine_ref[:, 4 * half :]
    vectors = small.astype(f32).T
    gain_ref[...] = vectors[experts : experts + 2]
    rows16 = lax.broadcasted_iota(jnp.int32, (16, vectors.shape[1]), 0)
    shifted = rows16 + core * (H // 2)
    wanted = jnp.where(rows16 < H, jnp.where(shifted >= H, shifted - H, shifted), -2)
    spread = jnp.where(head_ref[...] == wanted, vectors[experts + 2 : experts + 3], 0.0)
    bias_ref[...] = matmul(bf(spread), hot_ref[...])

    hidden = tok_ref[...].astype(f32)
    normed = bf(rms_apply(hidden, gain_ref[0:1]))
    n_ref[...] = normed
    for part, out in enumerate((q_ref, k_ref, v_ref)):
        cut = slice(part * half, (part + 1) * half)
        out[:, :half] = bf(matmul(normed, mine_ref[:, cut]))
        out[:, half:] = bf(matmul(normed, other_ref[:, cut]))
    scale = 1.0 / math.sqrt(DH)
    row_ids = lax.broadcasted_iota(jnp.int32, (half_seq, half_seq), 0)
    col_ids = lax.broadcasted_iota(jnp.int32, (half_seq, half_seq), 1)
    causal = row_ids >= col_ids

    def biased(raw, head, rows, cols):
        table = jnp.broadcast_to(bias_ref[pl.ds(head, 1), :], (half_seq, LANES))
        return raw * scale + jnp.take_along_axis(table, bucket_ref[rows, cols], axis=1)

    def softmax(blocks):
        peak = blocks[0].max(-1, keepdims=True)
        for b in blocks[1:]:
            peak = jnp.maximum(peak, b.max(-1, keepdims=True))
        exps = [jnp.exp(b - peak) for b in blocks]
        total = sum(x.sum(-1, keepdims=True) for x in exps)
        inverse = 1.0 / total
        return [x * inverse for x in exps]

    first, second = slice(0, half_seq), slice(half_seq, SEQ)

    def pair_step(pair, carry):
        lanes = pl.ds(pl.multiple_of(pair * 2 * DH, 2 * DH), 2 * DH)
        qp, kp, vp = q_ref[:, lanes], k_ref[:, lanes], v_ref[:, lanes]
        outs_low, outs_high = [], []
        for sub in range(2):
            head = pair * 2 + sub
            cut = slice(sub * DH, (sub + 1) * DH)
            q, k, v = qp[:, cut], kp[:, cut], vp[:, cut]
            s00 = biased(matmul_nt(q[first], k[first]), head, first, first)
            s1 = matmul_nt(q[second], k)
            s10 = biased(s1[:, first], head, second, first)
            s11 = biased(s1[:, second], head, second, second)
            (p00,) = softmax([jnp.where(causal, s00, -1e30)])
            p10, p11 = softmax([s10, jnp.where(causal, s11, -1e30)])
            low_ref[head] = p00
            high_ref[head, :, first] = p10
            high_ref[head, :, second] = p11
            outs_low.append(matmul(bf(p00), v[first]))
            outs_high.append(matmul(bf(p10), v[first]) + matmul(bf(p11), v[second]))
        att_ref[first, lanes] = bf(jnp.concatenate(outs_low, 1))
        att_ref[second, lanes] = bf(jnp.concatenate(outs_high, 1))
        return carry

    lax.fori_loop(0, H // 2, pair_step, 0)
    att_mine, att_other = att_ref[:, :half].astype(f32), att_ref[:, half:].astype(f32)
    flat_ref[:, :half] = bf(core_pick(core, att_mine, att_other))
    flat_ref[:, half:] = bf(core_pick(core, att_other, att_mine))
    flat = flat_ref[...]
    cut = slice(3 * half, 4 * half)
    out_mine, out_other = matmul(flat, mine_ref[:, cut]), matmul(flat, other_ref[:, cut])
    hidden_ref[:, :half] = hidden[:, :half] + core_pick(core, out_mine, out_other)
    hidden_ref[:, half:] = hidden[:, half:] + core_pick(core, out_other, out_mine)
    normed_two = bf(rms_apply(hidden_ref[...], gain_ref[1:2]))
    second_ref[...] = normed_two
    logits = matmul(normed_two, small)
    lane = lax.broadcasted_iota(jnp.int32, logits.shape, 1)
    chosen = [
        jnp.sum(jnp.where(lane == route_ref[:, k : k + 1], logits, 0.0), 1, keepdims=True)
        for k in range(2)
    ]
    peak = jnp.maximum(chosen[0], chosen[1])
    exps = [jnp.exp(c - peak) for c in chosen]
    total = exps[0] + exps[1]
    gate_ref[...] = jnp.where(lane == 0, exps[0] / total, jnp.where(lane == 1, exps[1] / total, 0.0))


def layer_forward(index, mine, other, tokens, buckets, routes, head_of, hot, experts):
    tok_count, width = tokens.shape
    b16, f32 = jnp.bfloat16, jnp.float32
    shaped = jax.ShapeDtypeStruct
    flat, total = shaped((tok_count, width), b16), mine[0].shape[-1]
    placed = mine[0].shape[2] % 16 == 0
    weights = (shaped((width, total), b16),) * 2
    if placed:
        inputs = tuple(mine) + tuple(other)
    else:
        inputs = (place(index, mine), place(index, other))
    tail = (tokens, buckets, routes, head_of, hot)
    result = pl.pallas_call(
        functools.partial(forward_kernel, placed, experts),
        out_shape=(weights if placed else ())
        + (flat, flat, flat, flat)
        + (shaped((H, SEQ // 2, SEQ // 2), f32), shaped((H, SEQ // 2, SEQ), f32), flat, flat)
        + (shaped((tok_count, width), f32), flat, shaped((tok_count, LANES), f32), shaped((2, width), f32)),
        in_specs=[SMEM] + [VMEM] * (len(inputs) + len(tail)),
        out_specs=(VMEM,) * (14 if placed else 12),
        scratch_shapes=[pltpu.VMEM((16, LANES), f32)],
        name="layer_forward",
    )(index, *inputs, *tail)
    return result if placed else inputs + result


def backward_kernel(
    index_ref, back_ref, logit_ref, cot_ref, hidden_ref, second_ref, flat_ref, att_ref, low_ref, high_ref,
    n_ref, q_ref, k_ref, v_ref, mine_ref, other_ref, tok_ref, gain_ref,
    keep_ref, send_ref, grad_ref, score_ref, qb_ref, kb_ref, vb_ref, ab_ref,
):
    f32 = jnp.float32
    half_seq = SEQ // 2
    scale = 1.0 / math.sqrt(DH)
    first, second = slice(0, half_seq), slice(half_seq, SEQ)
    half = ab_ref.shape[1] // 2
    replicas, chips, rows, width = keep_ref.shape
    dp_index, chip_index, experts, core = (index_ref[i] for i in range(4))
    payload = 4 * half

    def store(out, cut, value):
        for i in range(replicas):
            for j in range(chips):
                at = (i * chips + j) * rows
                out[dp_index ^ i, chip_index ^ j, :, cut] = value[at : at + rows]

    def norm_back(hidden, gain, upstream):
        factor = lax.rsqrt(jnp.mean(hidden * hidden, axis=-1, keepdims=True) + EPSILON)
        scaled = upstream * gain
        inner = jnp.mean(scaled * hidden, axis=-1, keepdims=True)
        gain_back = jnp.sum(upstream * (hidden * factor), axis=0, keepdims=True)
        return factor * (scaled - hidden * (factor * factor * inner)), gain_back

    logit_back = logit_ref[...]
    small_w = mine_ref[:, payload:]
    hidden_back, gain_two_back = norm_back(
        hidden_ref[...], gain_ref[1:2], back_ref[...] + matmul_nt(logit_back, small_w)
    )
    hidden_back = cot_ref[...] + hidden_back
    grad_ref[...] = hidden_back
    left, right = hidden_back[:, :half], hidden_back[:, half:]
    res_mine, res_other = bf(core_pick(core, left, right)), bf(core_pick(core, right, left))
    cut = slice(3 * half, payload)
    ab = matmul_nt(res_mine, mine_ref[:, cut]) + matmul_nt(res_other, other_ref[:, cut])
    left, right = ab[:, :half], ab[:, half:]
    ab_ref[:, :half] = bf(core_pick(core, left, right))
    ab_ref[:, half:] = bf(core_pick(core, right, left))
    flat = flat_ref[...]
    store(keep_ref, cut, matmul_tn(flat, res_mine))
    store(send_ref, cut, bf(matmul_tn(flat, res_other)))

    def pair_step(pair, carry):
        lanes = pl.ds(pl.multiple_of(pair * 2 * DH, 2 * DH), 2 * DH)
        qp, kp, vp = q_ref[:, lanes], k_ref[:, lanes], v_ref[:, lanes]
        abp, attp = ab_ref[:, lanes], att_ref[:, lanes]
        found = [[], [], []]
        for sub in range(2):
            head = pair * 2 + sub
            cut = slice(sub * DH, (sub + 1) * DH)
            q, k, v, ab, att = qp[:, cut], kp[:, cut], vp[:, cut], abp[:, cut], attp[:, cut]
            delta = jnp.sum(ab.astype(f32) * att.astype(f32), axis=1, keepdims=True)
            low, high = low_ref[head], high_ref[head]
            low_b, high_b = bf(low), bf(high)
            value_low = matmul_tn(low_b, ab[first])
            value_high = matmul_tn(high_b, ab[second])
            found[2].append(
                jnp.concatenate([value_low + value_high[first], value_high[second]], 0)
            )
            back_low = low * (matmul_nt(ab[first], v[first]) - delta[first])
            back_high = high * (matmul_nt(ab[second], v) - delta[second])
            score_ref[head, first, first] = back_low
            score_ref[head, first, second] = jnp.zeros_like(back_low)
            score_ref[head, second, :] = back_high
            low_r, high_r = bf(back_low), bf(back_high)
            found[0].append(
                jnp.concatenate([matmul(low_r, k[first]), matmul(high_r, k)], 0) * scale
            )
            key_low = matmul_tn(low_r, q[first])
            key_high = matmul_tn(high_r, q[second])
            found[1].append(
                jnp.concatenate([key_low + key_high[first], key_high[second]], 0) * scale
            )
        for out, value in zip((qb_ref, kb_ref, vb_ref), found):
            out[:, lanes] = bf(jnp.concatenate(value, 1))
        return carry

    lax.fori_loop(0, H // 2, pair_step, 0)

    normed = n_ref[...]
    normed_back = jnp.zeros(tok_ref.shape, f32)
    for part, ref in enumerate((qb_ref, kb_ref, vb_ref)):
        cut = slice(part * half, (part + 1) * half)
        mine_b, other_b = ref[:, :half], ref[:, half:]
        store(keep_ref, cut, matmul_tn(normed, mine_b))
        store(send_ref, cut, bf(matmul_tn(normed, other_b)))
        normed_back += matmul_nt(mine_b, mine_ref[:, cut]) + matmul_nt(other_b, other_ref[:, cut])
    token_back, gain_one_back = norm_back(tok_ref[...].astype(f32), gain_ref[0:1], normed_back)
    grad_ref[...] += token_back
    small = matmul_tn(second_ref[...], logit_back)
    lane = lax.broadcasted_iota(jnp.int32, small.shape, 1)
    for at, gain_back in ((experts, gain_one_back), (experts + 1, gain_two_back)):
        wide = jnp.broadcast_to(gain_back, (LANES, gain_back.shape[1])).T
        small = jnp.where(lane == at, wide, small)
    store(keep_ref, slice(payload, width), small)
    store(send_ref, slice(payload, width), bf(small))


def layer_backward(index, back, logit_back, cot, forward, tokens, chips, replicas):
    mine, other, normed, q, k, v, low, high, att, flat, hidden, second, _, gains = forward
    tok_count, width = tokens.shape
    b16, f32 = jnp.bfloat16, jnp.float32
    shaped = jax.ShapeDtypeStruct
    blocks = (replicas, chips, width // (replicas * chips), mine.shape[1])
    return pl.pallas_call(
        backward_kernel,
        out_shape=(
            shaped(blocks, f32),
            shaped(blocks, b16),
            shaped((tok_count, width), f32),
            shaped((H, SEQ, SEQ), f32),
        ),
        in_specs=[SMEM] + [VMEM] * 17,
        out_specs=(VMEM,) * 4,
        scratch_shapes=[pltpu.VMEM((tok_count, width), b16)] * 4,
        name="layer_backward",
    )(
        index, back, logit_back, cot, hidden, second, flat, att, low, high, normed, q, k, v,
        mine, other, tokens, gains,
    )


def core_split(parts, core):
    half = parts[0].shape[1] // 2
    keep = [jnp.where(core == 0, p[:, :half], p[:, half:]) for p in parts]
    send = [jnp.where(core == 0, p[:, half:], p[:, :half]) for p in parts]
    return keep, send


def core_join(mine, other, core, axis=1):
    return jnp.concatenate(
        [jnp.where(core == 0, mine, other), jnp.where(core == 0, other, mine)], axis
    )


def gather_pieces(keep, send, chips, core):
    got = swap(send, "expert", 1)
    block = core_join(keep, got, core, 0)
    found = chip_gather(block, chips)
    pieces = []
    for parity, part in enumerate((found[: chips // 2], found[chips // 2 :])):
        first, second = dp_steps(parity)
        part = jnp.stack(part)
        near = jnp.stack([part, swap(part, "dp", first)])
        far = swap(near, "dp", second)
        pieces += [near, far]
    return pieces


def partner_pieces(pieces):
    result = []
    for piece in pieces:
        result.append(swap(piece, "expert", 1))
    return result


def scatter_blocks(keep, send, column, lane_at, parts, chips, core):
    replicas = lax.axis_size("dp")
    got = swap(send, "expert", 1)
    lane = lax.broadcasted_iota(jnp.int32, keep.shape, 3)
    blocks = jnp.where(lane == lane_at, column[..., None], keep + got.astype(jnp.float32))
    lower, upper = blocks[:, : chips // 2], blocks[:, chips // 2 :]
    lower = dp_reduce([lower[k] for k in range(replicas)], 0)
    upper = dp_reduce([upper[k] for k in range(replicas)], 1)
    chip_blocks = [lower[k] for k in range(chips // 2)] + [upper[k] for k in range(chips // 2)]
    arrived = [swap(bf(chip_blocks[k]), "expert", 2 * k) for k in range(1, chips)]
    block = chip_blocks[0]
    for piece in arrived:
        block = block + piece.astype(jnp.float32)
    rows = block.shape[0] // 2
    mine = jnp.where(core == 0, block[:rows], block[rows:])
    theirs = jnp.where(core == 0, block[rows:], block[:rows])
    payload = block.shape[1] - LANES
    half = payload // parts
    got = swap(bf(theirs[:, :payload]), "expert", 1).astype(jnp.float32)
    result = [
        core_join(mine[:, i * half : (i + 1) * half], got[:, i * half : (i + 1) * half], core)
        for i in range(parts)
    ]
    return result, mine[:, payload:]


def slot_positions(routes, experts):
    flat = routes.reshape(-1)
    expert_hot = (flat[:, None] == jnp.arange(experts, dtype=jnp.int32)[None, :]).astype(jnp.int32)
    earlier = jnp.cumsum(expert_hot, axis=0) - expert_hot
    return jnp.sum(earlier * expert_hot, axis=1).reshape(routes.shape)


def per_device(
    tokens,
    cotangent,
    buckets,
    routes,
    gain_attn,
    gain_moe,
    rel_bias,
    w_query,
    w_key,
    w_value,
    w_out,
    w_router,
    w_gate,
    w_up,
    w_down,
):
    f32 = jnp.float32
    groups = lax.axis_size("expert")
    chips = groups // 2
    replicas = lax.axis_size("dp")
    expert_index, dp_index = lax.axis_index("expert"), lax.axis_index("dp")
    core, chip_index = expert_index & 1, expert_index >> 1

    shard_rows = w_query.shape[0]
    experts = w_router.shape[1]
    n_bias = rel_bias.shape[0]
    small = jnp.concatenate(
        [
            w_router,
            gain_attn[:, None],
            gain_moe[:, None],
            jnp.pad(rel_bias, (0, shard_rows - n_bias))[:, None],
            jnp.zeros((shard_rows, LANES - experts - 3), jnp.bfloat16),
        ],
        axis=1,
    )
    model_width = tokens.shape[1]
    half = model_width // 2
    index = jnp.stack([dp_index, chip_index, jnp.int32(experts), core]).astype(jnp.int32)
    keep, send = core_split([w_query, w_key, w_value, w_out], core)
    pieces = gather_pieces(
        jnp.concatenate(keep + [small], 1), jnp.concatenate(send + [small], 1), chips, core
    )
    others = partner_pieces(pieces)
    lane_ids = jnp.arange(model_width, dtype=jnp.int32)
    in_row = lane_ids % shard_rows
    flat_at = jnp.where(in_row < n_bias, lane_ids // shard_rows * n_bias + in_row, -1)
    head_of = jnp.where(flat_at >= 0, flat_at % H, -1)[None, :]
    bucket_of = jnp.where(flat_at >= 0, flat_at // H, -1)[:, None]
    hot = bf(bucket_of == jnp.arange(LANES, dtype=jnp.int32)[None, :])

    tok_count = tokens.shape[0]
    local_experts = w_gate.shape[0]
    capacity = max(2, 9 * tok_count // (4 * experts))
    unit = 2 * capacity
    chip_unit = local_experts * unit
    n_rows = chips * chip_unit
    group = routes // local_experts
    rel_core = (group & 1) ^ core
    rel_chip = (group >> 1) ^ chip_index
    targets = (
        rel_core * n_rows
        + rel_chip * chip_unit
        + (routes % local_experts) * unit
        + rel_core * capacity
        + slot_positions(routes, experts)
    )
    partner_targets = swap(targets, "expert", 1)
    partner_cot = swap(cotangent, "expert", 1)
    row_ids = jnp.arange(n_rows, dtype=jnp.int32)
    pick_own = [bf(row_ids[:, None] == targets[None, :, k]) for k in range(2)]
    pick_partner = [bf(row_ids[:, None] + n_rows == partner_targets[None, :, k]) for k in range(2)]
    return_ids = jnp.arange(2 * n_rows, dtype=jnp.int32)
    unpick = [bf(targets[:, k][:, None] == return_ids[None, :]) for k in range(2)]
    route_hot = (
        routes[:, :, None] == jnp.arange(experts, dtype=jnp.int32)[None, None, :]
    ).astype(f32)

    forward = layer_forward(index, pieces, others, tokens, buckets, routes, head_of, hot, experts)
    hidden_one, normed_two, gate_lanes = forward[10:13]
    partner_normed = swap(normed_two, "expert", 1)
    partner_gates = swap(gate_lanes, "expert", 1)
    gates = gate_lanes[:, :2]

    def dispatch(rows):
        found = [rows[:chip_unit]] + [
            swap(rows[k * chip_unit : (k + 1) * chip_unit], "expert", 2 * k)
            for k in range(1, chips)
        ]
        return [
            dp_gather(jnp.concatenate([f[e * unit : (e + 1) * unit] for f in found], 0), e % 2)
            for e in range(local_experts)
        ]

    picks = jnp.concatenate([pick_own[0] + pick_own[1], pick_partner[0] + pick_partner[1]], 1)
    rows = dispatch(bf(matmul(picks, jnp.concatenate([normed_two, partner_normed], 0))))
    grad_picks = jnp.concatenate(pick_own + pick_partner, 1)
    grads = dispatch(
        bf(
            matmul(
                grad_picks,
                jnp.concatenate(
                    [bf(gates[:, k : k + 1] * cotangent) for k in range(2)]
                    + [bf(partner_gates[:, k : k + 1] * partner_cot) for k in range(2)],
                    0,
                ),
            )
        ),
    )

    def reduce_rows(parts, e):
        split = parts.reshape(replicas, chips * unit, model_width)
        return bf(dp_reduce([split[k] for k in range(replicas)], e % 2))

    def send_home(totals):
        found = [
            jnp.concatenate([t[k * unit : (k + 1) * unit] for t in totals], 0)
            for k in range(chips)
        ]
        found = found[:1] + [swap(found[k], "expert", 2 * k) for k in range(1, chips)]
        mine = jnp.concatenate(found, 0)
        return jnp.concatenate([mine, swap(mine, "expert", 1)], 0)

    rows_e = [jnp.concatenate(rows[e], 0) for e in range(local_experts)]
    grads_e = [jnp.concatenate(grads[e], 0) for e in range(local_experts)]
    acts, saved, out_totals = [], [], []
    for e in range(local_experts):
        gate_pre = matmul(rows_e[e], w_gate[e])
        up_pre = matmul(rows_e[e], w_up[e])
        act = bf(geglu(gate_pre, up_pre))
        act, gate_pre, up_pre = lax.optimization_barrier((act, gate_pre, up_pre))
        acts.append(act)
        saved.append((gate_pre, up_pre))
        part = matmul_nt(act, w_down[e])
        out_totals.append(reduce_rows(part, e))
    back_totals, pres = [], []
    for e in range(local_experts):
        _, vjp = jax.vjp(geglu, *saved[e])
        gate_back_pre, up_back_pre = vjp(matmul(grads_e[e], w_down[e]))
        gate_back_pre, up_back_pre = bf(gate_back_pre), bf(up_back_pre)
        pres.append((gate_back_pre, up_back_pre))
        part = matmul_nt(gate_back_pre, w_gate[e]) + matmul_nt(up_back_pre, w_up[e])
        back_totals.append(reduce_rows(part, e))
    down_grad = jnp.stack([matmul_tn(grads_e[e], acts[e]) for e in range(local_experts)])
    gate_grad = jnp.stack([matmul_tn(rows_e[e], pres[e][0]) for e in range(local_experts)])
    up_grad = jnp.stack([matmul_tn(rows_e[e], pres[e][1]) for e in range(local_experts)])

    returned = send_home(out_totals)
    back_rows = send_home(back_totals)
    late_cot, returned, late_gates = lax.optimization_barrier((cotangent, returned, gates))
    first_out, second_out = matmul(unpick[0], returned), matmul(unpick[1], returned)
    layer_out = hidden_one + late_gates[:, 0:1] * first_out + late_gates[:, 1:2] * second_out
    gate_back = jnp.stack(
        [jnp.sum(late_cot * first_out, axis=-1), jnp.sum(late_cot * second_out, axis=-1)], axis=1
    )
    chosen_back = late_gates * (gate_back - jnp.sum(late_gates * gate_back, axis=-1, keepdims=True))
    logit_back = bf(jnp.sum(route_hot * chosen_back[:, :, None], axis=1))
    logit_back = jnp.pad(logit_back, ((0, 0), (0, LANES - experts)))
    token_back = matmul(unpick[0] + unpick[1], back_rows)
    keep, send, tokens_grad, score_back = layer_backward(
        index, token_back, logit_back, late_cot, forward, tokens, chips, replicas
    )
    bucket_hot = bf(buckets[None] == jnp.arange(NB, dtype=jnp.int32)[:, None, None])
    score_high = bf(score_back)
    score_low = bf(score_back - score_high.astype(f32))
    bias_grad = sum(
        lax.dot_general(bucket_hot, x, (((1, 2), (1, 2)), ((), ())), preferred_element_type=f32)
        for x in (score_high, score_low)
    )
    bias_grad = core_join(bias_grad[:, : H // 2], bias_grad[:, H // 2 :], core)
    bias_grad = jnp.pad(bias_grad, ((0, 0), (0, LANES - H)))
    bias_grad = (bias_grad + swap(bias_grad, "expert", 1))[:, :H].reshape(-1, n_bias)
    column = jnp.pad(bias_grad, ((0, 0), (0, shard_rows - n_bias)))
    column = column.reshape(replicas, chips, -1)
    column = xor_order(xor_order(column, dp_index, 0), chip_index, 1)
    (query_total, key_total, value_total, out_total), small_total = scatter_blocks(
        keep, send, column, 4 * half + experts + 2, 4, chips, core
    )
    return (
        layer_out,
        tokens_grad,
        small_total[:, experts],
        small_total[:, experts + 1],
        small_total[:n_bias, experts + 2],
        query_total,
        key_total,
        value_total,
        out_total,
        small_total[:, :experts],
        gate_grad,
        up_grad,
        down_grad,
    )


def solution(mesh):
    both = ("dp", "expert")
    row = P(both, None)

    return jax.shard_map(
        per_device,
        mesh=mesh,
        in_specs=(row, row, P(), row, P(both), P(both), P(both), row, row, row, row, row)
        + (P("expert", None, "dp"),) * 3,
        out_specs=(row, row, P(both), P(both), P(both), row, row, row, row, row)
        + (P("expert", None, "dp"),) * 3,
        check_vma=False,
    )
```

```python
import functools
import math

import jax
import jax.numpy as jnp
from jax import lax
from jax.experimental import pallas as pl
from jax.experimental.pallas import tpu as pltpu
from jax.sharding import PartitionSpec as P


H = 12
DH = 64
NB = 32
SEQ = 256
LANES = 128

EPSILON = 1e-06


def rms_apply(hidden, gain):
    factor = lax.rsqrt(jnp.mean(hidden * hidden, axis=-1, keepdims=True) + EPSILON)
    return hidden * factor * gain


def geglu(gate_pre, up_pre):
    return jax.nn.gelu(gate_pre, approximate=True) * up_pre


def matmul(left, right):
    return jnp.dot(left, right, preferred_element_type=jnp.float32)


def matmul_nt(left, right):
    return lax.dot_general(left, right, (((1,), (1,)), ((), ())), preferred_element_type=jnp.float32)


def matmul_tn(left, right):
    return lax.dot_general(left, right, (((0,), (0,)), ((), ())), preferred_element_type=jnp.float32)


def bf(value):
    return value.astype(jnp.bfloat16)


def swap(value, axis, distance):
    size = lax.axis_size(axis)
    return lax.ppermute(value, axis, [(i, i ^ distance) for i in range(size)])


def xor_order(blocks, index, axis):
    size = blocks.shape[axis]
    bit = 1
    while bit < size:
        shape = blocks.shape
        split = shape[:axis] + (size // (2 * bit), 2, bit) + shape[axis + 1 :]
        view = blocks.reshape(split)
        blocks = jnp.where((index & bit) != 0, jnp.flip(view, axis + 1), view).reshape(shape)
        bit *= 2
    return blocks


def dp_steps(parity):
    return (1, 2) if parity == 0 else (2, 1)


def dp_gather(block, parity):
    first, second = dp_steps(parity)
    near = swap(block, "dp", first)
    pair = jnp.stack([block, near])
    far = swap(pair, "dp", second)
    found = {0: block, first: near, second: far[0], first | second: far[1]}
    return [found[k] for k in range(4)]


def dp_reduce(parts, parity):
    second, first = dp_steps(parity)
    got = swap(jnp.stack([bf(parts[first]), bf(parts[first | second])]), "dp", first)
    mine = parts[0] + got[0].astype(jnp.float32)
    other = parts[second] + got[1].astype(jnp.float32)
    last = swap(bf(other), "dp", second)
    return mine + last.astype(jnp.float32)


def chip_gather(block, chips):
    return [block] + [swap(block, "expert", 2 * k) for k in range(1, chips)]


SMEM = pl.BlockSpec(memory_space=pltpu.SMEM)
VMEM = pl.BlockSpec(memory_space=pltpu.VMEM)


def place_kernel(index_ref, near_low, far_low, near_up, far_up, out_ref):
    dp_index, chip_index = index_ref[0], index_ref[1]
    half = near_low.shape[1]
    for pieces, parity, base in (((near_low, far_low), 0, 0), ((near_up, far_up), 1, half)):
        first, second = dp_steps(parity)
        for far in range(2):
            for i in range(2):
                step = first * i + second * far
                for j in range(half):
                    out_ref[dp_index ^ step, chip_index ^ (base + j)] = pieces[far][i, j]


def place(index, pieces):
    _, half, rows, width = pieces[0].shape
    return pl.pallas_call(
        place_kernel,
        out_shape=jax.ShapeDtypeStruct((4, 2 * half, rows, width), pieces[0].dtype),
        in_specs=[SMEM] + [VMEM] * 4,
        out_specs=VMEM,
        name="place_weights",
    )(index, *pieces).reshape(-1, width)


def core_pick(core, first, second):
    return jnp.where(jnp.broadcast_to(core, first.shape) == 0, first, second)


def forward_kernel(placed, experts, *refs):
    if placed:
        index_ref, *refs = refs
        pieces, refs = refs[:8], refs[8:]
        tok_ref, bucket_ref, route_ref, head_ref, hot_ref, mine_ref, other_ref, *refs = refs
        dp_index, chip_index = index_ref[0], index_ref[1]
        half_chips, rows = pieces[0].shape[1:3]
        for out, group in ((mine_ref, pieces[:4]), (other_ref, pieces[4:])):
            for parity in range(2):
                first, second = dp_steps(parity)
                for far in range(2):
                    for i in range(2):
                        dp_at = dp_index ^ (first * i + second * far)
                        for j in range(half_chips):
                            chip_at = chip_index ^ (half_chips * parity + j)
                            at = pl.multiple_of((dp_at * 2 * half_chips + chip_at) * rows, rows)
                            out[pl.ds(at, rows), :] = group[2 * parity + far][i, j]
    else:
        index_ref, mine_ref, other_ref, tok_ref, bucket_ref, route_ref, head_ref, hot_ref, *refs = refs
    n_ref, q_ref, k_ref, v_ref, low_ref, high_ref, att_ref, flat_ref = refs[:8]
    hidden_ref, second_ref, gate_ref, gain_ref, bias_ref = refs[8:]
    f32 = jnp.float32
    core = index_ref[3]
    half_seq = SEQ // 2
    half = q_ref.shape[1] // 2
    small = mine_ref[:, 4 * half :]
    vectors = small.astype(f32).T
    gain_ref[...] = vectors[experts : experts + 2]
    rows16 = lax.broadcasted_iota(jnp.int32, (16, vectors.shape[1]), 0)
    shifted = rows16 + core * (H // 2)
    wanted = jnp.where(rows16 < H, jnp.where(shifted >= H, shifted - H, shifted), -2)
    spread = jnp.where(head_ref[...] == wanted, vectors[experts + 2 : experts + 3], 0.0)
    bias_ref[...] = matmul(bf(spread), hot_ref[...])

    hidden = tok_ref[...].astype(f32)
    normed = bf(rms_apply(hidden, gain_ref[0:1]))
    n_ref[...] = normed
    for part, out in enumerate((q_ref, k_ref, v_ref)):
        cut = slice(part * half, (part + 1) * half)
        out[:, :half] = bf(matmul(normed, mine_ref[:, cut]))
        out[:, half:] = bf(matmul(normed, other_ref[:, cut]))
    scale = 1.0 / math.sqrt(DH)
    row_ids = lax.broadcasted_iota(jnp.int32, (half_seq, half_seq), 0)
    col_ids = lax.broadcasted_iota(jnp.int32, (half_seq, half_seq), 1)
    causal = row_ids >= col_ids

    def biased(raw, head, rows, cols):
        table = jnp.broadcast_to(bias_ref[pl.ds(head, 1), :], (half_seq, LANES))
        return raw * scale + jnp.take_along_axis(table, bucket_ref[rows, cols], axis=1)

    def softmax(blocks):
        peak = blocks[0].max(-1, keepdims=True)
        for b in blocks[1:]:
            peak = jnp.maximum(peak, b.max(-1, keepdims=True))
        exps = [jnp.exp(b - peak) for b in blocks]
        total = sum(x.sum(-1, keepdims=True) for x in exps)
        inverse = 1.0 / total
        return [x * inverse for x in exps]

    first, second = slice(0, half_seq), slice(half_seq, SEQ)

    def pair_step(pair, carry):
        lanes = pl.ds(pl.multiple_of(pair * 2 * DH, 2 * DH), 2 * DH)
        qp, kp, vp = q_ref[:, lanes], k_ref[:, lanes], v_ref[:, lanes]
        outs_low, outs_high = [], []
        for sub in range(2):
            head = pair * 2 + sub
            cut = slice(sub * DH, (sub + 1) * DH)
            q, k, v = qp[:, cut], kp[:, cut], vp[:, cut]
            s00 = biased(matmul_nt(q[first], k[first]), head, first, first)
            s1 = matmul_nt(q[second], k)
            s10 = biased(s1[:, first], head, second, first)
            s11 = biased(s1[:, second], head, second, second)
            (p00,) = softmax([jnp.where(causal, s00, -1e30)])
            p10, p11 = softmax([s10, jnp.where(causal, s11, -1e30)])
            low_ref[head] = p00
            high_ref[head, :, first] = p10
            high_ref[head, :, second] = p11
            outs_low.append(matmul(bf(p00), v[first]))
            outs_high.append(matmul(bf(p10), v[first]) + matmul(bf(p11), v[second]))
        att_ref[first, lanes] = bf(jnp.concatenate(outs_low, 1))
        att_ref[second, lanes] = bf(jnp.concatenate(outs_high, 1))
        return carry

    lax.fori_loop(0, H // 2, pair_step, 0)
    att_mine, att_other = att_ref[:, :half].astype(f32), att_ref[:, half:].astype(f32)
    flat_ref[:, :half] = bf(core_pick(core, att_mine, att_other))
    flat_ref[:, half:] = bf(core_pick(core, att_other, att_mine))
    flat = flat_ref[...]
    cut = slice(3 * half, 4 * half)
    out_mine, out_other = matmul(flat, mine_ref[:, cut]), matmul(flat, other_ref[:, cut])
    hidden_ref[:, :half] = hidden[:, :half] + core_pick(core, out_mine, out_other)
    hidden_ref[:, half:] = hidden[:, half:] + core_pick(core, out_other, out_mine)
    normed_two = bf(rms_apply(hidden_ref[...], gain_ref[1:2]))
    second_ref[...] = normed_two
    logits = matmul(normed_two, small)
    lane = lax.broadcasted_iota(jnp.int32, logits.shape, 1)
    chosen = [
        jnp.sum(jnp.where(lane == route_ref[:, k : k + 1], logits, 0.0), 1, keepdims=True)
        for k in range(2)
    ]
    peak = jnp.maximum(chosen[0], chosen[1])
    exps = [jnp.exp(c - peak) for c in chosen]
    total = exps[0] + exps[1]
    gate_ref[...] = jnp.where(lane == 0, exps[0] / total, jnp.where(lane == 1, exps[1] / total, 0.0))


def layer_forward(index, mine, other, tokens, buckets, routes, head_of, hot, experts):
    tok_count, width = tokens.shape
    b16, f32 = jnp.bfloat16, jnp.float32
    shaped = jax.ShapeDtypeStruct
    flat, total = shaped((tok_count, width), b16), mine[0].shape[-1]
    placed = mine[0].shape[2] % 16 == 0
    weights = (shaped((width, total), b16),) * 2
    if placed:
        inputs = tuple(mine) + tuple(other)
    else:
        inputs = (place(index, mine), place(index, other))
    tail = (tokens, buckets, routes, head_of, hot)
    result = pl.pallas_call(
        functools.partial(forward_kernel, placed, experts),
        out_shape=(weights if placed else ())
        + (flat, flat, flat, flat)
        + (shaped((H, SEQ // 2, SEQ // 2), f32), shaped((H, SEQ // 2, SEQ), f32), flat, flat)
        + (shaped((tok_count, width), f32), flat, shaped((tok_count, LANES), f32), shaped((2, width), f32)),
        in_specs=[SMEM] + [VMEM] * (len(inputs) + len(tail)),
        out_specs=(VMEM,) * (14 if placed else 12),
        scratch_shapes=[pltpu.VMEM((16, LANES), f32)],
        name="layer_forward",
    )(index, *inputs, *tail)
    return result if placed else inputs + result


def pick_rows(target_ref, k, at, count):
    ids = lax.broadcasted_iota(jnp.int32, (target_ref.shape[0], count), 1) + at
    return (ids == target_ref[:, k : k + 1]).astype(jnp.float32)


def combine_kernel(
    ret_mine_ref, ret_other_ref, target_ref, route_ref, gate_ref, cot_ref, hidden_ref, out_ref, logit_ref
):
    count = ret_mine_ref.shape[0]
    gates = [gate_ref[:, k : k + 1] for k in range(2)]
    total = hidden_ref[...]
    backs = []
    for k in range(2):
        value = matmul(bf(pick_rows(target_ref, k, 0, count)), ret_mine_ref[...])
        value += matmul(bf(pick_rows(target_ref, k, count, count)), ret_other_ref[...])
        total += gates[k] * value
        backs.append(jnp.sum(cot_ref[...] * value, axis=1, keepdims=True))
    out_ref[...] = total
    mean = gates[0] * backs[0] + gates[1] * backs[1]
    lane = lax.broadcasted_iota(jnp.int32, logit_ref.shape, 1)
    logit = jnp.zeros(logit_ref.shape, jnp.float32)
    for k in range(2):
        logit += jnp.where(lane == route_ref[:, k : k + 1], gates[k] * (backs[k] - mean), 0.0)
    logit_ref[...] = bf(logit)


def combine(returned, targets, routes, gate_lanes, cot, hidden):
    shaped = jax.ShapeDtypeStruct
    return pl.pallas_call(
        combine_kernel,
        out_shape=(
            shaped(hidden.shape, jnp.float32),
            shaped((hidden.shape[0], LANES), jnp.bfloat16),
        ),
        in_specs=[VMEM] * 7,
        out_specs=(VMEM,) * 2,
        name="combine_experts",
    )(*returned, targets, routes, gate_lanes, cot, hidden)


def pack_kernel(index_ref, q_ref, k_ref, v_ref, o_ref, router_ref, one_ref, two_ref, bias_ref, keep_ref, send_ref, pad_ref):
    core, experts = index_ref[3], router_ref.shape[1]
    rows, width = q_ref.shape
    half = width // 2
    f32 = jnp.float32
    for i, ref in enumerate((q_ref, k_ref, v_ref, o_ref)):
        left, right = ref[:, :half].astype(f32), ref[:, half:].astype(f32)
        keep_ref[:, i * half : (i + 1) * half] = bf(core_pick(core, left, right))
        send_ref[:, i * half : (i + 1) * half] = bf(core_pick(core, right, left))
    pad_ref[...] = jnp.zeros(pad_ref.shape, f32)
    for i, ref in enumerate((one_ref, two_ref, bias_ref)):
        pad_ref[experts + i : experts + i + 1, : ref.shape[1]] = ref[...].astype(f32)
    small = pad_ref[...].T[:rows]
    pad_ref[:rows, :experts] = router_ref[...].astype(f32)
    lane = lax.broadcasted_iota(jnp.int32, small.shape, 1)
    small = bf(jnp.where(lane < experts, pad_ref[:rows], small))
    keep_ref[:, 4 * half :] = small
    send_ref[:, 4 * half :] = small


def pack(index, weights, router, vectors):
    rows, width = weights[0].shape
    out = jax.ShapeDtypeStruct((rows, 2 * width + LANES), jnp.bfloat16)
    return pl.pallas_call(
        pack_kernel,
        out_shape=(out, out),
        in_specs=[SMEM] + [VMEM] * 8,
        out_specs=(VMEM,) * 2,
        scratch_shapes=[pltpu.VMEM((LANES, LANES), jnp.float32)],
        name="pack_shards",
    )(index, *weights, router, *[v[None, :] for v in vectors])


def finish_kernel(index_ref, mine_ref, got_ref, q_ref, k_ref, v_ref, o_ref, router_ref, vector_ref):
    core, experts = index_ref[3], router_ref.shape[1]
    rows, width = q_ref.shape
    half = width // 2
    for i, ref in enumerate((q_ref, k_ref, v_ref, o_ref)):
        cut = slice(i * half, (i + 1) * half)
        mine, other = mine_ref[:, cut], got_ref[:, cut].astype(jnp.float32)
        ref[:, :half] = core_pick(core, mine, other)
        ref[:, half:] = core_pick(core, other, mine)
    small = mine_ref[:, 4 * half :]
    router_ref[...] = small[:, :experts]
    padded = jnp.concatenate([small, jnp.zeros((LANES - rows, LANES), jnp.float32)], 0)
    vector_ref[...] = padded.T[experts : experts + 3, :rows]


def finish(index, mine, got, experts):
    rows, width = mine.shape[0], (mine.shape[1] - LANES) // 2
    shaped = lambda *dims: jax.ShapeDtypeStruct(dims, jnp.float32)
    return pl.pallas_call(
        finish_kernel,
        out_shape=(shaped(rows, width),) * 4 + (shaped(rows, experts), shaped(3, rows)),
        in_specs=[SMEM] + [VMEM] * 2,
        out_specs=(VMEM,) * 6,
        name="finish_shared",
    )(index, mine, got)


def backward_kernel(
    index_ref, ret_mine_ref, ret_other_ref, target_ref, logit_ref, cot_ref, hidden_ref, second_ref, flat_ref, att_ref, low_ref, high_ref,
    n_ref, q_ref, k_ref, v_ref, mine_ref, other_ref, tok_ref, gain_ref,
    keep_ref, send_ref, grad_ref, score_ref, qb_ref, kb_ref, vb_ref, ab_ref,
):
    f32 = jnp.float32
    half_seq = SEQ // 2
    scale = 1.0 / math.sqrt(DH)
    first, second = slice(0, half_seq), slice(half_seq, SEQ)
    half = ab_ref.shape[1] // 2
    replicas, chips, rows, width = keep_ref.shape
    dp_index, chip_index, experts, core = (index_ref[i] for i in range(4))
    payload = 4 * half

    def store(out, cut, value):
        for i in range(replicas):
            for j in range(chips):
                at = (i * chips + j) * rows
                out[dp_index ^ i, chip_index ^ j, :, cut] = value[at : at + rows]

    def norm_back(hidden, gain, upstream):
        factor = lax.rsqrt(jnp.mean(hidden * hidden, axis=-1, keepdims=True) + EPSILON)
        scaled = upstream * gain
        inner = jnp.mean(scaled * hidden, axis=-1, keepdims=True)
        gain_back = jnp.sum(upstream * (hidden * factor), axis=0, keepdims=True)
        return factor * (scaled - hidden * (factor * factor * inner)), gain_back

    token_back = jnp.zeros(tok_ref.shape, f32)
    for at, ref in ((0, ret_mine_ref), (ret_mine_ref.shape[0], ret_other_ref)):
        picked = sum(pick_rows(target_ref, k, at, ref.shape[0]) for k in range(2))
        token_back += matmul(bf(picked), ref[...])
    logit_back = logit_ref[...]
    small_w = mine_ref[:, payload:]
    hidden_back, gain_two_back = norm_back(
        hidden_ref[...], gain_ref[1:2], token_back + matmul_nt(logit_back, small_w)
    )
    hidden_back = cot_ref[...] + hidden_back
    grad_ref[...] = hidden_back
    left, right = hidden_back[:, :half], hidden_back[:, half:]
    res_mine, res_other = bf(core_pick(core, left, right)), bf(core_pick(core, right, left))
    cut = slice(3 * half, payload)
    ab = matmul_nt(res_mine, mine_ref[:, cut]) + matmul_nt(res_other, other_ref[:, cut])
    left, right = ab[:, :half], ab[:, half:]
    ab_ref[:, :half] = bf(core_pick(core, left, right))
    ab_ref[:, half:] = bf(core_pick(core, right, left))
    flat = flat_ref[...]
    store(keep_ref, cut, matmul_tn(flat, res_mine))
    store(send_ref, cut, bf(matmul_tn(flat, res_other)))

    def pair_step(pair, carry):
        lanes = pl.ds(pl.multiple_of(pair * 2 * DH, 2 * DH), 2 * DH)
        qp, kp, vp = q_ref[:, lanes], k_ref[:, lanes], v_ref[:, lanes]
        abp, attp = ab_ref[:, lanes], att_ref[:, lanes]
        found = [[], [], []]
        for sub in range(2):
            head = pair * 2 + sub
            cut = slice(sub * DH, (sub + 1) * DH)
            q, k, v, ab, att = qp[:, cut], kp[:, cut], vp[:, cut], abp[:, cut], attp[:, cut]
            delta = jnp.sum(ab.astype(f32) * att.astype(f32), axis=1, keepdims=True)
            low, high = low_ref[head], high_ref[head]
            low_b, high_b = bf(low), bf(high)
            value_low = matmul_tn(low_b, ab[first])
            value_high = matmul_tn(high_b, ab[second])
            found[2].append(
                jnp.concatenate([value_low + value_high[first], value_high[second]], 0)
            )
            back_low = low * (matmul_nt(ab[first], v[first]) - delta[first])
            back_high = high * (matmul_nt(ab[second], v) - delta[second])
            low_r, high_r = bf(back_low), bf(back_high)
            for at, low_s, high_s in (
                (head, low_r, high_r),
                (head + H, bf(back_low - low_r.astype(f32)), bf(back_high - high_r.astype(f32))),
            ):
                score_ref[at, first, first] = low_s
                score_ref[at, first, second] = jnp.zeros_like(low_s)
                score_ref[at, second, :] = high_s
            found[0].append(
                jnp.concatenate([matmul(low_r, k[first]), matmul(high_r, k)], 0) * scale
            )
            key_low = matmul_tn(low_r, q[first])
            key_high = matmul_tn(high_r, q[second])
            found[1].append(
                jnp.concatenate([key_low + key_high[first], key_high[second]], 0) * scale
            )
        for out, value in zip((qb_ref, kb_ref, vb_ref), found):
            out[:, lanes] = bf(jnp.concatenate(value, 1))
        return carry

    lax.fori_loop(0, H // 2, pair_step, 0)

    normed = n_ref[...]
    normed_back = jnp.zeros(tok_ref.shape, f32)
    for part, ref in enumerate((qb_ref, kb_ref, vb_ref)):
        cut = slice(part * half, (part + 1) * half)
        mine_b, other_b = ref[:, :half], ref[:, half:]
        store(keep_ref, cut, matmul_tn(normed, mine_b))
        store(send_ref, cut, bf(matmul_tn(normed, other_b)))
        normed_back += matmul_nt(mine_b, mine_ref[:, cut]) + matmul_nt(other_b, other_ref[:, cut])
    token_back, gain_one_back = norm_back(tok_ref[...].astype(f32), gain_ref[0:1], normed_back)
    grad_ref[...] += token_back
    small = matmul_tn(second_ref[...], logit_back)
    lane = lax.broadcasted_iota(jnp.int32, small.shape, 1)
    for at, gain_back in ((experts, gain_one_back), (experts + 1, gain_two_back)):
        wide = jnp.broadcast_to(gain_back, (LANES, gain_back.shape[1])).T
        small = jnp.where(lane == at, wide, small)
    store(keep_ref, slice(payload, width), small)
    store(send_ref, slice(payload, width), bf(small))


def layer_backward(index, returned, targets, logit_back, cot, forward, tokens, chips, replicas):
    mine, other, normed, q, k, v, low, high, att, flat, hidden, second, _, gains = forward
    tok_count, width = tokens.shape
    b16, f32 = jnp.bfloat16, jnp.float32
    shaped = jax.ShapeDtypeStruct
    blocks = (replicas, chips, width // (replicas * chips), mine.shape[1])
    return pl.pallas_call(
        backward_kernel,
        out_shape=(
            shaped(blocks, f32),
            shaped(blocks, b16),
            shaped((tok_count, width), f32),
            shaped((2 * H, SEQ, SEQ), b16),
        ),
        in_specs=[SMEM] + [VMEM] * 19,
        out_specs=(VMEM,) * 4,
        scratch_shapes=[pltpu.VMEM((tok_count, width), b16)] * 4,
        name="layer_backward",
    )(
        index, *returned, targets, logit_back, cot, hidden, second, flat, att, low, high, normed, q, k, v,
        mine, other, tokens, gains,
    )


def core_join(mine, other, core, axis=1):
    return jnp.concatenate(
        [jnp.where(core == 0, mine, other), jnp.where(core == 0, other, mine)], axis
    )


def gather_pieces(keep, send, chips, core):
    got = swap(send, "expert", 1)
    block = core_join(keep, got, core, 0)
    found = chip_gather(block, chips)
    pieces = []
    for parity, part in enumerate((found[: chips // 2], found[chips // 2 :])):
        first, second = dp_steps(parity)
        part = jnp.stack(part)
        near = jnp.stack([part, swap(part, "dp", first)])
        far = swap(near, "dp", second)
        pieces += [near, far]
    return pieces


def partner_pieces(pieces):
    result = []
    for piece in pieces:
        result.append(swap(piece, "expert", 1))
    return result


def scatter_blocks(keep, send, column, lane_at, chips, core):
    replicas = lax.axis_size("dp")
    got = swap(send, "expert", 1)
    lane = lax.broadcasted_iota(jnp.int32, keep.shape, 3)
    blocks = jnp.where(lane == lane_at, column[..., None], keep + got.astype(jnp.float32))
    lower, upper = blocks[:, : chips // 2], blocks[:, chips // 2 :]
    lower = dp_reduce([lower[k] for k in range(replicas)], 0)
    upper = dp_reduce([upper[k] for k in range(replicas)], 1)
    chip_blocks = [lower[k] for k in range(chips // 2)] + [upper[k] for k in range(chips // 2)]
    arrived = [swap(bf(chip_blocks[k]), "expert", 2 * k) for k in range(1, chips)]
    block = chip_blocks[0]
    for piece in arrived:
        block = block + piece.astype(jnp.float32)
    rows = block.shape[0] // 2
    mine = jnp.where(core == 0, block[:rows], block[rows:])
    theirs = jnp.where(core == 0, block[rows:], block[:rows])
    got = swap(bf(theirs[:, : block.shape[1] - LANES]), "expert", 1)
    return mine, got


def slot_positions(routes, experts):
    flat = routes.reshape(-1)
    expert_hot = (flat[:, None] == jnp.arange(experts, dtype=jnp.int32)[None, :]).astype(jnp.int32)
    earlier = jnp.cumsum(expert_hot, axis=0) - expert_hot
    return jnp.sum(earlier * expert_hot, axis=1).reshape(routes.shape)


def per_device(
    tokens,
    cotangent,
    buckets,
    routes,
    gain_attn,
    gain_moe,
    rel_bias,
    w_query,
    w_key,
    w_value,
    w_out,
    w_router,
    w_gate,
    w_up,
    w_down,
):
    f32 = jnp.float32
    groups = lax.axis_size("expert")
    chips = groups // 2
    replicas = lax.axis_size("dp")
    expert_index, dp_index = lax.axis_index("expert"), lax.axis_index("dp")
    core, chip_index = expert_index & 1, expert_index >> 1

    shard_rows = w_query.shape[0]
    experts = w_router.shape[1]
    n_bias = rel_bias.shape[0]
    model_width = tokens.shape[1]
    half = model_width // 2
    index = jnp.stack([dp_index, chip_index, jnp.int32(experts), core]).astype(jnp.int32)
    keep, send = pack(
        index,
        (w_query, w_key, w_value, w_out),
        w_router,
        (gain_attn, gain_moe, rel_bias),
    )
    pieces = gather_pieces(keep, send, chips, core)
    others = partner_pieces(pieces)
    lane_ids = jnp.arange(model_width, dtype=jnp.int32)
    in_row = lane_ids % shard_rows
    flat_at = jnp.where(in_row < n_bias, lane_ids // shard_rows * n_bias + in_row, -1)
    head_of = jnp.where(flat_at >= 0, flat_at % H, -1)[None, :]
    bucket_of = jnp.where(flat_at >= 0, flat_at // H, -1)[:, None]
    hot = bf(bucket_of == jnp.arange(LANES, dtype=jnp.int32)[None, :])

    tok_count = tokens.shape[0]
    local_experts = w_gate.shape[0]
    capacity = max(2, 9 * tok_count // (4 * experts))
    unit = 2 * capacity
    chip_unit = local_experts * unit
    n_rows = chips * chip_unit
    group = routes // local_experts
    rel_core = (group & 1) ^ core
    rel_chip = (group >> 1) ^ chip_index
    targets = (
        rel_core * n_rows
        + rel_chip * chip_unit
        + (routes % local_experts) * unit
        + rel_core * capacity
        + slot_positions(routes, experts)
    )
    partner_targets = swap(targets, "expert", 1)
    partner_cot = swap(cotangent, "expert", 1)
    row_ids = jnp.arange(n_rows, dtype=jnp.int32)
    pick_own = [bf(row_ids[:, None] == targets[None, :, k]) for k in range(2)]
    pick_partner = [bf(row_ids[:, None] + n_rows == partner_targets[None, :, k]) for k in range(2)]

    forward = layer_forward(index, pieces, others, tokens, buckets, routes, head_of, hot, experts)
    hidden_one, normed_two, gate_lanes = forward[10:13]
    partner_normed = swap(normed_two, "expert", 1)
    partner_gates = swap(gate_lanes, "expert", 1)
    gates = gate_lanes[:, :2]

    def dispatch(rows, split):
        def piece(k, e):
            at = k * chip_unit + e * unit
            return rows[at : at + unit]

        found = []
        if split:
            for e in range(local_experts):
                found.append(
                    [piece(0, e)] + [swap(piece(k, e), "expert", 2 * k) for k in range(1, chips)]
                )
        else:
            whole = [
                swap(rows[k * chip_unit : (k + 1) * chip_unit], "expert", 2 * k)
                for k in range(1, chips)
            ]
            for e in range(local_experts):
                found.append([piece(0, e)] + [w[e * unit : (e + 1) * unit] for w in whole])
        result = []
        for e in range(local_experts):
            block = jnp.concatenate(found[e], 0)
            result.append(dp_gather(block, e % 2))
        return result

    picks = jnp.concatenate([pick_own[0] + pick_own[1], pick_partner[0] + pick_partner[1]], 1)
    rows = dispatch(bf(matmul(picks, jnp.concatenate([normed_two, partner_normed], 0))), True)
    grad_picks = jnp.concatenate(pick_own + pick_partner, 1)
    grads = dispatch(
        bf(
            matmul(
                grad_picks,
                jnp.concatenate(
                    [bf(gates[:, k : k + 1] * cotangent) for k in range(2)]
                    + [bf(partner_gates[:, k : k + 1] * partner_cot) for k in range(2)],
                    0,
                ),
            )
        ),
        False,
    )

    def reduce_rows(parts, e):
        split = parts.reshape(replicas, chips * unit, model_width)
        return bf(dp_reduce([split[k] for k in range(replicas)], e % 2))

    def send_home(totals):
        found = [
            jnp.concatenate([t[k * unit : (k + 1) * unit] for t in totals], 0)
            for k in range(chips)
        ]
        found = found[:1] + [swap(found[k], "expert", 2 * k) for k in range(1, chips)]
        mine = jnp.concatenate(found, 0)
        return mine, swap(mine, "expert", 1)

    rows_e = [jnp.concatenate(rows[e], 0) for e in range(local_experts)]
    grads_e = [jnp.concatenate(grads[e], 0) for e in range(local_experts)]
    acts, saved, out_totals = [], [], []
    for e in range(local_experts):
        gate_pre = matmul(rows_e[e], w_gate[e])
        up_pre = matmul(rows_e[e], w_up[e])
        act = bf(geglu(gate_pre, up_pre))
        act, gate_pre, up_pre = lax.optimization_barrier((act, gate_pre, up_pre))
        acts.append(act)
        saved.append((gate_pre, up_pre))
        part = matmul_nt(act, w_down[e])
        out_totals.append(reduce_rows(part, e))
    back_totals, pres = [], []
    for e in range(local_experts):
        _, vjp = jax.vjp(geglu, *saved[e])
        gate_back_pre, up_back_pre = vjp(matmul(grads_e[e], w_down[e]))
        gate_back_pre, up_back_pre = bf(gate_back_pre), bf(up_back_pre)
        pres.append((gate_back_pre, up_back_pre))
        part = matmul_nt(gate_back_pre, w_gate[e]) + matmul_nt(up_back_pre, w_up[e])
        back_totals.append(reduce_rows(part, e))
    down_grad = jnp.stack([matmul_tn(grads_e[e], acts[e]) for e in range(local_experts)])
    gate_grad = jnp.stack([matmul_tn(rows_e[e], pres[e][0]) for e in range(local_experts)])
    up_grad = jnp.stack([matmul_tn(rows_e[e], pres[e][1]) for e in range(local_experts)])

    returned = send_home(out_totals)
    back_rows = send_home(back_totals)
    late_cot, *returned = lax.optimization_barrier((cotangent, *returned))
    layer_out, logit_back = combine(returned, targets, routes, gate_lanes, late_cot, hidden_one)
    keep, send, tokens_grad, score_back = layer_backward(
        index, back_rows, targets, logit_back, late_cot, forward, tokens, chips, replicas
    )
    bucket_hot = bf(buckets[None] == jnp.arange(NB, dtype=jnp.int32)[:, None, None])
    bias_grad = lax.dot_general(
        bucket_hot, score_back, (((1, 2), (1, 2)), ((), ())), preferred_element_type=f32
    )
    bias_grad = bias_grad[:, :H] + bias_grad[:, H:]
    bias_grad = core_join(bias_grad[:, : H // 2], bias_grad[:, H // 2 :], core)
    bias_grad = jnp.pad(bias_grad, ((0, 0), (0, LANES - H)))
    bias_grad = (bias_grad + swap(bias_grad, "expert", 1))[:, :H].reshape(-1, n_bias)
    column = jnp.pad(bias_grad, ((0, 0), (0, shard_rows - n_bias)))
    column = column.reshape(replicas, chips, -1)
    column = xor_order(xor_order(column, dp_index, 0), chip_index, 1)
    mine, got = scatter_blocks(keep, send, column, 4 * half + experts + 2, chips, core)
    query_total, key_total, value_total, out_total, router_total, vectors = finish(
        index, mine, got, experts
    )
    return (
        layer_out,
        tokens_grad,
        vectors[0],
        vectors[1],
        vectors[2, :n_bias],
        query_total,
        key_total,
        value_total,
        out_total,
        router_total,
        gate_grad,
        up_grad,
        down_grad,
    )


def solution(mesh):
    both = ("dp", "expert")
    row = P(both, None)

    return jax.shard_map(
        per_device,
        mesh=mesh,
        in_specs=(row, row, P(), row, P(both), P(both), P(both), row, row, row, row, row)
        + (P("expert", None, "dp"),) * 3,
        out_specs=(row, row, P(both), P(both), P(both), row, row, row, row, row)
        + (P("expert", None, "dp"),) * 3,
        check_vma=False,
    )
```

```python
import functools
import math

import jax
import jax.numpy as jnp
from jax import lax
from jax.experimental import pallas as pl
from jax.experimental.pallas import tpu as pltpu
from jax.sharding import PartitionSpec as P


H = 12
DH = 64
NB = 32
SEQ = 256
LANES = 128

EPSILON = 1e-06


def rms_apply(hidden, gain):
    factor = lax.rsqrt(jnp.mean(hidden * hidden, axis=-1, keepdims=True) + EPSILON)
    return hidden * factor * gain


def geglu(gate_pre, up_pre):
    return jax.nn.gelu(gate_pre, approximate=True) * up_pre


def matmul(left, right):
    return jnp.dot(left, right, preferred_element_type=jnp.float32)


def matmul_nt(left, right):
    return lax.dot_general(left, right, (((1,), (1,)), ((), ())), preferred_element_type=jnp.float32)


def matmul_tn(left, right):
    return lax.dot_general(left, right, (((0,), (0,)), ((), ())), preferred_element_type=jnp.float32)


def bf(value):
    return value.astype(jnp.bfloat16)


def swap(value, axis, distance):
    size = lax.axis_size(axis)
    return lax.ppermute(value, axis, [(i, i ^ distance) for i in range(size)])


def xor_order(blocks, index, axis):
    size = blocks.shape[axis]
    bit = 1
    while bit < size:
        shape = blocks.shape
        split = shape[:axis] + (size // (2 * bit), 2, bit) + shape[axis + 1 :]
        view = blocks.reshape(split)
        blocks = jnp.where((index & bit) != 0, jnp.flip(view, axis + 1), view).reshape(shape)
        bit *= 2
    return blocks


def dp_steps(parity):
    return (1, 2) if parity == 0 else (2, 1)


def dp_gather(block, parity):
    first, second = dp_steps(parity)
    near = swap(block, "dp", first)
    pair = jnp.stack([block, near])
    far = swap(pair, "dp", second)
    found = {0: block, first: near, second: far[0], first | second: far[1]}
    return [found[k] for k in range(4)]


def dp_reduce(parts, parity):
    second, first = dp_steps(parity)
    got = swap(jnp.stack([bf(parts[first]), bf(parts[first | second])]), "dp", first)
    mine = parts[0] + got[0].astype(jnp.float32)
    other = parts[second] + got[1].astype(jnp.float32)
    last = swap(bf(other), "dp", second)
    return mine + last.astype(jnp.float32)


def chip_gather(block, chips):
    return [block] + [swap(block, "expert", 2 * k) for k in range(1, chips)]


SMEM = pl.BlockSpec(memory_space=pltpu.SMEM)
VMEM = pl.BlockSpec(memory_space=pltpu.VMEM)


def place_kernel(index_ref, near_low, far_low, near_up, far_up, out_ref):
    dp_index, chip_index = index_ref[0], index_ref[1]
    half = near_low.shape[1]
    for pieces, parity, base in (((near_low, far_low), 0, 0), ((near_up, far_up), 1, half)):
        first, second = dp_steps(parity)
        for far in range(2):
            for i in range(2):
                step = first * i + second * far
                for j in range(half):
                    out_ref[dp_index ^ step, chip_index ^ (base + j)] = pieces[far][i, j]


def place(index, pieces):
    _, half, rows, width = pieces[0].shape
    return pl.pallas_call(
        place_kernel,
        out_shape=jax.ShapeDtypeStruct((4, 2 * half, rows, width), pieces[0].dtype),
        in_specs=[SMEM] + [VMEM] * 4,
        out_specs=VMEM,
        name="place_weights",
    )(index, *pieces).reshape(-1, width)


def core_pick(core, first, second):
    return jnp.where(jnp.broadcast_to(core, first.shape) == 0, first, second)


def forward_kernel(placed, experts, *refs):
    if placed:
        index_ref, *refs = refs
        pieces, refs = refs[:16], refs[16:]
        tok_ref, bucket_ref, route_ref, head_ref, hot_ref, mine_ref, other_ref, *refs = refs
        dp_index, chip_index = index_ref[0], index_ref[1]
        half_chips, rows, width = pieces[0].shape[1:]
        for group in range(4):
            out = (mine_ref, mine_ref, other_ref, other_ref)[group]
            cut = slice(0, width) if group % 2 == 0 else slice(width, out.shape[1])
            for parity in range(2):
                first, second = dp_steps(parity)
                for far in range(2):
                    for i in range(2):
                        dp_at = dp_index ^ (first * i + second * far)
                        for j in range(half_chips):
                            chip_at = chip_index ^ (half_chips * parity + j)
                            at = pl.multiple_of((dp_at * 2 * half_chips + chip_at) * rows, rows)
                            out[pl.ds(at, rows), cut] = pieces[4 * group + 2 * parity + far][i, j]
    else:
        index_ref, mine_ref, other_ref, tok_ref, bucket_ref, route_ref, head_ref, hot_ref, *refs = refs
    n_ref, q_ref, k_ref, v_ref, low_ref, high_ref, att_ref, flat_ref = refs[:8]
    hidden_ref, second_ref, gate_ref, gain_ref, bias_ref = refs[8:]
    f32 = jnp.float32
    core = index_ref[3]
    half_seq = SEQ // 2
    half = q_ref.shape[1] // 2
    small = mine_ref[:, 4 * half :]
    vectors = small.astype(f32).T
    gain_ref[...] = vectors[experts : experts + 2]
    rows16 = lax.broadcasted_iota(jnp.int32, (16, vectors.shape[1]), 0)
    shifted = rows16 + core * (H // 2)
    wanted = jnp.where(rows16 < H, jnp.where(shifted >= H, shifted - H, shifted), -2)
    spread = jnp.where(head_ref[...] == wanted, vectors[experts + 2 : experts + 3], 0.0)
    bias_ref[...] = matmul(bf(spread), hot_ref[...])

    hidden = tok_ref[...].astype(f32)
    normed = bf(rms_apply(hidden, gain_ref[0:1]))
    n_ref[...] = normed
    for part, out in enumerate((q_ref, k_ref, v_ref)):
        cut = slice(part * half, (part + 1) * half)
        out[:, :half] = bf(matmul(normed, mine_ref[:, cut]))
        out[:, half:] = bf(matmul(normed, other_ref[:, cut]))
    scale = 1.0 / math.sqrt(DH)
    row_ids = lax.broadcasted_iota(jnp.int32, (half_seq, half_seq), 0)
    col_ids = lax.broadcasted_iota(jnp.int32, (half_seq, half_seq), 1)
    causal = row_ids >= col_ids

    def biased(raw, head, rows, cols):
        table = jnp.broadcast_to(bias_ref[pl.ds(head, 1), :], (half_seq, LANES))
        return raw * scale + jnp.take_along_axis(table, bucket_ref[rows, cols], axis=1)

    def softmax(blocks):
        peak = blocks[0].max(-1, keepdims=True)
        for b in blocks[1:]:
            peak = jnp.maximum(peak, b.max(-1, keepdims=True))
        exps = [jnp.exp(b - peak) for b in blocks]
        total = sum(x.sum(-1, keepdims=True) for x in exps)
        inverse = 1.0 / total
        return [x * inverse for x in exps]

    first, second = slice(0, half_seq), slice(half_seq, SEQ)

    def pair_step(pair, carry):
        lanes = pl.ds(pl.multiple_of(pair * 2 * DH, 2 * DH), 2 * DH)
        qp, kp, vp = q_ref[:, lanes], k_ref[:, lanes], v_ref[:, lanes]
        outs_low, outs_high = [], []
        for sub in range(2):
            head = pair * 2 + sub
            cut = slice(sub * DH, (sub + 1) * DH)
            q, k, v = qp[:, cut], kp[:, cut], vp[:, cut]
            s00 = biased(matmul_nt(q[first], k[first]), head, first, first)
            s1 = matmul_nt(q[second], k)
            s10 = biased(s1[:, first], head, second, first)
            s11 = biased(s1[:, second], head, second, second)
            (p00,) = softmax([jnp.where(causal, s00, -1e30)])
            p10, p11 = softmax([s10, jnp.where(causal, s11, -1e30)])
            low_ref[head] = p00
            high_ref[head, :, first] = p10
            high_ref[head, :, second] = p11
            outs_low.append(matmul(bf(p00), v[first]))
            outs_high.append(matmul(bf(p10), v[first]) + matmul(bf(p11), v[second]))
        att_ref[first, lanes] = bf(jnp.concatenate(outs_low, 1))
        att_ref[second, lanes] = bf(jnp.concatenate(outs_high, 1))
        return carry

    lax.fori_loop(0, H // 2, pair_step, 0)
    att_mine, att_other = att_ref[:, :half].astype(f32), att_ref[:, half:].astype(f32)
    flat_ref[:, :half] = bf(core_pick(core, att_mine, att_other))
    flat_ref[:, half:] = bf(core_pick(core, att_other, att_mine))
    flat = flat_ref[...]
    cut = slice(3 * half, 4 * half)
    out_mine, out_other = matmul(flat, mine_ref[:, cut]), matmul(flat, other_ref[:, cut])
    hidden_ref[:, :half] = hidden[:, :half] + core_pick(core, out_mine, out_other)
    hidden_ref[:, half:] = hidden[:, half:] + core_pick(core, out_other, out_mine)
    normed_two = bf(rms_apply(hidden_ref[...], gain_ref[1:2]))
    second_ref[...] = normed_two
    logits = matmul(normed_two, small)
    lane = lax.broadcasted_iota(jnp.int32, logits.shape, 1)
    chosen = [
        jnp.sum(jnp.where(lane == route_ref[:, k : k + 1], logits, 0.0), 1, keepdims=True)
        for k in range(2)
    ]
    peak = jnp.maximum(chosen[0], chosen[1])
    exps = [jnp.exp(c - peak) for c in chosen]
    total = exps[0] + exps[1]
    gate_ref[...] = jnp.where(lane == 0, exps[0] / total, jnp.where(lane == 1, exps[1] / total, 0.0))


def layer_forward(index, mine, other, tokens, buckets, routes, head_of, hot, experts):
    tok_count, width = tokens.shape
    b16, f32 = jnp.bfloat16, jnp.float32
    shaped = jax.ShapeDtypeStruct
    flat, total = shaped((tok_count, width), b16), mine[0].shape[-1] + mine[4].shape[-1]
    placed = mine[0].shape[2] % 16 == 0
    weights = (shaped((width, total), b16),) * 2
    if placed:
        inputs = tuple(mine) + tuple(other)
    else:
        inputs = tuple(
            jnp.concatenate([place(index, p[:4]), place(index, p[4:])], 1) for p in (mine, other)
        )
    tail = (tokens, buckets, routes, head_of, hot)
    result = pl.pallas_call(
        functools.partial(forward_kernel, placed, experts),
        out_shape=(weights if placed else ())
        + (flat, flat, flat, flat)
        + (shaped((H, SEQ // 2, SEQ // 2), f32), shaped((H, SEQ // 2, SEQ), f32), flat, flat)
        + (shaped((tok_count, width), f32), flat, shaped((tok_count, LANES), f32), shaped((2, width), f32)),
        in_specs=[SMEM] + [VMEM] * (len(inputs) + len(tail)),
        out_specs=(VMEM,) * (14 if placed else 12),
        scratch_shapes=[pltpu.VMEM((16, LANES), f32)],
        name="layer_forward",
    )(index, *inputs, *tail)
    return result if placed else inputs + result


def pick_rows(target_ref, k, at, count):
    ids = lax.broadcasted_iota(jnp.int32, (target_ref.shape[0], count), 1) + at
    return (ids == target_ref[:, k : k + 1]).astype(jnp.float32)


def combine_kernel(
    ret_mine_ref, ret_other_ref, target_ref, route_ref, gate_ref, cot_ref, hidden_ref, out_ref, logit_ref
):
    count = ret_mine_ref.shape[0]
    gates = [gate_ref[:, k : k + 1] for k in range(2)]
    total = hidden_ref[...]
    backs = []
    for k in range(2):
        value = matmul(bf(pick_rows(target_ref, k, 0, count)), ret_mine_ref[...])
        value += matmul(bf(pick_rows(target_ref, k, count, count)), ret_other_ref[...])
        total += gates[k] * value
        backs.append(jnp.sum(cot_ref[...] * value, axis=1, keepdims=True))
    out_ref[...] = total
    mean = gates[0] * backs[0] + gates[1] * backs[1]
    lane = lax.broadcasted_iota(jnp.int32, logit_ref.shape, 1)
    logit = jnp.zeros(logit_ref.shape, jnp.float32)
    for k in range(2):
        logit += jnp.where(lane == route_ref[:, k : k + 1], gates[k] * (backs[k] - mean), 0.0)
    logit_ref[...] = bf(logit)


def combine(returned, targets, routes, gate_lanes, cot, hidden):
    shaped = jax.ShapeDtypeStruct
    return pl.pallas_call(
        combine_kernel,
        out_shape=(
            shaped(hidden.shape, jnp.float32),
            shaped((hidden.shape[0], LANES), jnp.bfloat16),
        ),
        in_specs=[VMEM] * 7,
        out_specs=(VMEM,) * 2,
        name="combine_experts",
    )(*returned, targets, routes, gate_lanes, cot, hidden)


def pack_kernel(index_ref, q_ref, k_ref, v_ref, o_ref, router_ref, one_ref, two_ref, bias_ref, *outs):
    keep_a, keep_b, send_a, send_b, pad_ref = outs
    core, experts = index_ref[3], router_ref.shape[1]
    rows, width = q_ref.shape
    half = width // 2
    f32 = jnp.float32
    for i, ref in enumerate((q_ref, k_ref, v_ref, o_ref)):
        left, right = ref[:, :half].astype(f32), ref[:, half:].astype(f32)
        cut = slice(i % 2 * half, (i % 2 + 1) * half)
        (keep_a if i < 2 else keep_b)[:, cut] = bf(core_pick(core, left, right))
        (send_a if i < 2 else send_b)[:, cut] = bf(core_pick(core, right, left))
    pad_ref[...] = jnp.zeros(pad_ref.shape, f32)
    for i, ref in enumerate((one_ref, two_ref, bias_ref)):
        pad_ref[experts + i : experts + i + 1, : ref.shape[1]] = ref[...].astype(f32)
    small = pad_ref[...].T[:rows]
    pad_ref[:rows, :experts] = router_ref[...].astype(f32)
    lane = lax.broadcasted_iota(jnp.int32, small.shape, 1)
    small = bf(jnp.where(lane < experts, pad_ref[:rows], small))
    keep_b[:, width:] = small
    send_b[:, width:] = small


def pack(index, weights, router, vectors):
    rows, width = weights[0].shape
    out_a = jax.ShapeDtypeStruct((rows, width), jnp.bfloat16)
    out_b = jax.ShapeDtypeStruct((rows, width + LANES), jnp.bfloat16)
    return pl.pallas_call(
        pack_kernel,
        out_shape=(out_a, out_b) * 2,
        in_specs=[SMEM] + [VMEM] * 8,
        out_specs=(VMEM,) * 4,
        scratch_shapes=[pltpu.VMEM((LANES, LANES), jnp.float32)],
        name="pack_shards",
    )(index, *weights, router, *[v[None, :] for v in vectors])


def finish_kernel(index_ref, mine_a, got_a, mine_b, got_b, q_ref, k_ref, v_ref, o_ref, router_ref, vector_ref):
    core, experts = index_ref[3], router_ref.shape[1]
    rows, width = q_ref.shape
    half = width // 2
    for i, ref in enumerate((q_ref, k_ref, v_ref, o_ref)):
        cut = slice(i % 2 * half, (i % 2 + 1) * half)
        mine_ref, got_ref = (mine_a, got_a) if i < 2 else (mine_b, got_b)
        mine, other = mine_ref[:, cut], got_ref[:, cut].astype(jnp.float32)
        ref[:, :half] = core_pick(core, mine, other)
        ref[:, half:] = core_pick(core, other, mine)
    small = mine_b[:, width:]
    router_ref[...] = small[:, :experts]
    padded = jnp.concatenate([small, jnp.zeros((LANES - rows, LANES), jnp.float32)], 0)
    vector_ref[...] = padded.T[experts : experts + 3, :rows]


def finish(index, groups, experts):
    rows, width = groups[0].shape
    shaped = lambda *dims: jax.ShapeDtypeStruct(dims, jnp.float32)
    return pl.pallas_call(
        finish_kernel,
        out_shape=(shaped(rows, width),) * 4 + (shaped(rows, experts), shaped(3, rows)),
        in_specs=[SMEM] + [VMEM] * 4,
        out_specs=(VMEM,) * 6,
        name="finish_shared",
    )(index, *groups)


def backward_kernel(
    index_ref, ret_mine_ref, ret_other_ref, target_ref, logit_ref, cot_ref, hidden_ref, second_ref, flat_ref, att_ref, low_ref, high_ref,
    n_ref, q_ref, k_ref, v_ref, mine_ref, other_ref, tok_ref, gain_ref,
    keep_a, keep_b, send_a, send_b, grad_ref, score_ref, qb_ref, kb_ref, vb_ref, ab_ref,
):
    f32 = jnp.float32
    half_seq = SEQ // 2
    scale = 1.0 / math.sqrt(DH)
    first, second = slice(0, half_seq), slice(half_seq, SEQ)
    half = ab_ref.shape[1] // 2
    replicas, chips, rows, _ = keep_a.shape
    dp_index, chip_index, experts, core = (index_ref[i] for i in range(4))
    payload = 4 * half

    def store(kept, sent, part):
        at = (part if part < 2 else part - 2) * half
        cut = slice(at, at + kept.shape[1])
        outs = (keep_a, send_a) if part < 2 else (keep_b, send_b)
        for out, value in zip(outs, (bf(kept), bf(sent))):
            for i in range(replicas):
                for j in range(chips):
                    at = (i * chips + j) * rows
                    out[dp_index ^ i, chip_index ^ j, :, cut] = value[at : at + rows]

    def norm_back(hidden, gain, upstream):
        factor = lax.rsqrt(jnp.mean(hidden * hidden, axis=-1, keepdims=True) + EPSILON)
        scaled = upstream * gain
        inner = jnp.mean(scaled * hidden, axis=-1, keepdims=True)
        gain_back = jnp.sum(upstream * (hidden * factor), axis=0, keepdims=True)
        return factor * (scaled - hidden * (factor * factor * inner)), gain_back

    token_back = jnp.zeros(tok_ref.shape, f32)
    for at, ref in ((0, ret_mine_ref), (ret_mine_ref.shape[0], ret_other_ref)):
        picked = sum(pick_rows(target_ref, k, at, ref.shape[0]) for k in range(2))
        token_back += matmul(bf(picked), ref[...])
    logit_back = logit_ref[...]
    small_w = mine_ref[:, payload:]
    hidden_back, gain_two_back = norm_back(
        hidden_ref[...], gain_ref[1:2], token_back + matmul_nt(logit_back, small_w)
    )
    hidden_back = cot_ref[...] + hidden_back
    grad_ref[...] = hidden_back
    left, right = hidden_back[:, :half], hidden_back[:, half:]
    res_mine, res_other = bf(core_pick(core, left, right)), bf(core_pick(core, right, left))
    cut = slice(3 * half, payload)
    ab = matmul_nt(res_mine, mine_ref[:, cut]) + matmul_nt(res_other, other_ref[:, cut])
    left, right = ab[:, :half], ab[:, half:]
    ab_ref[:, :half] = bf(core_pick(core, left, right))
    ab_ref[:, half:] = bf(core_pick(core, right, left))
    flat = flat_ref[...]
    store(matmul_tn(flat, res_mine), matmul_tn(flat, res_other), 3)

    def pair_step(pair, carry):
        lanes = pl.ds(pl.multiple_of(pair * 2 * DH, 2 * DH), 2 * DH)
        qp, kp, vp = q_ref[:, lanes], k_ref[:, lanes], v_ref[:, lanes]
        abp, attp = ab_ref[:, lanes], att_ref[:, lanes]
        found = [[], [], []]
        for sub in range(2):
            head = pair * 2 + sub
            cut = slice(sub * DH, (sub + 1) * DH)
            q, k, v, ab, att = qp[:, cut], kp[:, cut], vp[:, cut], abp[:, cut], attp[:, cut]
            delta = jnp.sum(ab.astype(f32) * att.astype(f32), axis=1, keepdims=True)
            low, high = low_ref[head], high_ref[head]
            low_b, high_b = bf(low), bf(high)
            value_low = matmul_tn(low_b, ab[first])
            value_high = matmul_tn(high_b, ab[second])
            found[2].append(
                jnp.concatenate([value_low + value_high[first], value_high[second]], 0)
            )
            back_low = low * (matmul_nt(ab[first], v[first]) - delta[first])
            back_high = high * (matmul_nt(ab[second], v) - delta[second])
            low_r, high_r = bf(back_low), bf(back_high)
            for at, low_s, high_s in (
                (head, low_r, high_r),
                (head + H, bf(back_low - low_r.astype(f32)), bf(back_high - high_r.astype(f32))),
            ):
                score_ref[at, first, first] = low_s
                score_ref[at, first, second] = jnp.zeros_like(low_s)
                score_ref[at, second, :] = high_s
            found[0].append(
                jnp.concatenate([matmul(low_r, k[first]), matmul(high_r, k)], 0) * scale
            )
            key_low = matmul_tn(low_r, q[first])
            key_high = matmul_tn(high_r, q[second])
            found[1].append(
                jnp.concatenate([key_low + key_high[first], key_high[second]], 0) * scale
            )
        for out, value in zip((qb_ref, kb_ref, vb_ref), found):
            out[:, lanes] = bf(jnp.concatenate(value, 1))
        return carry

    lax.fori_loop(0, H // 2, pair_step, 0)

    normed = n_ref[...]
    normed_back = jnp.zeros(tok_ref.shape, f32)
    for part, ref in enumerate((qb_ref, kb_ref, vb_ref)):
        cut = slice(part * half, (part + 1) * half)
        mine_b, other_b = ref[:, :half], ref[:, half:]
        store(matmul_tn(normed, mine_b), matmul_tn(normed, other_b), part)
        normed_back += matmul_nt(mine_b, mine_ref[:, cut]) + matmul_nt(other_b, other_ref[:, cut])
    token_back, gain_one_back = norm_back(tok_ref[...].astype(f32), gain_ref[0:1], normed_back)
    grad_ref[...] += token_back
    small = matmul_tn(second_ref[...], logit_back)
    lane = lax.broadcasted_iota(jnp.int32, small.shape, 1)
    for at, gain_back in ((experts, gain_one_back), (experts + 1, gain_two_back)):
        wide = jnp.broadcast_to(gain_back, (LANES, gain_back.shape[1])).T
        small = jnp.where(lane == at, wide, small)
    store(small, small, 4)


def layer_backward(index, returned, targets, logit_back, cot, forward, tokens, chips, replicas):
    mine, other, normed, q, k, v, low, high, att, flat, hidden, second, _, gains = forward
    tok_count, width = tokens.shape
    b16, f32 = jnp.bfloat16, jnp.float32
    shaped = jax.ShapeDtypeStruct
    blocks = (replicas, chips, width // (replicas * chips))
    group_a, group_b = blocks + (width,), blocks + (mine.shape[1] - width,)
    return pl.pallas_call(
        backward_kernel,
        out_shape=(
            shaped(group_a, b16),
            shaped(group_b, b16),
            shaped(group_a, b16),
            shaped(group_b, b16),
            shaped((tok_count, width), f32),
            shaped((2 * H, SEQ, SEQ), b16),
        ),
        in_specs=[SMEM] + [VMEM] * 19,
        out_specs=(VMEM,) * 6,
        scratch_shapes=[pltpu.VMEM((tok_count, width), b16)] * 4,
        name="layer_backward",
    )(
        index, *returned, targets, logit_back, cot, hidden, second, flat, att, low, high, normed, q, k, v,
        mine, other, tokens, gains,
    )


def core_join(mine, other, core, axis=1):
    return jnp.concatenate(
        [jnp.where(core == 0, mine, other), jnp.where(core == 0, other, mine)], axis
    )


def gather_pieces(keep, send, chips, core):
    got = swap(send, "expert", 1)
    block = core_join(keep, got, core, 0)
    found = chip_gather(block, chips)
    pieces = []
    for parity, part in enumerate((found[: chips // 2], found[chips // 2 :])):
        first, second = dp_steps(parity)
        part = jnp.stack(part)
        near = jnp.stack([part, swap(part, "dp", first)])
        far = swap(near, "dp", second)
        pieces += [near, far]
    return pieces


def partner_pieces(pieces):
    result = []
    for piece in pieces:
        result.append(swap(piece, "expert", 1))
    return result


def scatter_blocks(keep, send, column, lane_at, chips, core):
    replicas = lax.axis_size("dp")
    got = swap(send, "expert", 1)
    blocks = keep.astype(jnp.float32) + got.astype(jnp.float32)
    if column is not None:
        lane = lax.broadcasted_iota(jnp.int32, keep.shape, 3)
        blocks = jnp.where(lane == lane_at, column[..., None], blocks)
    lower, upper = blocks[:, : chips // 2], blocks[:, chips // 2 :]
    lower = dp_reduce([lower[k] for k in range(replicas)], 0)
    upper = dp_reduce([upper[k] for k in range(replicas)], 1)
    chip_blocks = [lower[k] for k in range(chips // 2)] + [upper[k] for k in range(chips // 2)]
    arrived = [swap(bf(chip_blocks[k]), "expert", 2 * k) for k in range(1, chips)]
    block = chip_blocks[0]
    for piece in arrived:
        block = block + piece.astype(jnp.float32)
    rows = block.shape[0] // 2
    mine = jnp.where(core == 0, block[:rows], block[rows:])
    theirs = jnp.where(core == 0, block[rows:], block[:rows])
    got = swap(bf(theirs), "expert", 1)
    return mine, got


def slot_positions(routes, experts):
    flat = routes.reshape(-1)
    expert_hot = (flat[:, None] == jnp.arange(experts, dtype=jnp.int32)[None, :]).astype(jnp.int32)
    earlier = jnp.cumsum(expert_hot, axis=0) - expert_hot
    return jnp.sum(earlier * expert_hot, axis=1).reshape(routes.shape)


def per_device(
    tokens,
    cotangent,
    buckets,
    routes,
    gain_attn,
    gain_moe,
    rel_bias,
    w_query,
    w_key,
    w_value,
    w_out,
    w_router,
    w_gate,
    w_up,
    w_down,
):
    f32 = jnp.float32
    groups = lax.axis_size("expert")
    chips = groups // 2
    replicas = lax.axis_size("dp")
    expert_index, dp_index = lax.axis_index("expert"), lax.axis_index("dp")
    core, chip_index = expert_index & 1, expert_index >> 1

    shard_rows = w_query.shape[0]
    experts = w_router.shape[1]
    n_bias = rel_bias.shape[0]
    model_width = tokens.shape[1]
    index = jnp.stack([dp_index, chip_index, jnp.int32(experts), core]).astype(jnp.int32)
    keep_a, keep_b, send_a, send_b = pack(
        index,
        (w_query, w_key, w_value, w_out),
        w_router,
        (gain_attn, gain_moe, rel_bias),
    )
    pieces = gather_pieces(keep_a, send_a, chips, core)
    pieces += gather_pieces(keep_b, send_b, chips, core)
    others = partner_pieces(pieces[:4]) + partner_pieces(pieces[4:])
    lane_ids = jnp.arange(model_width, dtype=jnp.int32)
    in_row = lane_ids % shard_rows
    flat_at = jnp.where(in_row < n_bias, lane_ids // shard_rows * n_bias + in_row, -1)
    head_of = jnp.where(flat_at >= 0, flat_at % H, -1)[None, :]
    bucket_of = jnp.where(flat_at >= 0, flat_at // H, -1)[:, None]
    hot = bf(bucket_of == jnp.arange(LANES, dtype=jnp.int32)[None, :])

    tok_count = tokens.shape[0]
    local_experts = w_gate.shape[0]
    capacity = max(2, 9 * tok_count // (4 * experts))
    unit = 2 * capacity
    chip_unit = local_experts * unit
    n_rows = chips * chip_unit
    group = routes // local_experts
    rel_core = (group & 1) ^ core
    rel_chip = (group >> 1) ^ chip_index
    targets = (
        rel_core * n_rows
        + rel_chip * chip_unit
        + (routes % local_experts) * unit
        + rel_core * capacity
        + slot_positions(routes, experts)
    )
    partner_targets = swap(targets, "expert", 1)
    partner_cot = swap(cotangent, "expert", 1)
    row_ids = jnp.arange(n_rows, dtype=jnp.int32)
    pick_own = [bf(row_ids[:, None] == targets[None, :, k]) for k in range(2)]
    pick_partner = [
        bf(row_ids[:, None] + n_rows == partner_targets[None, :, k]) for k in range(2)
    ]

    forward = layer_forward(
        index, pieces, others, tokens, buckets, routes, head_of, hot, experts
    )
    hidden_one, normed_two, gate_lanes = forward[10:13]
    partner_normed = swap(normed_two, "expert", 1)
    partner_gates = swap(gate_lanes, "expert", 1)
    gates = gate_lanes[:, :2]

    def dispatch(rows, split):
        def piece(k, e):
            at = k * chip_unit + e * unit
            return rows[at : at + unit]

        found = []
        if split:
            for e in range(local_experts):
                found.append(
                    [piece(0, e)] + [swap(piece(k, e), "expert", 2 * k) for k in range(1, chips)]
                )
        else:
            whole = [
                swap(rows[k * chip_unit : (k + 1) * chip_unit], "expert", 2 * k)
                for k in range(1, chips)
            ]
            for e in range(local_experts):
                found.append([piece(0, e)] + [w[e * unit : (e + 1) * unit] for w in whole])
        result = []
        for e in range(local_experts):
            block = jnp.concatenate(found[e], 0)
            if split:
                middle = block.shape[0] // 2
                halves = [dp_gather(block[:middle], 0), dp_gather(block[middle:], 1)]
                result.append([part for pair in zip(*halves) for part in pair])
            else:
                result.append(dp_gather(block, e % 2))
        return result

    picks = jnp.concatenate([pick_own[0] + pick_own[1], pick_partner[0] + pick_partner[1]], 1)
    rows = dispatch(bf(matmul(picks, jnp.concatenate([normed_two, partner_normed], 0))), True)
    grad_picks = jnp.concatenate(pick_own + pick_partner, 1)
    grads = dispatch(
        bf(
            matmul(
                grad_picks,
                jnp.concatenate(
                    [bf(gates[:, k : k + 1] * cotangent) for k in range(2)]
                    + [bf(partner_gates[:, k : k + 1] * partner_cot) for k in range(2)],
                    0,
                ),
            )
        ),
        False,
    )

    def reduce_rows(parts, e):
        split = parts.reshape(replicas, chips * unit, model_width)
        total = dp_reduce([split[k] for k in range(replicas)], e % 2)
        return bf(total)

    def send_home(totals):
        found = [
            jnp.concatenate([t[k * unit : (k + 1) * unit] for t in totals], 0)
            for k in range(chips)
        ]
        found = found[:1] + [swap(found[k], "expert", 2 * k) for k in range(1, chips)]
        mine = jnp.concatenate(found, 0)
        return mine, swap(mine, "expert", 1)

    rows_e = [jnp.concatenate(rows[e], 0) for e in range(local_experts)]
    grads_e = [jnp.concatenate(grads[e], 0) for e in range(local_experts)]
    acts, saved, out_totals = [], [], []
    for e in range(local_experts):
        gate_pre = matmul(rows_e[e], w_gate[e])
        up_pre = matmul(rows_e[e], w_up[e])
        act = bf(geglu(gate_pre, up_pre))
        act, gate_pre, up_pre = lax.optimization_barrier((act, gate_pre, up_pre))
        acts.append(act)
        saved.append((gate_pre, up_pre))
        part = matmul_nt(act, w_down[e])
        out_totals.append(reduce_rows(part, e))
    back_totals, pres = [], []
    for e in range(local_experts):
        _, vjp = jax.vjp(geglu, *saved[e])
        gate_back_pre, up_back_pre = vjp(matmul(grads_e[e], w_down[e]))
        gate_back_pre, up_back_pre = bf(gate_back_pre), bf(up_back_pre)
        pres.append((gate_back_pre, up_back_pre))
        part = matmul_nt(gate_back_pre, w_gate[e]) + matmul_nt(up_back_pre, w_up[e])
        back_totals.append(reduce_rows(part, e))
    down_grad = jnp.stack([matmul_tn(grads_e[e], acts[e]) for e in range(local_experts)])
    gate_grad = jnp.stack([matmul_tn(rows_e[e], pres[e][0]) for e in range(local_experts)])
    up_grad = jnp.stack([matmul_tn(rows_e[e], pres[e][1]) for e in range(local_experts)])

    returned = send_home(out_totals)
    back_rows = send_home(back_totals)
    late_cot, *returned = lax.optimization_barrier((cotangent, *returned))
    layer_out, logit_back = combine(returned, targets, routes, gate_lanes, late_cot, hidden_one)
    keep_a, keep_b, send_a, send_b, tokens_grad, score_back = layer_backward(
        index, back_rows, targets, logit_back, late_cot, forward, tokens, chips, replicas
    )
    bucket_hot = bf(buckets[None] == jnp.arange(NB, dtype=jnp.int32)[:, None, None])
    bias_grad = lax.dot_general(
        bucket_hot, score_back, (((1, 2), (1, 2)), ((), ())), preferred_element_type=f32
    )
    bias_grad = bias_grad[:, :H] + bias_grad[:, H:]
    bias_grad = core_join(bias_grad[:, : H // 2], bias_grad[:, H // 2 :], core)
    bias_grad = jnp.pad(bias_grad, ((0, 0), (0, LANES - H)))
    bias_grad = (bias_grad + swap(bias_grad, "expert", 1))[:, :H].reshape(-1, n_bias)
    column = jnp.pad(bias_grad, ((0, 0), (0, shard_rows - n_bias)))
    column = column.reshape(replicas, chips, -1)
    column = xor_order(xor_order(column, dp_index, 0), chip_index, 1)
    groups = scatter_blocks(keep_a, send_a, None, 0, chips, core)
    groups += scatter_blocks(keep_b, send_b, column, model_width + experts + 2, chips, core)
    query_total, key_total, value_total, out_total, router_total, vectors = finish(
        index, groups, experts
    )
    return (
        layer_out,
        tokens_grad,
        vectors[0],
        vectors[1],
        vectors[2, :n_bias],
        query_total,
        key_total,
        value_total,
        out_total,
        router_total,
        gate_grad,
        up_grad,
        down_grad,
    )


def solution(mesh):
    both = ("dp", "expert")
    row = P(both, None)

    return jax.shard_map(
        per_device,
        mesh=mesh,
        in_specs=(row, row, P(), row, P(both), P(both), P(both), row, row, row, row, row)
        + (P("expert", None, "dp"),) * 3,
        out_specs=(row, row, P(both), P(both), P(both), row, row, row, row, row)
        + (P("expert", None, "dp"),) * 3,
        check_vma=False,
    )
```

```python
import functools
import math

import jax
import jax.numpy as jnp
from jax import lax
from jax.experimental import pallas as pl
from jax.experimental.pallas import tpu as pltpu
from jax.sharding import PartitionSpec as P


H = 12
DH = 64
NB = 32
SEQ = 256
LANES = 128

EPSILON = 1e-06


def rms_apply(hidden, gain):
    factor = lax.rsqrt(jnp.mean(hidden * hidden, axis=-1, keepdims=True) + EPSILON)
    return hidden * factor * gain


def geglu(gate_pre, up_pre):
    return jax.nn.gelu(gate_pre, approximate=True) * up_pre


def matmul(left, right):
    return jnp.dot(left, right, preferred_element_type=jnp.float32)


def matmul_nt(left, right):
    return lax.dot_general(left, right, (((1,), (1,)), ((), ())), preferred_element_type=jnp.float32)


def matmul_tn(left, right):
    return lax.dot_general(left, right, (((0,), (0,)), ((), ())), preferred_element_type=jnp.float32)


def bf(value):
    return value.astype(jnp.bfloat16)


def swap(value, axis, distance):
    size = lax.axis_size(axis)
    return lax.ppermute(value, axis, [(i, i ^ distance) for i in range(size)])


def dp_steps(parity):
    return (1, 2) if parity == 0 else (2, 1)


def dp_gather(block, parity):
    first, second = dp_steps(parity)
    near = swap(block, "dp", first)
    pair = jnp.stack([block, near])
    far = swap(pair, "dp", second)
    found = {0: block, first: near, second: far[0], first | second: far[1]}
    return [found[k] for k in range(4)]


def dp_reduce(parts, parity):
    second, first = dp_steps(parity)
    got = swap(jnp.stack([bf(parts[first]), bf(parts[first | second])]), "dp", first)
    mine = parts[0] + got[0].astype(jnp.float32)
    other = parts[second] + got[1].astype(jnp.float32)
    last = swap(bf(other), "dp", second)
    return mine + last.astype(jnp.float32)


def chip_gather(block, chips):
    return [block] + [swap(block, "expert", 2 * k) for k in range(1, chips)]


SMEM = pl.BlockSpec(memory_space=pltpu.SMEM)
VMEM = pl.BlockSpec(memory_space=pltpu.VMEM)


def place_kernel(index_ref, near_low, far_low, near_up, far_up, out_ref):
    dp_index, chip_index = index_ref[0], index_ref[1]
    half = near_low.shape[1]
    for pieces, parity, base in (((near_low, far_low), 0, 0), ((near_up, far_up), 1, half)):
        first, second = dp_steps(parity)
        for far in range(2):
            for i in range(2):
                step = first * i + second * far
                for j in range(half):
                    out_ref[dp_index ^ step, chip_index ^ (base + j)] = pieces[far][i, j]


def place(index, pieces):
    _, half, rows, width = pieces[0].shape
    return pl.pallas_call(
        place_kernel,
        out_shape=jax.ShapeDtypeStruct((4, 2 * half, rows, width), pieces[0].dtype),
        in_specs=[SMEM] + [VMEM] * 4,
        out_specs=VMEM,
        name="place_weights",
    )(index, *pieces).reshape(-1, width)


def core_pick(core, first, second):
    return jnp.where(jnp.broadcast_to(core, first.shape) == 0, first, second)


def forward_kernel(placed, experts, *refs):
    if placed:
        index_ref, *refs = refs
        pieces, refs = refs[:16], refs[16:]
        tok_ref, bucket_ref, route_ref, head_ref, hot_ref, mine_ref, other_ref, *refs = refs
        dp_index, chip_index = index_ref[0], index_ref[1]
        half_chips, rows, width = pieces[0].shape[1:]
        for group in range(4):
            out = (mine_ref, mine_ref, other_ref, other_ref)[group]
            cut = slice(0, width) if group % 2 == 0 else slice(width, out.shape[1])
            for parity in range(2):
                first, second = dp_steps(parity)
                for far in range(2):
                    for i in range(2):
                        dp_at = dp_index ^ (first * i + second * far)
                        for j in range(half_chips):
                            chip_at = chip_index ^ (half_chips * parity + j)
                            at = pl.multiple_of((dp_at * 2 * half_chips + chip_at) * rows, rows)
                            out[pl.ds(at, rows), cut] = pieces[4 * group + 2 * parity + far][i, j]
    else:
        index_ref, mine_ref, other_ref, tok_ref, bucket_ref, route_ref, head_ref, hot_ref, *refs = refs
    n_ref, q_ref, k_ref, v_ref, low_ref, high_ref, att_ref, flat_ref = refs[:8]
    hidden_ref, second_ref, gate_ref, gain_ref, bias_ref = refs[8:]
    f32 = jnp.float32
    core = index_ref[3]
    half_seq = SEQ // 2
    half = q_ref.shape[1] // 2
    small = mine_ref[:, 4 * half :]
    vectors = small.astype(f32).T
    gain_ref[...] = vectors[experts : experts + 2]
    rows16 = lax.broadcasted_iota(jnp.int32, (16, vectors.shape[1]), 0)
    shifted = rows16 + core * (H // 2)
    wanted = jnp.where(rows16 < H, jnp.where(shifted >= H, shifted - H, shifted), -2)
    spread = jnp.where(head_ref[...] == wanted, vectors[experts + 2 : experts + 3], 0.0)
    bias_ref[...] = matmul(bf(spread), hot_ref[...])

    hidden = tok_ref[...].astype(f32)
    normed = bf(rms_apply(hidden, gain_ref[0:1]))
    n_ref[...] = normed
    for part, out in enumerate((q_ref, k_ref, v_ref)):
        cut = slice(part * half, (part + 1) * half)
        out[:, :half] = bf(matmul(normed, mine_ref[:, cut]))
        out[:, half:] = bf(matmul(normed, other_ref[:, cut]))
    scale = 1.0 / math.sqrt(DH)
    row_ids = lax.broadcasted_iota(jnp.int32, (half_seq, half_seq), 0)
    col_ids = lax.broadcasted_iota(jnp.int32, (half_seq, half_seq), 1)
    causal = row_ids >= col_ids

    def biased(raw, head, rows, cols):
        table = jnp.broadcast_to(bias_ref[pl.ds(head, 1), :], (half_seq, LANES))
        return raw * scale + jnp.take_along_axis(table, bucket_ref[rows, cols], axis=1)

    def softmax(blocks):
        peak = blocks[0].max(-1, keepdims=True)
        for b in blocks[1:]:
            peak = jnp.maximum(peak, b.max(-1, keepdims=True))
        exps = [jnp.exp(b - peak) for b in blocks]
        total = sum(x.sum(-1, keepdims=True) for x in exps)
        inverse = 1.0 / total
        return [x * inverse for x in exps]

    first, second = slice(0, half_seq), slice(half_seq, SEQ)

    def pair_step(pair, carry):
        lanes = pl.ds(pl.multiple_of(pair * 2 * DH, 2 * DH), 2 * DH)
        qp, kp, vp = q_ref[:, lanes], k_ref[:, lanes], v_ref[:, lanes]
        outs_low, outs_high = [], []
        for sub in range(2):
            head = pair * 2 + sub
            cut = slice(sub * DH, (sub + 1) * DH)
            q, k, v = qp[:, cut], kp[:, cut], vp[:, cut]
            s00 = biased(matmul_nt(q[first], k[first]), head, first, first)
            s1 = matmul_nt(q[second], k)
            s10 = biased(s1[:, first], head, second, first)
            s11 = biased(s1[:, second], head, second, second)
            (p00,) = softmax([jnp.where(causal, s00, -1e30)])
            p10, p11 = softmax([s10, jnp.where(causal, s11, -1e30)])
            low_ref[head] = p00
            high_ref[head, :, first] = p10
            high_ref[head, :, second] = p11
            outs_low.append(matmul(bf(p00), v[first]))
            outs_high.append(matmul(bf(p10), v[first]) + matmul(bf(p11), v[second]))
        att_ref[first, lanes] = bf(jnp.concatenate(outs_low, 1))
        att_ref[second, lanes] = bf(jnp.concatenate(outs_high, 1))
        return carry

    lax.fori_loop(0, H // 2, pair_step, 0)
    att_mine, att_other = att_ref[:, :half].astype(f32), att_ref[:, half:].astype(f32)
    flat_ref[:, :half] = bf(core_pick(core, att_mine, att_other))
    flat_ref[:, half:] = bf(core_pick(core, att_other, att_mine))
    flat = flat_ref[...]
    cut = slice(3 * half, 4 * half)
    out_mine, out_other = matmul(flat, mine_ref[:, cut]), matmul(flat, other_ref[:, cut])
    hidden_ref[:, :half] = hidden[:, :half] + core_pick(core, out_mine, out_other)
    hidden_ref[:, half:] = hidden[:, half:] + core_pick(core, out_other, out_mine)
    normed_two = bf(rms_apply(hidden_ref[...], gain_ref[1:2]))
    second_ref[...] = normed_two
    logits = matmul(normed_two, small)
    lane = lax.broadcasted_iota(jnp.int32, logits.shape, 1)
    chosen = [
        jnp.sum(jnp.where(lane == route_ref[:, k : k + 1], logits, 0.0), 1, keepdims=True)
        for k in range(2)
    ]
    peak = jnp.maximum(chosen[0], chosen[1])
    exps = [jnp.exp(c - peak) for c in chosen]
    total = exps[0] + exps[1]
    gate_ref[...] = jnp.where(lane == 0, exps[0] / total, jnp.where(lane == 1, exps[1] / total, 0.0))


def layer_forward(index, mine, other, tokens, buckets, routes, head_of, hot, experts):
    tok_count, width = tokens.shape
    b16, f32 = jnp.bfloat16, jnp.float32
    shaped = jax.ShapeDtypeStruct
    flat, total = shaped((tok_count, width), b16), mine[0].shape[-1] + mine[4].shape[-1]
    placed = mine[0].shape[2] % 16 == 0
    weights = (shaped((width, total), b16),) * 2
    if placed:
        inputs = tuple(mine) + tuple(other)
    else:
        inputs = tuple(
            jnp.concatenate([place(index, p[:4]), place(index, p[4:])], 1) for p in (mine, other)
        )
    tail = (tokens, buckets, routes, head_of, hot)
    result = pl.pallas_call(
        functools.partial(forward_kernel, placed, experts),
        out_shape=(weights if placed else ())
        + (flat, flat, flat, flat)
        + (shaped((H, SEQ // 2, SEQ // 2), f32), shaped((H, SEQ // 2, SEQ), f32), flat, flat)
        + (shaped((tok_count, width), f32), flat, shaped((tok_count, LANES), f32), shaped((2, width), f32)),
        in_specs=[SMEM] + [VMEM] * (len(inputs) + len(tail)),
        out_specs=(VMEM,) * (14 if placed else 12),
        scratch_shapes=[pltpu.VMEM((16, LANES), f32)],
        name="layer_forward",
    )(index, *inputs, *tail)
    return result if placed else inputs + result


def pick_rows(target_ref, k, at, count):
    ids = lax.broadcasted_iota(jnp.int32, (target_ref.shape[0], count), 1) + at
    return (ids == target_ref[:, k : k + 1]).astype(jnp.float32)


def combine_kernel(
    ret_mine_ref, ret_other_ref, target_ref, route_ref, gate_ref, cot_ref, hidden_ref, out_ref, logit_ref
):
    count = ret_mine_ref.shape[0]
    gates = [gate_ref[:, k : k + 1] for k in range(2)]
    total = hidden_ref[...]
    backs = []
    for k in range(2):
        value = matmul(bf(pick_rows(target_ref, k, 0, count)), ret_mine_ref[...])
        value += matmul(bf(pick_rows(target_ref, k, count, count)), ret_other_ref[...])
        total += gates[k] * value
        backs.append(jnp.sum(cot_ref[...] * value, axis=1, keepdims=True))
    out_ref[...] = total
    mean = gates[0] * backs[0] + gates[1] * backs[1]
    lane = lax.broadcasted_iota(jnp.int32, logit_ref.shape, 1)
    logit = jnp.zeros(logit_ref.shape, jnp.float32)
    for k in range(2):
        logit += jnp.where(lane == route_ref[:, k : k + 1], gates[k] * (backs[k] - mean), 0.0)
    logit_ref[...] = bf(logit)


def combine(returned, targets, routes, gate_lanes, cot, hidden):
    shaped = jax.ShapeDtypeStruct
    return pl.pallas_call(
        combine_kernel,
        out_shape=(
            shaped(hidden.shape, jnp.float32),
            shaped((hidden.shape[0], LANES), jnp.bfloat16),
        ),
        in_specs=[VMEM] * 7,
        out_specs=(VMEM,) * 2,
        name="combine_experts",
    )(*returned, targets, routes, gate_lanes, cot, hidden)


def pack_kernel(index_ref, q_ref, k_ref, v_ref, o_ref, router_ref, one_ref, two_ref, bias_ref, *outs):
    keep_a, keep_b, send_a, send_b, pad_ref = outs
    core, experts = index_ref[3], router_ref.shape[0]
    rows, width = q_ref.shape
    half = width // 2
    f32 = jnp.float32
    for i, ref in enumerate((q_ref, k_ref, v_ref, o_ref)):
        left, right = ref[:, :half].astype(f32), ref[:, half:].astype(f32)
        cut = slice(i % 2 * half, (i % 2 + 1) * half)
        (keep_a if i < 2 else keep_b)[:, cut] = bf(core_pick(core, left, right))
        (send_a if i < 2 else send_b)[:, cut] = bf(core_pick(core, right, left))
    pad_ref[...] = jnp.zeros(pad_ref.shape, f32)
    for i, ref in enumerate((one_ref, two_ref, bias_ref)):
        pad_ref[experts + i : experts + i + 1, : ref.shape[1]] = ref[...].astype(f32)
    pad_ref[:experts, :rows] = router_ref[...].astype(f32)
    small = bf(pad_ref[...].T[:rows])
    keep_b[:, width:] = small
    send_b[:, width:] = small


def pack(index, weights, router, vectors):
    rows, width = weights[0].shape
    out_a = jax.ShapeDtypeStruct((rows, width), jnp.bfloat16)
    out_b = jax.ShapeDtypeStruct((rows, width + LANES), jnp.bfloat16)
    return pl.pallas_call(
        pack_kernel,
        out_shape=(out_a, out_b) * 2,
        in_specs=[SMEM] + [VMEM] * 8,
        out_specs=(VMEM,) * 4,
        scratch_shapes=[pltpu.VMEM((LANES, LANES), jnp.float32)],
        name="pack_shards",
    )(index, *weights, router.T, *[v[None, :] for v in vectors])


def bias_kernel(index_ref, mine_ref, other_ref, hot_ref, head_ref, out_ref):
    f32 = jnp.float32
    core = index_ref[3]
    replicas, chips, rows, lanes = out_ref.shape
    lane = lax.broadcasted_iota(jnp.int32, (hot_ref.shape[0], lanes), 1)
    head = jnp.broadcast_to(head_ref[...], lane.shape)
    total = jnp.zeros(lane.shape, f32)
    for i, ref in enumerate((mine_ref, other_ref)):
        shifted = head + (core ^ i) * (H // 2)
        local = jnp.where(head < 0, -1, jnp.where(shifted >= H, shifted - H, shifted))
        rest = ref[...]
        for _ in range(3):
            part = bf(rest)
            rest = rest - part.astype(f32)
            spread = matmul(hot_ref[...], part)
            total += jnp.where((lane == local) | (lane == jnp.where(local < 0, -1, local + H)), spread, 0.0)
    column = jnp.sum(total, axis=1, keepdims=True)
    value = jnp.where(lane == index_ref[2] + 2, column, 0.0)
    for i in range(replicas):
        for j in range(chips):
            at = (i * chips + j) * rows
            out_ref[index_ref[0] ^ i, index_ref[1] ^ j] = value[at : at + rows]


def bias_blocks(index, mine, other, hot, head_of, chips, replicas):
    rows = hot.shape[0] // (replicas * chips)
    return pl.pallas_call(
        bias_kernel,
        out_shape=jax.ShapeDtypeStruct((replicas, chips, rows, LANES), jnp.float32),
        in_specs=[SMEM] + [VMEM] * 4,
        out_specs=VMEM,
        name="bias_column",
    )(index, mine, other, hot, head_of)


def finish_kernel(index_ref, mine_a, got_a, mine_b, got_b, q_ref, k_ref, v_ref, o_ref, router_ref, *vector_refs):
    core, experts = index_ref[3], router_ref.shape[0]
    rows, width = q_ref.shape
    half = width // 2
    for i, ref in enumerate((q_ref, k_ref, v_ref, o_ref)):
        cut = slice(i % 2 * half, (i % 2 + 1) * half)
        mine_ref, got_ref = (mine_a, got_a) if i < 2 else (mine_b, got_b)
        mine, other = mine_ref[:, cut], got_ref[:, cut].astype(jnp.float32)
        ref[:, :half] = core_pick(core, mine, other)
        ref[:, half:] = core_pick(core, other, mine)
    small = mine_b[:, width:]
    padded = jnp.concatenate([small, jnp.zeros((LANES - rows, LANES), jnp.float32)], 0).T
    router_ref[...] = padded[:experts, :rows]
    for i, ref in enumerate(vector_refs):
        ref[...] = padded[experts + i : experts + i + 1, : ref.shape[1]]


def finish(index, groups, experts, n_bias):
    rows, width = groups[0].shape
    shaped = lambda *dims: jax.ShapeDtypeStruct(dims, jnp.float32)
    return pl.pallas_call(
        finish_kernel,
        out_shape=(shaped(rows, width),) * 4
        + (shaped(experts, rows), shaped(1, rows), shaped(1, rows), shaped(1, n_bias)),
        in_specs=[SMEM] + [VMEM] * 4,
        out_specs=(VMEM,) * 8,
        name="finish_shared",
    )(index, *groups)


def backward_kernel(
    index_ref, ret_mine_ref, ret_other_ref, target_ref, logit_ref, cot_ref, hidden_ref, second_ref, flat_ref, att_ref, low_ref, high_ref,
    n_ref, q_ref, k_ref, v_ref, mine_ref, other_ref, tok_ref, gain_ref,
    keep_a, keep_b, send_a, send_b, grad_ref, score_ref, qb_ref, kb_ref, vb_ref, ab_ref,
):
    f32 = jnp.float32
    half_seq = SEQ // 2
    scale = 1.0 / math.sqrt(DH)
    first, second = slice(0, half_seq), slice(half_seq, SEQ)
    half = ab_ref.shape[1] // 2
    replicas, chips, rows, _ = keep_a.shape
    dp_index, chip_index, experts, core = (index_ref[i] for i in range(4))
    payload = 4 * half

    def store(kept, sent, part):
        at = (part if part < 2 else part - 2) * half
        cut = slice(at, at + kept.shape[1])
        outs = (keep_a, send_a) if part < 2 else (keep_b, send_b)
        for out, value in zip(outs, (bf(kept), bf(sent))):
            for i in range(replicas):
                for j in range(chips):
                    at = (i * chips + j) * rows
                    out[dp_index ^ i, chip_index ^ j, :, cut] = value[at : at + rows]

    def norm_back(hidden, gain, upstream):
        factor = lax.rsqrt(jnp.mean(hidden * hidden, axis=-1, keepdims=True) + EPSILON)
        scaled = upstream * gain
        inner = jnp.mean(scaled * hidden, axis=-1, keepdims=True)
        gain_back = jnp.sum(upstream * (hidden * factor), axis=0, keepdims=True)
        return factor * (scaled - hidden * (factor * factor * inner)), gain_back

    token_back = jnp.zeros(tok_ref.shape, f32)
    for at, ref in ((0, ret_mine_ref), (ret_mine_ref.shape[0], ret_other_ref)):
        picked = sum(pick_rows(target_ref, k, at, ref.shape[0]) for k in range(2))
        token_back += matmul(bf(picked), ref[...])
    logit_back = logit_ref[...]
    small_w = mine_ref[:, payload:]
    hidden_back, gain_two_back = norm_back(
        hidden_ref[...], gain_ref[1:2], token_back + matmul_nt(logit_back, small_w)
    )
    hidden_back = cot_ref[...] + hidden_back
    grad_ref[...] = hidden_back
    left, right = hidden_back[:, :half], hidden_back[:, half:]
    res_mine, res_other = bf(core_pick(core, left, right)), bf(core_pick(core, right, left))
    cut = slice(3 * half, payload)
    ab = matmul_nt(res_mine, mine_ref[:, cut]) + matmul_nt(res_other, other_ref[:, cut])
    left, right = ab[:, :half], ab[:, half:]
    ab_ref[:, :half] = bf(core_pick(core, left, right))
    ab_ref[:, half:] = bf(core_pick(core, right, left))
    flat = flat_ref[...]
    store(matmul_tn(flat, res_mine), matmul_tn(flat, res_other), 3)

    def pair_step(pair, carry):
        lanes = pl.ds(pl.multiple_of(pair * 2 * DH, 2 * DH), 2 * DH)
        qp, kp, vp = q_ref[:, lanes], k_ref[:, lanes], v_ref[:, lanes]
        abp, attp = ab_ref[:, lanes], att_ref[:, lanes]
        found = [[], [], []]
        for sub in range(2):
            head = pair * 2 + sub
            cut = slice(sub * DH, (sub + 1) * DH)
            q, k, v, ab, att = qp[:, cut], kp[:, cut], vp[:, cut], abp[:, cut], attp[:, cut]
            delta = jnp.sum(ab.astype(f32) * att.astype(f32), axis=1, keepdims=True)
            low, high = low_ref[head], high_ref[head]
            low_b, high_b = bf(low), bf(high)
            value_low = matmul_tn(low_b, ab[first])
            value_high = matmul_tn(high_b, ab[second])
            found[2].append(
                jnp.concatenate([value_low + value_high[first], value_high[second]], 0)
            )
            back_low = low * (matmul_nt(ab[first], v[first]) - delta[first])
            back_high = high * (matmul_nt(ab[second], v) - delta[second])
            low_r, high_r = bf(back_low), bf(back_high)
            for at, low_s, high_s in (
                (head, low_r, high_r),
                (head + H, bf(back_low - low_r.astype(f32)), bf(back_high - high_r.astype(f32))),
            ):
                score_ref[at, first, first] = low_s
                score_ref[at, first, second] = jnp.zeros_like(low_s)
                score_ref[at, second, :] = high_s
            found[0].append(
                jnp.concatenate([matmul(low_r, k[first]), matmul(high_r, k)], 0) * scale
            )
            key_low = matmul_tn(low_r, q[first])
            key_high = matmul_tn(high_r, q[second])
            found[1].append(
                jnp.concatenate([key_low + key_high[first], key_high[second]], 0) * scale
            )
        for out, value in zip((qb_ref, kb_ref, vb_ref), found):
            out[:, lanes] = bf(jnp.concatenate(value, 1))
        return carry

    lax.fori_loop(0, H // 2, pair_step, 0)

    normed = n_ref[...]
    normed_back = jnp.zeros(tok_ref.shape, f32)
    for part, ref in enumerate((qb_ref, kb_ref, vb_ref)):
        cut = slice(part * half, (part + 1) * half)
        mine_b, other_b = ref[:, :half], ref[:, half:]
        store(matmul_tn(normed, mine_b), matmul_tn(normed, other_b), part)
        normed_back += matmul_nt(mine_b, mine_ref[:, cut]) + matmul_nt(other_b, other_ref[:, cut])
    token_back, gain_one_back = norm_back(tok_ref[...].astype(f32), gain_ref[0:1], normed_back)
    grad_ref[...] += token_back
    small = matmul_tn(second_ref[...], logit_back)
    lane = lax.broadcasted_iota(jnp.int32, small.shape, 1)
    for at, gain_back in ((experts, gain_one_back), (experts + 1, gain_two_back)):
        wide = jnp.broadcast_to(gain_back, (LANES, gain_back.shape[1])).T
        small = jnp.where(lane == at, wide, small)
    store(small, small, 4)


def layer_backward(index, returned, targets, logit_back, cot, forward, tokens, chips, replicas):
    mine, other, normed, q, k, v, low, high, att, flat, hidden, second, _, gains = forward
    tok_count, width = tokens.shape
    b16, f32 = jnp.bfloat16, jnp.float32
    shaped = jax.ShapeDtypeStruct
    blocks = (replicas, chips, width // (replicas * chips))
    group_a, group_b = blocks + (width,), blocks + (mine.shape[1] - width,)
    return pl.pallas_call(
        backward_kernel,
        out_shape=(
            shaped(group_a, b16),
            shaped(group_b, b16),
            shaped(group_a, b16),
            shaped(group_b, b16),
            shaped((tok_count, width), f32),
            shaped((2 * H, SEQ, SEQ), b16),
        ),
        in_specs=[SMEM] + [VMEM] * 19,
        out_specs=(VMEM,) * 6,
        scratch_shapes=[pltpu.VMEM((tok_count, width), b16)] * 4,
        name="layer_backward",
    )(
        index, *returned, targets, logit_back, cot, hidden, second, flat, att, low, high, normed, q, k, v,
        mine, other, tokens, gains,
    )


def core_join(mine, other, core, axis=1):
    return jnp.concatenate(
        [jnp.where(core == 0, mine, other), jnp.where(core == 0, other, mine)], axis
    )


def gather_pieces(keep, send, chips, core):
    got = swap(send, "expert", 1)
    block = core_join(keep, got, core, 0)
    found = chip_gather(block, chips)
    pieces = []
    for parity, part in enumerate((found[: chips // 2], found[chips // 2 :])):
        first, second = dp_steps(parity)
        part = jnp.stack(part)
        near = jnp.stack([part, swap(part, "dp", first)])
        far = swap(near, "dp", second)
        pieces += [near, far]
    return pieces


def partner_pieces(pieces):
    result = []
    for piece in pieces:
        result.append(swap(piece, "expert", 1))
    return result


def scatter_blocks(keep, send, extra, chips, core):
    replicas = lax.axis_size("dp")
    got = swap(send, "expert", 1)
    blocks = keep.astype(jnp.float32) + got.astype(jnp.float32)
    if extra is not None:
        blocks = blocks + jnp.pad(extra, ((0, 0),) * 3 + ((blocks.shape[3] - LANES, 0),))
    lower, upper = blocks[:, : chips // 2], blocks[:, chips // 2 :]
    lower = dp_reduce([lower[k] for k in range(replicas)], 0)
    upper = dp_reduce([upper[k] for k in range(replicas)], 1)
    chip_blocks = [lower[k] for k in range(chips // 2)] + [upper[k] for k in range(chips // 2)]
    arrived = [swap(bf(chip_blocks[k]), "expert", 2 * k) for k in range(1, chips)]
    block = chip_blocks[0]
    for piece in arrived:
        block = block + piece.astype(jnp.float32)
    rows = block.shape[0] // 2
    mine = jnp.where(core == 0, block[:rows], block[rows:])
    theirs = jnp.where(core == 0, block[rows:], block[:rows])
    got = swap(bf(theirs), "expert", 1)
    return mine, got


def slot_positions(routes, experts):
    flat = routes.reshape(-1)
    expert_hot = (flat[:, None] == jnp.arange(experts, dtype=jnp.int32)[None, :]).astype(jnp.int32)
    earlier = jnp.cumsum(expert_hot, axis=0) - expert_hot
    return jnp.sum(earlier * expert_hot, axis=1).reshape(routes.shape)


def per_device(
    tokens,
    cotangent,
    buckets,
    routes,
    gain_attn,
    gain_moe,
    rel_bias,
    w_query,
    w_key,
    w_value,
    w_out,
    w_router,
    w_gate,
    w_up,
    w_down,
):
    f32 = jnp.float32
    groups = lax.axis_size("expert")
    chips = groups // 2
    replicas = lax.axis_size("dp")
    expert_index, dp_index = lax.axis_index("expert"), lax.axis_index("dp")
    core, chip_index = expert_index & 1, expert_index >> 1

    shard_rows = w_query.shape[0]
    experts = w_router.shape[1]
    n_bias = rel_bias.shape[0]
    model_width = tokens.shape[1]
    index = jnp.stack([dp_index, chip_index, jnp.int32(experts), core]).astype(jnp.int32)
    keep_a, keep_b, send_a, send_b = pack(
        index,
        (w_query, w_key, w_value, w_out),
        w_router,
        (gain_attn, gain_moe, rel_bias),
    )
    pieces = gather_pieces(keep_a, send_a, chips, core)
    pieces += gather_pieces(keep_b, send_b, chips, core)
    others = partner_pieces(pieces[:4]) + partner_pieces(pieces[4:])
    lane_ids = jnp.arange(model_width, dtype=jnp.int32)
    in_row = lane_ids % shard_rows
    flat_at = jnp.where(in_row < n_bias, lane_ids // shard_rows * n_bias + in_row, -1)
    head_of = jnp.where(flat_at >= 0, flat_at % H, -1)[None, :]
    bucket_of = jnp.where(flat_at >= 0, flat_at // H, -1)[:, None]
    hot = bf(bucket_of == jnp.arange(LANES, dtype=jnp.int32)[None, :])

    tok_count = tokens.shape[0]
    local_experts = w_gate.shape[0]
    capacity = max(2, 9 * tok_count // (4 * experts))
    unit = 2 * capacity
    chip_unit = local_experts * unit
    n_rows = chips * chip_unit
    group = routes // local_experts
    rel_core = (group & 1) ^ core
    rel_chip = (group >> 1) ^ chip_index
    targets = (
        rel_core * n_rows
        + rel_chip * chip_unit
        + (routes % local_experts) * unit
        + rel_core * capacity
        + slot_positions(routes, experts)
    )
    partner_targets = swap(targets, "expert", 1)
    partner_cot = swap(cotangent, "expert", 1)
    row_ids = jnp.arange(n_rows, dtype=jnp.int32)
    pick_own = [bf(row_ids[:, None] == targets[None, :, k]) for k in range(2)]
    pick_partner = [
        bf(row_ids[:, None] + n_rows == partner_targets[None, :, k]) for k in range(2)
    ]

    forward = layer_forward(
        index, pieces, others, tokens, buckets, routes, head_of, hot, experts
    )
    hidden_one, normed_two, gate_lanes = forward[10:13]
    partner_normed = swap(normed_two, "expert", 1)
    partner_gates = swap(gate_lanes, "expert", 1)
    gates = gate_lanes[:, :2]

    def dispatch(rows, split):
        def piece(k, e):
            at = k * chip_unit + e * unit
            return rows[at : at + unit]

        found = []
        if split:
            for e in range(local_experts):
                found.append(
                    [piece(0, e)] + [swap(piece(k, e), "expert", 2 * k) for k in range(1, chips)]
                )
        else:
            whole = [
                swap(rows[k * chip_unit : (k + 1) * chip_unit], "expert", 2 * k)
                for k in range(1, chips)
            ]
            for e in range(local_experts):
                found.append([piece(0, e)] + [w[e * unit : (e + 1) * unit] for w in whole])
        result = []
        for e in range(local_experts):
            block = jnp.concatenate(found[e], 0)
            if split:
                middle = block.shape[0] // 2
                halves = [dp_gather(block[:middle], 0), dp_gather(block[middle:], 1)]
                result.append([part for pair in zip(*halves) for part in pair])
            else:
                result.append(dp_gather(block, e % 2))
        return result

    picks = jnp.concatenate([pick_own[0] + pick_own[1], pick_partner[0] + pick_partner[1]], 1)
    picked = bf(matmul(picks, jnp.concatenate([normed_two, partner_normed], 0)))
    rows = dispatch(picked, True)
    grad_picks = jnp.concatenate(pick_own + pick_partner, 1)
    gated = [bf(gates[:, k : k + 1] * cotangent) for k in range(2)]
    gated += [bf(partner_gates[:, k : k + 1] * partner_cot) for k in range(2)]
    picked = bf(matmul(grad_picks, jnp.concatenate(gated, 0)))
    grads = dispatch(picked, False)

    def reduce_rows(parts, e):
        split = parts.reshape(replicas, chips * unit, model_width)
        total = dp_reduce([split[k] for k in range(replicas)], e % 2)
        return bf(total)

    def send_home(totals):
        found = [
            jnp.concatenate([t[k * unit : (k + 1) * unit] for t in totals], 0)
            for k in range(chips)
        ]
        found = found[:1] + [swap(found[k], "expert", 2 * k) for k in range(1, chips)]
        mine = jnp.concatenate(found, 0)
        return mine, swap(mine, "expert", 1)

    rows_e = [jnp.concatenate(rows[e], 0) for e in range(local_experts)]
    grads_e = [jnp.concatenate(grads[e], 0) for e in range(local_experts)]
    acts, saved, out_totals = [], [], []
    for e in range(local_experts):
        gate_pre = matmul(rows_e[e], w_gate[e])
        up_pre = matmul(rows_e[e], w_up[e])
        act = bf(geglu(gate_pre, up_pre))
        act, gate_pre, up_pre = lax.optimization_barrier((act, gate_pre, up_pre))
        acts.append(act)
        saved.append((gate_pre, up_pre))
        part = matmul_nt(act, w_down[e])
        out_totals.append(reduce_rows(part, e))
    back_totals, pres = [], []
    for e in range(local_experts):
        _, vjp = jax.vjp(geglu, *saved[e])
        gate_back_pre, up_back_pre = vjp(matmul(grads_e[e], w_down[e]))
        gate_back_pre, up_back_pre = bf(gate_back_pre), bf(up_back_pre)
        pres.append((gate_back_pre, up_back_pre))
        part = matmul_nt(gate_back_pre, w_gate[e]) + matmul_nt(up_back_pre, w_up[e])
        back_totals.append(reduce_rows(part, e))
    down_grad = jnp.stack([matmul_tn(grads_e[e], acts[e]) for e in range(local_experts)])
    gate_grad = jnp.stack([matmul_tn(rows_e[e], pres[e][0]) for e in range(local_experts)])
    up_grad = jnp.stack([matmul_tn(rows_e[e], pres[e][1]) for e in range(local_experts)])

    returned = send_home(out_totals)
    back_rows = send_home(back_totals)
    late_cot, *returned = lax.optimization_barrier((cotangent, *returned))
    layer_out, logit_back = combine(returned, targets, routes, gate_lanes, late_cot, hidden_one)
    keep_a, keep_b, send_a, send_b, tokens_grad, score_back = layer_backward(
        index, back_rows, targets, logit_back, late_cot, forward, tokens, chips, replicas
    )
    bucket_hot = bf(buckets[None] == jnp.arange(NB, dtype=jnp.int32)[:, None, None])
    bias_grad = lax.dot_general(
        bucket_hot, score_back, (((1, 2), (1, 2)), ((), ())), preferred_element_type=f32
    )
    bias_grad = jnp.pad(bias_grad, ((0, LANES - NB), (0, LANES - 2 * H)))
    extra = bias_blocks(index, bias_grad, swap(bias_grad, "expert", 1), hot, head_of.reshape(-1, 1), chips, replicas)
    groups = scatter_blocks(keep_a, send_a, None, chips, core)
    groups += scatter_blocks(keep_b, send_b, extra, chips, core)
    query_total, key_total, value_total, out_total, router_total, *vectors = finish(
        index, groups, experts, n_bias
    )
    return (
        layer_out,
        tokens_grad,
        vectors[0].reshape(-1),
        vectors[1].reshape(-1),
        vectors[2].reshape(-1),
        query_total,
        key_total,
        value_total,
        out_total,
        router_total.T,
        gate_grad,
        up_grad,
        down_grad,
    )


def solution(mesh):
    both = ("dp", "expert")
    row = P(both, None)

    return jax.shard_map(
        per_device,
        mesh=mesh,
        in_specs=(row, row, P(), row, P(both), P(both), P(both), row, row, row, row, row)
        + (P("expert", None, "dp"),) * 3,
        out_specs=(row, row, P(both), P(both), P(both), row, row, row, row, row)
        + (P("expert", None, "dp"),) * 3,
        check_vma=False,
    )
```

```python
import functools
import math

import jax
import jax.numpy as jnp
from jax import lax
from jax.experimental import pallas as pl
from jax.experimental.pallas import tpu as pltpu
from jax.sharding import PartitionSpec as P


H = 12
DH = 64
NB = 32
SEQ = 256
LANES = 128

EPSILON = 1e-06


def rms_apply(hidden, gain):
    factor = lax.rsqrt(jnp.mean(hidden * hidden, axis=-1, keepdims=True) + EPSILON)
    return hidden * factor * gain


def geglu(gate_pre, up_pre):
    return jax.nn.gelu(gate_pre, approximate=True) * up_pre


def matmul(left, right):
    return jnp.dot(left, right, preferred_element_type=jnp.float32)


def matmul_nt(left, right):
    return lax.dot_general(left, right, (((1,), (1,)), ((), ())), preferred_element_type=jnp.float32)


def matmul_tn(left, right):
    return lax.dot_general(left, right, (((0,), (0,)), ((), ())), preferred_element_type=jnp.float32)


def bf(value):
    return value.astype(jnp.bfloat16)


def swap(value, axis, distance):
    size = lax.axis_size(axis)
    return lax.ppermute(value, axis, [(i, i ^ distance) for i in range(size)])


def dp_steps(parity):
    return (1, 2) if parity == 0 else (2, 1)


def dp_gather(block, parity):
    first, second = dp_steps(parity)
    near = swap(block, "dp", first)
    pair = (block[None], near[None])
    far = swap(jnp.concatenate(pair, 0), "dp", second)
    found = {0: block, first: near, second: far[0], first | second: far[1]}
    return [found[k] for k in range(4)]


def dp_reduce(parts, parity):
    second, first = dp_steps(parity)
    got = swap(jnp.stack([bf(parts[first]), bf(parts[first | second])]), "dp", first)
    mine = parts[0] + got[0].astype(jnp.float32)
    other = parts[second] + got[1].astype(jnp.float32)
    last = swap(bf(other), "dp", second)
    return mine + last.astype(jnp.float32)


def chip_gather(block, chips):
    return [block] + [swap(block, "expert", 2 * k) for k in range(1, chips)]


SMEM = pl.BlockSpec(memory_space=pltpu.SMEM)
VMEM = pl.BlockSpec(memory_space=pltpu.VMEM)


def place_kernel(index_ref, near_low, far_low, near_up, far_up, out_ref):
    dp_index, chip_index = index_ref[0], index_ref[1]
    half = near_low.shape[1]
    for pieces, parity, base in (((near_low, far_low), 0, 0), ((near_up, far_up), 1, half)):
        first, second = dp_steps(parity)
        for far in range(2):
            for i in range(2):
                step = first * i + second * far
                for j in range(half):
                    out_ref[dp_index ^ step, chip_index ^ (base + j)] = pieces[far][i, j]


def place(index, pieces):
    _, half, rows, width = pieces[0].shape
    return pl.pallas_call(
        place_kernel,
        out_shape=jax.ShapeDtypeStruct((4, 2 * half, rows, width), pieces[0].dtype),
        in_specs=[SMEM] + [VMEM] * 4,
        out_specs=VMEM,
        name="place_weights",
    )(index, *pieces).reshape(-1, width)


def core_pick(core, first, second):
    return jnp.where(jnp.broadcast_to(core, first.shape) == 0, first, second)


def forward_kernel(placed, experts, *refs):
    if placed:
        index_ref, *refs = refs
        pieces, refs = refs[:16], refs[16:]
        tok_ref, bucket_ref, route_ref, head_ref, hot_ref, mine_ref, other_ref, *refs = refs
        dp_index, chip_index = index_ref[0], index_ref[1]
        half_chips, rows, width = pieces[0].shape[1:]
        for group in range(4):
            out = (mine_ref, mine_ref, other_ref, other_ref)[group]
            cut = slice(0, width) if group % 2 == 0 else slice(width, out.shape[1])
            for parity in range(2):
                first, second = dp_steps(parity)
                for far in range(2):
                    for i in range(2):
                        dp_at = dp_index ^ (first * i + second * far)
                        for j in range(half_chips):
                            chip_at = chip_index ^ (half_chips * parity + j)
                            at = pl.multiple_of((dp_at * 2 * half_chips + chip_at) * rows, rows)
                            out[pl.ds(at, rows), cut] = pieces[4 * group + 2 * parity + far][i, j]
    else:
        index_ref, mine_ref, other_ref, tok_ref, bucket_ref, route_ref, head_ref, hot_ref, *refs = refs
    n_ref, q_ref, k_ref, v_ref, low_ref, high_ref, att_ref, flat_ref = refs[:8]
    hidden_ref, second_ref, gate_ref, gain_ref, bias_ref = refs[8:]
    f32 = jnp.float32
    core = index_ref[3]
    half_seq = SEQ // 2
    half = q_ref.shape[1] // 2
    small = mine_ref[:, 4 * half :]
    vectors = small.astype(f32).T
    gain_ref[...] = vectors[experts : experts + 2]
    rows16 = lax.broadcasted_iota(jnp.int32, (16, vectors.shape[1]), 0)
    shifted = rows16 + core * (H // 2)
    wanted = jnp.where(rows16 < H, jnp.where(shifted >= H, shifted - H, shifted), -2)
    spread = jnp.where(head_ref[...] == wanted, vectors[experts + 2 : experts + 3], 0.0)
    bias_ref[...] = matmul(bf(spread), hot_ref[...])

    hidden = tok_ref[...].astype(f32)
    normed = bf(rms_apply(hidden, gain_ref[0:1]))
    n_ref[...] = normed
    for part, out in enumerate((q_ref, k_ref, v_ref)):
        cut = slice(part * half, (part + 1) * half)
        out[:, :half] = bf(matmul(normed, mine_ref[:, cut]))
        out[:, half:] = bf(matmul(normed, other_ref[:, cut]))
    scale = 1.0 / math.sqrt(DH)
    row_ids = lax.broadcasted_iota(jnp.int32, (half_seq, half_seq), 0)
    col_ids = lax.broadcasted_iota(jnp.int32, (half_seq, half_seq), 1)
    causal = row_ids >= col_ids

    def biased(raw, head, rows, cols):
        table = jnp.broadcast_to(bias_ref[pl.ds(head, 1), :], (half_seq, LANES))
        return raw * scale + jnp.take_along_axis(table, bucket_ref[rows, cols], axis=1)

    def softmax(blocks):
        peak = blocks[0].max(-1, keepdims=True)
        for b in blocks[1:]:
            peak = jnp.maximum(peak, b.max(-1, keepdims=True))
        exps = [jnp.exp(b - peak) for b in blocks]
        total = sum(x.sum(-1, keepdims=True) for x in exps)
        inverse = 1.0 / total
        return [x * inverse for x in exps]

    first, second = slice(0, half_seq), slice(half_seq, SEQ)

    def pair_step(pair, carry):
        lanes = pl.ds(pl.multiple_of(pair * 2 * DH, 2 * DH), 2 * DH)
        qp, kp, vp = q_ref[:, lanes], k_ref[:, lanes], v_ref[:, lanes]
        outs_low, outs_high = [], []
        for sub in range(2):
            head = pair * 2 + sub
            cut = slice(sub * DH, (sub + 1) * DH)
            q, k, v = qp[:, cut], kp[:, cut], vp[:, cut]
            s00 = biased(matmul_nt(q[first], k[first]), head, first, first)
            s1 = matmul_nt(q[second], k)
            s10 = biased(s1[:, first], head, second, first)
            s11 = biased(s1[:, second], head, second, second)
            (p00,) = softmax([jnp.where(causal, s00, -1e30)])
            p10, p11 = softmax([s10, jnp.where(causal, s11, -1e30)])
            low_ref[head] = p00
            high_ref[head, :, first] = p10
            high_ref[head, :, second] = p11
            outs_low.append(matmul(bf(p00), v[first]))
            outs_high.append(matmul(bf(p10), v[first]) + matmul(bf(p11), v[second]))
        att_ref[first, lanes] = bf(jnp.concatenate(outs_low, 1))
        att_ref[second, lanes] = bf(jnp.concatenate(outs_high, 1))
        return carry

    lax.fori_loop(0, H // 2, pair_step, 0)
    att_mine, att_other = att_ref[:, :half].astype(f32), att_ref[:, half:].astype(f32)
    flat_ref[:, :half] = bf(core_pick(core, att_mine, att_other))
    flat_ref[:, half:] = bf(core_pick(core, att_other, att_mine))
    flat = flat_ref[...]
    cut = slice(3 * half, 4 * half)
    out_mine, out_other = matmul(flat, mine_ref[:, cut]), matmul(flat, other_ref[:, cut])
    hidden_ref[:, :half] = hidden[:, :half] + core_pick(core, out_mine, out_other)
    hidden_ref[:, half:] = hidden[:, half:] + core_pick(core, out_other, out_mine)
    normed_two = bf(rms_apply(hidden_ref[...], gain_ref[1:2]))
    second_ref[...] = normed_two
    logits = matmul(normed_two, small)
    lane = lax.broadcasted_iota(jnp.int32, logits.shape, 1)
    chosen = [
        jnp.sum(jnp.where(lane == route_ref[:, k : k + 1], logits, 0.0), 1, keepdims=True)
        for k in range(2)
    ]
    peak = jnp.maximum(chosen[0], chosen[1])
    exps = [jnp.exp(c - peak) for c in chosen]
    total = exps[0] + exps[1]
    gate_ref[...] = jnp.where(lane == 0, exps[0] / total, jnp.where(lane == 1, exps[1] / total, 0.0))


def layer_forward(index, mine, other, tokens, buckets, routes, head_of, hot, experts):
    tok_count, width = tokens.shape
    b16, f32 = jnp.bfloat16, jnp.float32
    shaped = jax.ShapeDtypeStruct
    flat, total = shaped((tok_count, width), b16), mine[0].shape[-1] + mine[4].shape[-1]
    placed = mine[0].shape[2] % 16 == 0
    weights = (shaped((width, total), b16),) * 2
    if placed:
        inputs = tuple(mine) + tuple(other)
    else:
        inputs = tuple(
            jnp.concatenate([place(index, p[:4]), place(index, p[4:])], 1) for p in (mine, other)
        )
    tail = (tokens, buckets, routes, head_of, hot)
    result = pl.pallas_call(
        functools.partial(forward_kernel, placed, experts),
        out_shape=(weights if placed else ())
        + (flat, flat, flat, flat)
        + (shaped((H, SEQ // 2, SEQ // 2), f32), shaped((H, SEQ // 2, SEQ), f32), flat, flat)
        + (shaped((tok_count, width), f32), flat, shaped((tok_count, LANES), f32), shaped((2, width), f32)),
        in_specs=[SMEM] + [VMEM] * (len(inputs) + len(tail)),
        out_specs=(VMEM,) * (14 if placed else 12),
        scratch_shapes=[pltpu.VMEM((16, LANES), f32)],
        name="layer_forward",
    )(index, *inputs, *tail)
    return result if placed else inputs + result


def pick_rows(target_ref, k, at, count):
    ids = lax.broadcasted_iota(jnp.int32, (target_ref.shape[0], count), 1) + at
    return (ids == target_ref[:, k : k + 1]).astype(jnp.float32)


def combine_kernel(
    ret_mine_ref, ret_other_ref, target_ref, route_ref, gate_ref, cot_ref, hidden_ref, out_ref, logit_ref
):
    count = ret_mine_ref.shape[0]
    gates = [gate_ref[:, k : k + 1] for k in range(2)]
    total = hidden_ref[...]
    backs = []
    for k in range(2):
        value = matmul(bf(pick_rows(target_ref, k, 0, count)), ret_mine_ref[...])
        value += matmul(bf(pick_rows(target_ref, k, count, count)), ret_other_ref[...])
        total += gates[k] * value
        backs.append(jnp.sum(cot_ref[...] * value, axis=1, keepdims=True))
    out_ref[...] = total
    mean = gates[0] * backs[0] + gates[1] * backs[1]
    lane = lax.broadcasted_iota(jnp.int32, logit_ref.shape, 1)
    logit = jnp.zeros(logit_ref.shape, jnp.float32)
    for k in range(2):
        logit += jnp.where(lane == route_ref[:, k : k + 1], gates[k] * (backs[k] - mean), 0.0)
    logit_ref[...] = bf(logit)


def combine(returned, targets, routes, gate_lanes, cot, hidden):
    shaped = jax.ShapeDtypeStruct
    return pl.pallas_call(
        combine_kernel,
        out_shape=(
            shaped(hidden.shape, jnp.float32),
            shaped((hidden.shape[0], LANES), jnp.bfloat16),
        ),
        in_specs=[VMEM] * 7,
        out_specs=(VMEM,) * 2,
        name="combine_experts",
    )(*returned, targets, routes, gate_lanes, cot, hidden)


def pack_kernel(index_ref, q_ref, k_ref, v_ref, o_ref, router_ref, one_ref, two_ref, bias_ref, *outs):
    keep_a, keep_b, send_a, send_b, pad_ref = outs
    core, experts = index_ref[3], router_ref.shape[0]
    rows, width = q_ref.shape
    half = width // 2
    f32 = jnp.float32
    for i, ref in enumerate((q_ref, k_ref, v_ref, o_ref)):
        left, right = ref[:, :half].astype(f32), ref[:, half:].astype(f32)
        cut = slice(i % 2 * half, (i % 2 + 1) * half)
        (keep_a if i < 2 else keep_b)[:, cut] = bf(core_pick(core, left, right))
        (send_a if i < 2 else send_b)[:, cut] = bf(core_pick(core, right, left))
    pad_ref[...] = jnp.zeros(pad_ref.shape, f32)
    for i, ref in enumerate((one_ref, two_ref, bias_ref)):
        pad_ref[experts + i : experts + i + 1, : ref.shape[1]] = ref[...].astype(f32)
    pad_ref[:experts, :rows] = router_ref[...].astype(f32)
    small = bf(pad_ref[...].T[:rows])
    keep_b[:, width:] = small
    send_b[:, width:] = small


def pack(index, weights, router, vectors):
    rows, width = weights[0].shape
    out_a = jax.ShapeDtypeStruct((rows, width), jnp.bfloat16)
    out_b = jax.ShapeDtypeStruct((rows, width + LANES), jnp.bfloat16)
    return pl.pallas_call(
        pack_kernel,
        out_shape=(out_a, out_b) * 2,
        in_specs=[SMEM] + [VMEM] * 8,
        out_specs=(VMEM,) * 4,
        scratch_shapes=[pltpu.VMEM((LANES, LANES), jnp.float32)],
        name="pack_shards",
    )(index, *weights, router.T, *[v[None, :] for v in vectors])


def bias_kernel(index_ref, mine_ref, other_ref, hot_ref, head_ref, out_ref):
    f32 = jnp.float32
    core = index_ref[3]
    replicas, chips, rows, lanes = out_ref.shape
    lane = lax.broadcasted_iota(jnp.int32, (hot_ref.shape[0], lanes), 1)
    head = jnp.broadcast_to(head_ref[...].astype(f32), (lanes, lane.shape[0])).T.astype(jnp.int32)
    total = jnp.zeros(lane.shape, f32)
    for i, ref in enumerate((mine_ref, other_ref)):
        shifted = head + (core ^ i) * (H // 2)
        local = jnp.where(head < 0, -1, jnp.where(shifted >= H, shifted - H, shifted))
        rest = ref[...]
        for _ in range(2):
            part = bf(rest)
            rest = rest - part.astype(f32)
            spread = matmul(hot_ref[...], part)
            total += jnp.where((lane == local) | (lane == jnp.where(local < 0, -1, local + H)), spread, 0.0)
    column = jnp.sum(total, axis=1, keepdims=True)
    value = jnp.where(lane == index_ref[2] + 2, column, 0.0)
    for i in range(replicas):
        for j in range(chips):
            at = (i * chips + j) * rows
            out_ref[index_ref[0] ^ i, index_ref[1] ^ j] = value[at : at + rows]


def bias_blocks(index, mine, other, hot, head_of, chips, replicas):
    rows = hot.shape[0] // (replicas * chips)
    return pl.pallas_call(
        bias_kernel,
        out_shape=jax.ShapeDtypeStruct((replicas, chips, rows, LANES), jnp.float32),
        in_specs=[SMEM] + [VMEM] * 4,
        out_specs=VMEM,
        name="bias_column",
    )(index, mine, other, hot, head_of)


def finish_kernel(index_ref, mine_a, got_a, mine_b, got_b, q_ref, k_ref, v_ref, o_ref, router_ref, *vector_refs):
    core, experts = index_ref[3], router_ref.shape[0]
    rows, width = q_ref.shape
    half = width // 2
    for i, ref in enumerate((q_ref, k_ref, v_ref, o_ref)):
        cut = slice(i % 2 * half, (i % 2 + 1) * half)
        mine_ref, got_ref = (mine_a, got_a) if i < 2 else (mine_b, got_b)
        mine, other = mine_ref[:, cut], got_ref[:, cut].astype(jnp.float32)
        ref[:, :half] = core_pick(core, mine, other)
        ref[:, half:] = core_pick(core, other, mine)
    small = mine_b[:, width:]
    padded = jnp.concatenate([small, jnp.zeros((LANES - rows, LANES), jnp.float32)], 0).T
    router_ref[...] = padded[:experts, :rows]
    for i, ref in enumerate(vector_refs):
        ref[...] = padded[experts + i : experts + i + 1, : ref.shape[1]]


def finish(index, groups, experts, n_bias):
    rows, width = groups[0].shape
    shaped = lambda *dims: jax.ShapeDtypeStruct(dims, jnp.float32)
    return pl.pallas_call(
        finish_kernel,
        out_shape=(shaped(rows, width),) * 4
        + (shaped(experts, rows), shaped(1, rows), shaped(1, rows), shaped(1, n_bias)),
        in_specs=[SMEM] + [VMEM] * 4,
        out_specs=(VMEM,) * 8,
        name="finish_shared",
    )(index, *groups)


def backward_kernel(
    index_ref, ret_mine_ref, ret_other_ref, target_ref, logit_ref, cot_ref, hidden_ref, second_ref, flat_ref, att_ref, low_ref, high_ref,
    n_ref, q_ref, k_ref, v_ref, mine_ref, other_ref, tok_ref, gain_ref,
    keep_a, keep_b, keep_c, send_a, send_b, send_c, grad_ref, score_ref, qb_ref, kb_ref, vb_ref, ab_ref,
):
    f32 = jnp.float32
    half_seq = SEQ // 2
    scale = 1.0 / math.sqrt(DH)
    first, second = slice(0, half_seq), slice(half_seq, SEQ)
    half = ab_ref.shape[1] // 2
    replicas, chips, rows, _ = keep_a.shape
    dp_index, chip_index, experts, core = (index_ref[i] for i in range(4))
    payload = 4 * half

    def store(kept, sent, part):
        at = part % 2 * half
        cut = slice(at, at + kept.shape[1])
        outs = ((keep_a, send_a), (keep_b, send_b), (keep_c, send_c))[part // 2]
        for out, value in zip(outs, (bf(kept), bf(sent))):
            for i in range(replicas):
                for j in range(chips):
                    at = (i * chips + j) * rows
                    out[dp_index ^ i, chip_index ^ j, :, cut] = value[at : at + rows]

    def norm_back(hidden, gain, upstream):
        factor = lax.rsqrt(jnp.mean(hidden * hidden, axis=-1, keepdims=True) + EPSILON)
        scaled = upstream * gain
        inner = jnp.mean(scaled * hidden, axis=-1, keepdims=True)
        gain_back = jnp.sum(upstream * (hidden * factor), axis=0, keepdims=True)
        return factor * (scaled - hidden * (factor * factor * inner)), gain_back

    token_back = jnp.zeros(tok_ref.shape, f32)
    for at, ref in ((0, ret_mine_ref), (ret_mine_ref.shape[0], ret_other_ref)):
        picked = sum(pick_rows(target_ref, k, at, ref.shape[0]) for k in range(2))
        token_back += matmul(bf(picked), ref[...])
    logit_back = logit_ref[...]
    small_w = mine_ref[:, payload:]
    hidden_back, gain_two_back = norm_back(
        hidden_ref[...], gain_ref[1:2], token_back + matmul_nt(logit_back, small_w)
    )
    hidden_back = cot_ref[...] + hidden_back
    grad_ref[...] = hidden_back
    left, right = hidden_back[:, :half], hidden_back[:, half:]
    res_mine, res_other = bf(core_pick(core, left, right)), bf(core_pick(core, right, left))
    cut = slice(3 * half, payload)
    ab = matmul_nt(res_mine, mine_ref[:, cut]) + matmul_nt(res_other, other_ref[:, cut])
    left, right = ab[:, :half], ab[:, half:]
    ab_ref[:, :half] = bf(core_pick(core, left, right))
    ab_ref[:, half:] = bf(core_pick(core, right, left))
    flat = flat_ref[...]
    store(matmul_tn(flat, res_mine), matmul_tn(flat, res_other), 3)

    def pair_step(pair, carry):
        lanes = pl.ds(pl.multiple_of(pair * 2 * DH, 2 * DH), 2 * DH)
        qp, kp, vp = q_ref[:, lanes], k_ref[:, lanes], v_ref[:, lanes]
        abp, attp = ab_ref[:, lanes], att_ref[:, lanes]
        found = [[], [], []]
        for sub in range(2):
            head = pair * 2 + sub
            cut = slice(sub * DH, (sub + 1) * DH)
            q, k, v, ab, att = qp[:, cut], kp[:, cut], vp[:, cut], abp[:, cut], attp[:, cut]
            delta = jnp.sum(ab.astype(f32) * att.astype(f32), axis=1, keepdims=True)
            low, high = low_ref[head], high_ref[head]
            low_b, high_b = bf(low), bf(high)
            value_low = matmul_tn(low_b, ab[first])
            value_high = matmul_tn(high_b, ab[second])
            found[2].append(
                jnp.concatenate([value_low + value_high[first], value_high[second]], 0)
            )
            back_low = low * (matmul_nt(ab[first], v[first]) - delta[first])
            back_high = high * (matmul_nt(ab[second], v) - delta[second])
            low_r, high_r = bf(back_low), bf(back_high)
            for at, low_s, high_s in (
                (head, low_r, high_r),
                (head + H, bf(back_low - low_r.astype(f32)), bf(back_high - high_r.astype(f32))),
            ):
                score_ref[at, first, first] = low_s
                score_ref[at, first, second] = jnp.zeros_like(low_s)
                score_ref[at, second, :] = high_s
            found[0].append(
                jnp.concatenate([matmul(low_r, k[first]), matmul(high_r, k)], 0) * scale
            )
            key_low = matmul_tn(low_r, q[first])
            key_high = matmul_tn(high_r, q[second])
            found[1].append(
                jnp.concatenate([key_low + key_high[first], key_high[second]], 0) * scale
            )
        for out, value in zip((qb_ref, kb_ref, vb_ref), found):
            out[:, lanes] = bf(jnp.concatenate(value, 1))
        return carry

    lax.fori_loop(0, H // 2, pair_step, 0)

    normed = n_ref[...]
    normed_back = jnp.zeros(tok_ref.shape, f32)
    for part, ref in enumerate((qb_ref, kb_ref, vb_ref)):
        cut = slice(part * half, (part + 1) * half)
        mine_b, other_b = ref[:, :half], ref[:, half:]
        store(matmul_tn(normed, mine_b), matmul_tn(normed, other_b), part)
        normed_back += matmul_nt(mine_b, mine_ref[:, cut]) + matmul_nt(other_b, other_ref[:, cut])
    token_back, gain_one_back = norm_back(tok_ref[...].astype(f32), gain_ref[0:1], normed_back)
    grad_ref[...] += token_back
    small = matmul_tn(second_ref[...], logit_back)
    lane = lax.broadcasted_iota(jnp.int32, small.shape, 1)
    for at, gain_back in ((experts, gain_one_back), (experts + 1, gain_two_back)):
        wide = jnp.broadcast_to(gain_back, (LANES, gain_back.shape[1])).T
        small = jnp.where(lane == at, wide, small)
    store(small, small, 4)


def layer_backward(index, returned, targets, logit_back, cot, forward, tokens, chips, replicas):
    mine, other, normed, q, k, v, low, high, att, flat, hidden, second, _, gains = forward
    tok_count, width = tokens.shape
    b16, f32 = jnp.bfloat16, jnp.float32
    shaped = jax.ShapeDtypeStruct
    blocks = (replicas, chips, width // (replicas * chips))
    groups = tuple(shaped(blocks + (w,), b16) for w in (width, width, LANES))
    return pl.pallas_call(
        backward_kernel,
        out_shape=groups
        + groups
        + (
            shaped((tok_count, width), f32),
            shaped((2 * H, SEQ, SEQ), b16),
        ),
        in_specs=[SMEM] + [VMEM] * 19,
        out_specs=(VMEM,) * 8,
        scratch_shapes=[pltpu.VMEM((tok_count, width), b16)] * 4,
        name="layer_backward",
    )(
        index, *returned, targets, logit_back, cot, hidden, second, flat, att, low, high, normed, q, k, v,
        mine, other, tokens, gains,
    )


def core_join(mine, other, core, axis=1):
    return jnp.concatenate(
        [jnp.where(core == 0, mine, other), jnp.where(core == 0, other, mine)], axis
    )


def gather_pieces(keep, send, chips, core):
    got = swap(send, "expert", 1)
    block = core_join(keep, got, core, 0)
    found = chip_gather(block, chips)
    pieces = []
    for parity, part in enumerate((found[: chips // 2], found[chips // 2 :])):
        first, second = dp_steps(parity)
        part = jnp.stack(part)
        near = jnp.stack([part, swap(part, "dp", first)])
        far = swap(near, "dp", second)
        pieces += [near, far]
    return pieces


def partner_pieces(pieces):
    result = []
    for piece in pieces:
        result.append(swap(piece, "expert", 1))
    return result


def reduce_dp(keep, send, extra, chips):
    replicas = lax.axis_size("dp")
    got = swap(send, "expert", 1)
    blocks = keep.astype(jnp.float32) + got.astype(jnp.float32)
    if extra is not None:
        blocks = blocks + extra
    lower, upper = blocks[:, : chips // 2], blocks[:, chips // 2 :]
    lower = dp_reduce([lower[k] for k in range(replicas)], 0)
    upper = dp_reduce([upper[k] for k in range(replicas)], 1)
    return [lower[k] for k in range(chips // 2)] + [upper[k] for k in range(chips // 2)]


def reduce_chips(chip_blocks, core):
    arrived = [
        swap(bf(chip_blocks[k]), "expert", 2 * k) for k in range(1, len(chip_blocks))
    ]
    block = chip_blocks[0]
    for piece in arrived:
        block = block + piece.astype(jnp.float32)
    rows = block.shape[0] // 2
    mine = jnp.where(core == 0, block[:rows], block[rows:])
    theirs = jnp.where(core == 0, block[rows:], block[:rows])
    got = swap(bf(theirs), "expert", 1)
    return mine, got


def slot_positions(routes, experts):
    flat = routes.reshape(-1)
    expert_hot = (flat[:, None] == jnp.arange(experts, dtype=jnp.int32)[None, :]).astype(jnp.int32)
    earlier = jnp.cumsum(expert_hot, axis=0) - expert_hot
    return jnp.sum(earlier * expert_hot, axis=1).reshape(routes.shape)


def per_device(
    tokens,
    cotangent,
    buckets,
    routes,
    gain_attn,
    gain_moe,
    rel_bias,
    w_query,
    w_key,
    w_value,
    w_out,
    w_router,
    w_gate,
    w_up,
    w_down,
):
    f32 = jnp.float32
    groups = lax.axis_size("expert")
    chips = groups // 2
    replicas = lax.axis_size("dp")
    expert_index, dp_index = lax.axis_index("expert"), lax.axis_index("dp")
    core, chip_index = expert_index & 1, expert_index >> 1

    shard_rows = w_query.shape[0]
    experts = w_router.shape[1]
    n_bias = rel_bias.shape[0]
    model_width = tokens.shape[1]
    index = jnp.stack([dp_index, chip_index, jnp.int32(experts), core]).astype(jnp.int32)
    keep_a, keep_b, send_a, send_b = pack(
        index,
        (w_query, w_key, w_value, w_out),
        w_router,
        (gain_attn, gain_moe, rel_bias),
    )
    pieces = gather_pieces(keep_a, send_a, chips, core)
    pieces += gather_pieces(keep_b, send_b, chips, core)
    others = partner_pieces(pieces[:4]) + partner_pieces(pieces[4:])
    lane_ids = jnp.arange(model_width, dtype=jnp.int32)
    in_row = lane_ids % shard_rows
    flat_at = jnp.where(in_row < n_bias, lane_ids // shard_rows * n_bias + in_row, -1)
    head_of = jnp.where(flat_at >= 0, flat_at % H, -1)[None, :]
    bucket_of = jnp.where(flat_at >= 0, flat_at // H, -1)[:, None]
    hot = bf(bucket_of == jnp.arange(LANES, dtype=jnp.int32)[None, :])

    tok_count = tokens.shape[0]
    local_experts = w_gate.shape[0]
    capacity = max(2, 9 * tok_count // (4 * experts))
    unit = 2 * capacity
    chip_unit = local_experts * unit
    n_rows = chips * chip_unit
    group = routes // local_experts
    rel_core = (group & 1) ^ core
    rel_chip = (group >> 1) ^ chip_index
    targets = (
        rel_core * n_rows
        + rel_chip * chip_unit
        + (routes % local_experts) * unit
        + rel_core * capacity
        + slot_positions(routes, experts)
    )
    partner_targets = swap(targets, "expert", 1)
    partner_cot = swap(cotangent, "expert", 1)
    row_ids = jnp.arange(n_rows, dtype=jnp.int32)
    pick_own = [bf(row_ids[:, None] == targets[None, :, k]) for k in range(2)]
    pick_partner = [
        bf(row_ids[:, None] + n_rows == partner_targets[None, :, k]) for k in range(2)
    ]

    forward = layer_forward(
        index, pieces, others, tokens, buckets, routes, head_of, hot, experts
    )
    hidden_one, normed_two, gate_lanes = forward[10:13]
    partner_normed = swap(normed_two, "expert", 1)
    partner_gates = swap(gate_lanes, "expert", 1)
    gates = gate_lanes[:, :2]

    def dispatch(rows, split):
        def piece(k, e):
            at = k * chip_unit + e * unit
            return rows[at : at + unit]

        found = []
        if split:
            for e in range(local_experts):
                found.append(
                    [piece(0, e)] + [swap(piece(k, e), "expert", 2 * k) for k in range(1, chips)]
                )
        else:
            whole = [
                swap(rows[k * chip_unit : (k + 1) * chip_unit], "expert", 2 * k)
                for k in range(1, chips)
            ]
            for e in range(local_experts):
                found.append([piece(0, e)] + [w[e * unit : (e + 1) * unit] for w in whole])
        result = []
        for e in range(local_experts):
            block = jnp.concatenate(found[e], 0)
            if split:
                middle = block.shape[0] // 2
                halves = [dp_gather(block[:middle], 0), dp_gather(block[middle:], 1)]
                result.append([part for pair in zip(*halves) for part in pair])
            else:
                result.append(dp_gather(block, e % 2))
        return result

    picks = jnp.concatenate([pick_own[0] + pick_own[1], pick_partner[0] + pick_partner[1]], 1)
    picked = bf(matmul(picks, jnp.concatenate([normed_two, partner_normed], 0)))
    rows = dispatch(picked, True)
    grad_picks = jnp.concatenate(pick_own + pick_partner, 1)
    gated = [bf(gates[:, k : k + 1] * cotangent) for k in range(2)]
    gated += [bf(partner_gates[:, k : k + 1] * partner_cot) for k in range(2)]
    picked = bf(matmul(grad_picks, jnp.concatenate(gated, 0)))
    grads = dispatch(picked, False)

    def reduce_rows(parts, e):
        split = parts.reshape(replicas, chips * unit, model_width)
        total = dp_reduce([split[k] for k in range(replicas)], e % 2)
        return bf(total)

    def send_home(totals):
        found = [
            jnp.concatenate([t[k * unit : (k + 1) * unit] for t in totals], 0)
            for k in range(chips)
        ]
        found = found[:1] + [swap(found[k], "expert", 2 * k) for k in range(1, chips)]
        mine = jnp.concatenate(found, 0)
        return mine, swap(mine, "expert", 1)

    rows_e = [jnp.concatenate(rows[e], 0) for e in range(local_experts)]
    grads_e = [jnp.concatenate(grads[e], 0) for e in range(local_experts)]
    acts, saved, out_totals = [], [], []
    for e in range(local_experts):
        gate_pre = matmul(rows_e[e], w_gate[e])
        up_pre = matmul(rows_e[e], w_up[e])
        act = bf(geglu(gate_pre, up_pre))
        act, gate_pre, up_pre = lax.optimization_barrier((act, gate_pre, up_pre))
        acts.append(act)
        saved.append((gate_pre, up_pre))
        part = matmul_nt(act, w_down[e])
        out_totals.append(reduce_rows(part, e))
    back_totals, pres = [], []
    for e in range(local_experts):
        _, vjp = jax.vjp(geglu, *saved[e])
        gate_back_pre, up_back_pre = vjp(matmul(grads_e[e], w_down[e]))
        gate_back_pre, up_back_pre = bf(gate_back_pre), bf(up_back_pre)
        pres.append((gate_back_pre, up_back_pre))
        part = matmul_nt(gate_back_pre, w_gate[e]) + matmul_nt(up_back_pre, w_up[e])
        back_totals.append(reduce_rows(part, e))
    down_grad = jnp.stack([matmul_tn(grads_e[e], acts[e]) for e in range(local_experts)])
    gate_grad = jnp.stack([matmul_tn(rows_e[e], pres[e][0]) for e in range(local_experts)])
    up_grad = jnp.stack([matmul_tn(rows_e[e], pres[e][1]) for e in range(local_experts)])

    returned = send_home(out_totals)
    back_rows = send_home(back_totals)
    late_cot, *returned = lax.optimization_barrier((cotangent, *returned))
    layer_out, logit_back = combine(returned, targets, routes, gate_lanes, late_cot, hidden_one)
    *shared, tokens_grad, score_back = layer_backward(
        index, back_rows, targets, logit_back, late_cot, forward, tokens, chips, replicas
    )
    bucket_hot = bf(buckets[None] == jnp.arange(NB, dtype=jnp.int32)[:, None, None])
    bias_grad = lax.dot_general(
        bucket_hot, score_back, (((1, 2), (1, 2)), ((), ())), preferred_element_type=f32
    )
    bias_grad = jnp.pad(bias_grad, ((0, LANES - NB), (0, LANES - 2 * H)))
    extra = bias_blocks(
        index, bias_grad, swap(bias_grad, "expert", 1), hot, head_of, chips, replicas
    )
    keep_a, keep_b, keep_c, send_a, send_b, send_c = shared
    groups = reduce_chips(reduce_dp(keep_a, send_a, None, chips), core)
    blocks_b = reduce_dp(keep_b, send_b, None, chips)
    blocks_c = reduce_dp(keep_c, send_c, extra, chips)
    joined = [jnp.concatenate(pair, 1) for pair in zip(blocks_b, blocks_c)]
    groups += reduce_chips(joined, core)
    query_total, key_total, value_total, out_total, router_total, *vectors = finish(
        index, groups, experts, n_bias
    )
    return (
        layer_out,
        tokens_grad,
        vectors[0].reshape(-1),
        vectors[1].reshape(-1),
        vectors[2].reshape(-1),
        query_total,
        key_total,
        value_total,
        out_total,
        router_total.T,
        gate_grad,
        up_grad,
        down_grad,
    )


def solution(mesh):
    both = ("dp", "expert")
    row = P(both, None)

    return jax.shard_map(
        per_device,
        mesh=mesh,
        in_specs=(row, row, P(), row, P(both), P(both), P(both), row, row, row, row, row)
        + (P("expert", None, "dp"),) * 3,
        out_specs=(row, row, P(both), P(both), P(both), row, row, row, row, row)
        + (P("expert", None, "dp"),) * 3,
        check_vma=False,
    )
```

```python
import functools
import math

import jax
import jax.numpy as jnp
from jax import lax
from jax.experimental import pallas as pl
from jax.experimental.pallas import tpu as pltpu
from jax.sharding import PartitionSpec as P


H = 12
DH = 64
NB = 32
SEQ = 256
LANES = 128

EPSILON = 1e-06


def rms_apply(hidden, gain):
    factor = lax.rsqrt(jnp.mean(hidden * hidden, axis=-1, keepdims=True) + EPSILON)
    return hidden * factor * gain


def geglu(gate_pre, up_pre):
    return jax.nn.gelu(gate_pre, approximate=True) * up_pre


def matmul(left, right):
    return jnp.dot(left, right, preferred_element_type=jnp.float32)


def matmul_nt(left, right):
    return lax.dot_general(left, right, (((1,), (1,)), ((), ())), preferred_element_type=jnp.float32)


def matmul_tn(left, right):
    return lax.dot_general(left, right, (((0,), (0,)), ((), ())), preferred_element_type=jnp.float32)


def bf(value):
    return value.astype(jnp.bfloat16)


def swap(value, axis, distance):
    size = lax.axis_size(axis)
    return lax.ppermute(value, axis, [(i, i ^ distance) for i in range(size)])


def dp_steps(parity):
    return (1, 2) if parity == 0 else (2, 1)


def dp_gather(block, parity):
    first, second = dp_steps(parity)
    near = swap(block, "dp", first)
    pair = (block[None], near[None])
    far = swap(jnp.concatenate(pair, 0), "dp", second)
    found = {0: block, first: near, second: far[0], first | second: far[1]}
    return [found[k] for k in range(4)]


def dp_finish(held, sent, parity):
    second, first = dp_steps(parity)
    got = swap(sent, "dp", first)
    other = held[1] + got[1].astype(jnp.float32)
    last = swap(bf(other), "dp", second)
    return held[0] + got[0].astype(jnp.float32) + last.astype(jnp.float32)


def dp_reduce(parts, parity):
    second, first = dp_steps(parity)
    sent = jnp.stack([bf(parts[first]), bf(parts[first | second])])
    return dp_finish((parts[0], parts[second]), sent, parity)


def chip_gather(block, chips):
    return [block] + [swap(block, "expert", 2 * k) for k in range(1, chips)]


SMEM = pl.BlockSpec(memory_space=pltpu.SMEM)
VMEM = pl.BlockSpec(memory_space=pltpu.VMEM)


def place_kernel(index_ref, near_low, far_low, near_up, far_up, out_ref):
    dp_index, chip_index = index_ref[0], index_ref[1]
    half = near_low.shape[1]
    for pieces, parity, base in (((near_low, far_low), 0, 0), ((near_up, far_up), 1, half)):
        first, second = dp_steps(parity)
        for far in range(2):
            for i in range(2):
                step = first * i + second * far
                for j in range(half):
                    out_ref[dp_index ^ step, chip_index ^ (base + j)] = pieces[far][i, j]


def place(index, pieces):
    _, half, rows, width = pieces[0].shape
    return pl.pallas_call(
        place_kernel,
        out_shape=jax.ShapeDtypeStruct((4, 2 * half, rows, width), pieces[0].dtype),
        in_specs=[SMEM] + [VMEM] * 4,
        out_specs=VMEM,
        name="place_weights",
    )(index, *pieces).reshape(-1, width)


def core_pick(core, first, second):
    return jnp.where(jnp.broadcast_to(core, first.shape) == 0, first, second)


def forward_kernel(placed, experts, *refs):
    if placed:
        index_ref, *refs = refs
        pieces, refs = refs[:16], refs[16:]
        tok_ref, bucket_ref, route_ref, head_ref, hot_ref, mine_ref, other_ref, *refs = refs
        dp_index, chip_index = index_ref[0], index_ref[1]
        half_chips, rows, width = pieces[0].shape[1:]
        for group in range(4):
            out = (mine_ref, mine_ref, other_ref, other_ref)[group]
            cut = slice(0, width) if group % 2 == 0 else slice(width, out.shape[1])
            for parity in range(2):
                first, second = dp_steps(parity)
                for far in range(2):
                    for i in range(2):
                        dp_at = dp_index ^ (first * i + second * far)
                        for j in range(half_chips):
                            chip_at = chip_index ^ (half_chips * parity + j)
                            at = pl.multiple_of((dp_at * 2 * half_chips + chip_at) * rows, rows)
                            out[pl.ds(at, rows), cut] = pieces[4 * group + 2 * parity + far][i, j]
    else:
        index_ref, mine_ref, other_ref, tok_ref, bucket_ref, route_ref, head_ref, hot_ref, *refs = refs
    n_ref, q_ref, k_ref, v_ref, low_ref, high_ref, att_ref, flat_ref = refs[:8]
    hidden_ref, second_ref, gate_ref, gain_ref, bias_ref = refs[8:]
    f32 = jnp.float32
    core = index_ref[3]
    half_seq = SEQ // 2
    half = q_ref.shape[1] // 2
    small = mine_ref[:, 4 * half :]
    vectors = small.astype(f32).T
    gain_ref[...] = vectors[experts : experts + 2]
    rows16 = lax.broadcasted_iota(jnp.int32, (16, vectors.shape[1]), 0)
    shifted = rows16 + core * (H // 2)
    wanted = jnp.where(rows16 < H, jnp.where(shifted >= H, shifted - H, shifted), -2)
    spread = jnp.where(head_ref[...] == wanted, vectors[experts + 2 : experts + 3], 0.0)
    bias_ref[...] = matmul(bf(spread), hot_ref[...])

    hidden = tok_ref[...].astype(f32)
    normed = bf(rms_apply(hidden, gain_ref[0:1]))
    n_ref[...] = normed
    for part, out in enumerate((q_ref, k_ref, v_ref)):
        cut = slice(part * half, (part + 1) * half)
        out[:, :half] = bf(matmul(normed, mine_ref[:, cut]))
        out[:, half:] = bf(matmul(normed, other_ref[:, cut]))
    scale = 1.0 / math.sqrt(DH)
    row_ids = lax.broadcasted_iota(jnp.int32, (half_seq, half_seq), 0)
    col_ids = lax.broadcasted_iota(jnp.int32, (half_seq, half_seq), 1)
    causal = row_ids >= col_ids

    def biased(raw, head, rows, cols):
        table = jnp.broadcast_to(bias_ref[pl.ds(head, 1), :], (half_seq, LANES))
        return raw * scale + jnp.take_along_axis(table, bucket_ref[rows, cols], axis=1)

    def softmax(blocks):
        peak = blocks[0].max(-1, keepdims=True)
        for b in blocks[1:]:
            peak = jnp.maximum(peak, b.max(-1, keepdims=True))
        exps = [jnp.exp(b - peak) for b in blocks]
        total = sum(x.sum(-1, keepdims=True) for x in exps)
        inverse = 1.0 / total
        return [x * inverse for x in exps]

    first, second = slice(0, half_seq), slice(half_seq, SEQ)

    def pair_step(pair, carry):
        lanes = pl.ds(pl.multiple_of(pair * 2 * DH, 2 * DH), 2 * DH)
        qp, kp, vp = q_ref[:, lanes], k_ref[:, lanes], v_ref[:, lanes]
        outs_low, outs_high = [], []
        for sub in range(2):
            head = pair * 2 + sub
            cut = slice(sub * DH, (sub + 1) * DH)
            q, k, v = qp[:, cut], kp[:, cut], vp[:, cut]
            s00 = biased(matmul_nt(q[first], k[first]), head, first, first)
            s1 = matmul_nt(q[second], k)
            s10 = biased(s1[:, first], head, second, first)
            s11 = biased(s1[:, second], head, second, second)
            (p00,) = softmax([jnp.where(causal, s00, -1e30)])
            p10, p11 = softmax([s10, jnp.where(causal, s11, -1e30)])
            low_ref[head] = p00
            high_ref[head, :, first] = p10
            high_ref[head, :, second] = p11
            outs_low.append(matmul(bf(p00), v[first]))
            outs_high.append(matmul(bf(p10), v[first]) + matmul(bf(p11), v[second]))
        att_ref[first, lanes] = bf(jnp.concatenate(outs_low, 1))
        att_ref[second, lanes] = bf(jnp.concatenate(outs_high, 1))
        return carry

    lax.fori_loop(0, H // 2, pair_step, 0)
    att_mine, att_other = att_ref[:, :half].astype(f32), att_ref[:, half:].astype(f32)
    flat_ref[:, :half] = bf(core_pick(core, att_mine, att_other))
    flat_ref[:, half:] = bf(core_pick(core, att_other, att_mine))
    flat = flat_ref[...]
    cut = slice(3 * half, 4 * half)
    out_mine, out_other = matmul(flat, mine_ref[:, cut]), matmul(flat, other_ref[:, cut])
    hidden_ref[:, :half] = hidden[:, :half] + core_pick(core, out_mine, out_other)
    hidden_ref[:, half:] = hidden[:, half:] + core_pick(core, out_other, out_mine)
    normed_two = bf(rms_apply(hidden_ref[...], gain_ref[1:2]))
    second_ref[...] = normed_two
    logits = matmul(normed_two, small)
    lane = lax.broadcasted_iota(jnp.int32, logits.shape, 1)
    chosen = [
        jnp.sum(jnp.where(lane == route_ref[:, k : k + 1], logits, 0.0), 1, keepdims=True)
        for k in range(2)
    ]
    peak = jnp.maximum(chosen[0], chosen[1])
    exps = [jnp.exp(c - peak) for c in chosen]
    total = exps[0] + exps[1]
    gate_ref[...] = jnp.where(lane == 0, exps[0] / total, jnp.where(lane == 1, exps[1] / total, 0.0))


def layer_forward(index, mine, other, tokens, buckets, routes, head_of, hot, experts):
    tok_count, width = tokens.shape
    b16, f32 = jnp.bfloat16, jnp.float32
    shaped = jax.ShapeDtypeStruct
    flat, total = shaped((tok_count, width), b16), mine[0].shape[-1] + mine[4].shape[-1]
    placed = mine[0].shape[2] % 16 == 0
    weights = (shaped((width, total), b16),) * 2
    if placed:
        inputs = tuple(mine) + tuple(other)
    else:
        inputs = tuple(
            jnp.concatenate([place(index, p[:4]), place(index, p[4:])], 1) for p in (mine, other)
        )
    tail = (tokens, buckets, routes, head_of, hot)
    result = pl.pallas_call(
        functools.partial(forward_kernel, placed, experts),
        out_shape=(weights if placed else ())
        + (flat, flat, flat, flat)
        + (shaped((H, SEQ // 2, SEQ // 2), f32), shaped((H, SEQ // 2, SEQ), f32), flat, flat)
        + (shaped((tok_count, width), f32), flat, shaped((tok_count, LANES), f32), shaped((2, width), f32)),
        in_specs=[SMEM] + [VMEM] * (len(inputs) + len(tail)),
        out_specs=(VMEM,) * (14 if placed else 12),
        scratch_shapes=[pltpu.VMEM((16, LANES), f32)],
        name="layer_forward",
    )(index, *inputs, *tail)
    return result if placed else inputs + result


def pick_rows(target_ref, k, count):
    ids = lax.broadcasted_iota(jnp.int32, (target_ref.shape[0], count), 1)
    return (ids == target_ref[:, k : k + 1]).astype(jnp.float32)


def join_pieces(pieces, out_ref):
    rows = pieces[0].shape[0]
    for i, piece in enumerate(pieces):
        out_ref[i * rows : (i + 1) * rows] = piece[...]


def combine_kernel(count, *refs):
    pieces, refs = refs[:count], refs[count:]
    target_ref, route_ref, gate_ref, cot_ref, hidden_ref, out_ref, logit_ref, ret_ref = refs
    join_pieces(pieces, ret_ref)
    gates = [gate_ref[:, k : k + 1] for k in range(2)]
    total = hidden_ref[...]
    backs = []
    for k in range(2):
        value = matmul(bf(pick_rows(target_ref, k, ret_ref.shape[0])), ret_ref[...])
        total += gates[k] * value
        backs.append(jnp.sum(cot_ref[...] * value, axis=1, keepdims=True))
    out_ref[...] = total
    mean = gates[0] * backs[0] + gates[1] * backs[1]
    lane = lax.broadcasted_iota(jnp.int32, logit_ref.shape, 1)
    logit = jnp.zeros(logit_ref.shape, jnp.float32)
    for k in range(2):
        logit += jnp.where(lane == route_ref[:, k : k + 1], gates[k] * (backs[k] - mean), 0.0)
    logit_ref[...] = bf(logit)


def joined_scratch(returned):
    rows = sum(r.shape[0] for r in returned)
    return pltpu.VMEM((rows, returned[0].shape[1]), jnp.bfloat16)


def combine(returned, targets, routes, gate_lanes, cot, hidden):
    shaped = jax.ShapeDtypeStruct
    return pl.pallas_call(
        functools.partial(combine_kernel, len(returned)),
        out_shape=(
            shaped(hidden.shape, jnp.float32),
            shaped((hidden.shape[0], LANES), jnp.bfloat16),
        ),
        in_specs=[VMEM] * (5 + len(returned)),
        out_specs=(VMEM,) * 2,
        scratch_shapes=[joined_scratch(returned)],
        name="combine_experts",
    )(*returned, targets, routes, gate_lanes, cot, hidden)


def pack_kernel(index_ref, q_ref, k_ref, v_ref, o_ref, router_ref, one_ref, two_ref, bias_ref, *outs):
    keep_a, keep_b, send_a, send_b, pad_ref = outs
    core, experts = index_ref[3], router_ref.shape[0]
    rows, width = q_ref.shape
    half = width // 2
    f32 = jnp.float32
    for i, ref in enumerate((q_ref, k_ref, v_ref, o_ref)):
        left, right = ref[:, :half].astype(f32), ref[:, half:].astype(f32)
        cut = slice(i % 2 * half, (i % 2 + 1) * half)
        (keep_a if i < 2 else keep_b)[:, cut] = bf(core_pick(core, left, right))
        (send_a if i < 2 else send_b)[:, cut] = bf(core_pick(core, right, left))
    pad_ref[...] = jnp.zeros(pad_ref.shape, f32)
    for i, ref in enumerate((one_ref, two_ref, bias_ref)):
        pad_ref[experts + i : experts + i + 1, : ref.shape[1]] = ref[...].astype(f32)
    pad_ref[:experts, :rows] = router_ref[...].astype(f32)
    small = bf(pad_ref[...].T[:rows])
    keep_b[:, width:] = small
    send_b[:, width:] = small


def pack(index, weights, router, vectors):
    rows, width = weights[0].shape
    out_a = jax.ShapeDtypeStruct((rows, width), jnp.bfloat16)
    out_b = jax.ShapeDtypeStruct((rows, width + LANES), jnp.bfloat16)
    return pl.pallas_call(
        pack_kernel,
        out_shape=(out_a, out_b) * 2,
        in_specs=[SMEM] + [VMEM] * 8,
        out_specs=(VMEM,) * 4,
        scratch_shapes=[pltpu.VMEM((LANES, LANES), jnp.float32)],
        name="pack_shards",
    )(index, *weights, router.T, *[v[None, :] for v in vectors])


def bias_kernel(index_ref, mine_ref, other_ref, hot_ref, head_ref, out_ref):
    f32 = jnp.float32
    core = index_ref[3]
    replicas, chips, rows, lanes = out_ref.shape
    lane = lax.broadcasted_iota(jnp.int32, (hot_ref.shape[0], lanes), 1)
    head = jnp.broadcast_to(head_ref[...].astype(f32), (lanes, lane.shape[0])).T.astype(jnp.int32)
    total = jnp.zeros(lane.shape, f32)
    for i, ref in enumerate((mine_ref, other_ref)):
        shifted = head + (core ^ i) * (H // 2)
        local = jnp.where(head < 0, -1, jnp.where(shifted >= H, shifted - H, shifted))
        rest = ref[...]
        for _ in range(2):
            part = bf(rest)
            rest = rest - part.astype(f32)
            spread = matmul(hot_ref[...], part)
            total += jnp.where((lane == local) | (lane == jnp.where(local < 0, -1, local + H)), spread, 0.0)
    column = jnp.sum(total, axis=1, keepdims=True)
    value = jnp.where(lane == index_ref[2] + 2, column, 0.0)
    for i in range(replicas):
        for j in range(chips):
            at = (i * chips + j) * rows
            out_ref[index_ref[0] ^ i, index_ref[1] ^ j] = value[at : at + rows]


def bias_blocks(index, mine, other, hot, head_of, chips, replicas):
    rows = hot.shape[0] // (replicas * chips)
    return pl.pallas_call(
        bias_kernel,
        out_shape=jax.ShapeDtypeStruct((replicas, chips, rows, LANES), jnp.float32),
        in_specs=[SMEM] + [VMEM] * 4,
        out_specs=VMEM,
        name="bias_column",
    )(index, mine, other, hot, head_of)


def finish_kernel(index_ref, mine_a, got_a, mine_b, got_b, q_ref, k_ref, v_ref, o_ref, router_ref, *vector_refs):
    core, experts = index_ref[3], router_ref.shape[0]
    rows, width = q_ref.shape
    half = width // 2
    for i, ref in enumerate((q_ref, k_ref, v_ref, o_ref)):
        cut = slice(i % 2 * half, (i % 2 + 1) * half)
        mine_ref, got_ref = (mine_a, got_a) if i < 2 else (mine_b, got_b)
        mine, other = mine_ref[:, cut], got_ref[:, cut].astype(jnp.float32)
        ref[:, :half] = core_pick(core, mine, other)
        ref[:, half:] = core_pick(core, other, mine)
    small = mine_b[:, width:]
    padded = jnp.concatenate([small, jnp.zeros((LANES - rows, LANES), jnp.float32)], 0).T
    router_ref[...] = padded[:experts, :rows]
    for i, ref in enumerate(vector_refs):
        ref[...] = padded[experts + i : experts + i + 1, : ref.shape[1]]


def finish(index, groups, experts, n_bias):
    rows, width = groups[0].shape
    shaped = lambda *dims: jax.ShapeDtypeStruct(dims, jnp.float32)
    return pl.pallas_call(
        finish_kernel,
        out_shape=(shaped(rows, width),) * 4
        + (shaped(experts, rows), shaped(1, rows), shaped(1, rows), shaped(1, n_bias)),
        in_specs=[SMEM] + [VMEM] * 4,
        out_specs=(VMEM,) * 8,
        name="finish_shared",
    )(index, *groups)


def backward_kernel(count, index_ref, *refs):
    pieces, refs = refs[:count], refs[count:]
    target_ref, logit_ref, cot_ref, hidden_ref, *refs = refs
    (
        second_ref, flat_ref, att_ref, low_ref, high_ref,
        n_ref, q_ref, k_ref, v_ref, mine_ref, other_ref, tok_ref, gain_ref,
        keep_a, keep_b, keep_c, send_a, send_b, send_c, grad_ref, score_ref,
        qb_ref, kb_ref, vb_ref, ab_ref, ret_ref,
    ) = refs
    f32 = jnp.float32
    half_seq = SEQ // 2
    scale = 1.0 / math.sqrt(DH)
    first, second = slice(0, half_seq), slice(half_seq, SEQ)
    half = ab_ref.shape[1] // 2
    replicas, chips, rows, _ = keep_a.shape
    dp_index, chip_index, experts, core = (index_ref[i] for i in range(4))
    payload = 4 * half

    def store(kept, sent, part):
        at = part % 2 * half
        cut = slice(at, at + kept.shape[1])
        outs = ((keep_a, send_a), (keep_b, send_b), (keep_c, send_c))[part // 2]
        for out, value in zip(outs, (bf(kept), bf(sent))):
            for i in range(replicas):
                for j in range(chips):
                    at = (i * chips + j) * rows
                    out[dp_index ^ i, chip_index ^ j, :, cut] = value[at : at + rows]

    def norm_back(hidden, gain, upstream):
        factor = lax.rsqrt(jnp.mean(hidden * hidden, axis=-1, keepdims=True) + EPSILON)
        scaled = upstream * gain
        inner = jnp.mean(scaled * hidden, axis=-1, keepdims=True)
        gain_back = jnp.sum(upstream * (hidden * factor), axis=0, keepdims=True)
        return factor * (scaled - hidden * (factor * factor * inner)), gain_back

    join_pieces(pieces, ret_ref)
    picked = pick_rows(target_ref, 0, ret_ref.shape[0]) + pick_rows(target_ref, 1, ret_ref.shape[0])
    token_back = matmul(bf(picked), ret_ref[...])
    logit_back = logit_ref[...]
    small_w = mine_ref[:, payload:]
    hidden_back, gain_two_back = norm_back(
        hidden_ref[...], gain_ref[1:2], token_back + matmul_nt(logit_back, small_w)
    )
    hidden_back = cot_ref[...] + hidden_back
    grad_ref[...] = hidden_back
    left, right = hidden_back[:, :half], hidden_back[:, half:]
    res_mine, res_other = bf(core_pick(core, left, right)), bf(core_pick(core, right, left))
    cut = slice(3 * half, payload)
    ab = matmul_nt(res_mine, mine_ref[:, cut]) + matmul_nt(res_other, other_ref[:, cut])
    left, right = ab[:, :half], ab[:, half:]
    ab_ref[:, :half] = bf(core_pick(core, left, right))
    ab_ref[:, half:] = bf(core_pick(core, right, left))
    flat = flat_ref[...]
    store(matmul_tn(flat, res_mine), matmul_tn(flat, res_other), 3)

    def pair_step(pair, carry):
        lanes = pl.ds(pl.multiple_of(pair * 2 * DH, 2 * DH), 2 * DH)
        qp, kp, vp = q_ref[:, lanes], k_ref[:, lanes], v_ref[:, lanes]
        abp, attp = ab_ref[:, lanes], att_ref[:, lanes]
        found = [[], [], []]
        for sub in range(2):
            head = pair * 2 + sub
            cut = slice(sub * DH, (sub + 1) * DH)
            q, k, v, ab, att = qp[:, cut], kp[:, cut], vp[:, cut], abp[:, cut], attp[:, cut]
            delta = jnp.sum(ab.astype(f32) * att.astype(f32), axis=1, keepdims=True)
            low, high = low_ref[head], high_ref[head]
            low_b, high_b = bf(low), bf(high)
            value_low = matmul_tn(low_b, ab[first])
            value_high = matmul_tn(high_b, ab[second])
            found[2].append(
                jnp.concatenate([value_low + value_high[first], value_high[second]], 0)
            )
            back_low = low * (matmul_nt(ab[first], v[first]) - delta[first])
            back_high = high * (matmul_nt(ab[second], v) - delta[second])
            low_r, high_r = bf(back_low), bf(back_high)
            for at, low_s, high_s in (
                (head, low_r, high_r),
                (head + H, bf(back_low - low_r.astype(f32)), bf(back_high - high_r.astype(f32))),
            ):
                score_ref[at, first, first] = low_s
                score_ref[at, first, second] = jnp.zeros_like(low_s)
                score_ref[at, second, :] = high_s
            found[0].append(
                jnp.concatenate([matmul(low_r, k[first]), matmul(high_r, k)], 0) * scale
            )
            key_low = matmul_tn(low_r, q[first])
            key_high = matmul_tn(high_r, q[second])
            found[1].append(
                jnp.concatenate([key_low + key_high[first], key_high[second]], 0) * scale
            )
        for out, value in zip((qb_ref, kb_ref, vb_ref), found):
            out[:, lanes] = bf(jnp.concatenate(value, 1))
        return carry

    lax.fori_loop(0, H // 2, pair_step, 0)

    normed = n_ref[...]
    normed_back = jnp.zeros(tok_ref.shape, f32)
    for part, ref in enumerate((qb_ref, kb_ref, vb_ref)):
        cut = slice(part * half, (part + 1) * half)
        mine_b, other_b = ref[:, :half], ref[:, half:]
        store(matmul_tn(normed, mine_b), matmul_tn(normed, other_b), part)
        normed_back += matmul_nt(mine_b, mine_ref[:, cut]) + matmul_nt(other_b, other_ref[:, cut])
    token_back, gain_one_back = norm_back(tok_ref[...].astype(f32), gain_ref[0:1], normed_back)
    grad_ref[...] += token_back
    small = matmul_tn(second_ref[...], logit_back)
    lane = lax.broadcasted_iota(jnp.int32, small.shape, 1)
    for at, gain_back in ((experts, gain_one_back), (experts + 1, gain_two_back)):
        wide = jnp.broadcast_to(gain_back, (LANES, gain_back.shape[1])).T
        small = jnp.where(lane == at, wide, small)
    store(small, small, 4)


def layer_backward(index, returned, targets, logit_back, cot, forward, tokens, chips, replicas):
    mine, other, normed, q, k, v, low, high, att, flat, hidden, second, _, gains = forward
    tok_count, width = tokens.shape
    b16, f32 = jnp.bfloat16, jnp.float32
    shaped = jax.ShapeDtypeStruct
    blocks = (replicas, chips, width // (replicas * chips))
    groups = tuple(shaped(blocks + (w,), b16) for w in (width, width, LANES))
    return pl.pallas_call(
        functools.partial(backward_kernel, len(returned)),
        out_shape=groups
        + groups
        + (
            shaped((tok_count, width), f32),
            shaped((2 * H, SEQ, SEQ), b16),
        ),
        in_specs=[SMEM] + [VMEM] * (17 + len(returned)),
        out_specs=(VMEM,) * 8,
        scratch_shapes=[pltpu.VMEM((tok_count, width), b16)] * 4 + [joined_scratch(returned)],
        name="layer_backward",
    )(
        index, *returned, targets, logit_back, cot, hidden, second, flat, att, low, high, normed, q, k, v,
        mine, other, tokens, gains,
    )


def core_join(mine, other, core, axis=1):
    return jnp.concatenate(
        [jnp.where(core == 0, mine, other), jnp.where(core == 0, other, mine)], axis
    )


def gather_pieces(keep, send, chips, core):
    got = swap(send, "expert", 1)
    block = core_join(keep, got, core, 0)
    found = chip_gather(block, chips)
    pieces = []
    for parity, part in enumerate((found[: chips // 2], found[chips // 2 :])):
        first, second = dp_steps(parity)
        part = jnp.stack(part)
        near = jnp.stack([part, swap(part, "dp", first)])
        far = swap(near, "dp", second)
        pieces += [near, far]
    return pieces


def partner_pieces(pieces):
    result = []
    for piece in pieces:
        result.append(swap(piece, "expert", 1))
    return result


def core_sum_kernel(with_extra, keep_ref, got_ref, *refs):
    f32 = jnp.float32
    extra_ref, refs = (refs[0], refs[1:]) if with_extra else (None, refs)
    _, chips = keep_ref.shape[:2]
    half = chips // 2
    for parity in range(2):
        held_ref, sent_ref = refs[2 * parity : 2 * parity + 2]
        second, first = dp_steps(parity)
        for out, at in ((held_ref, (0, second)), (sent_ref, (first, first | second))):
            for i in range(2):
                for j in range(half):
                    chip = parity * half + j
                    total = keep_ref[at[i], chip].astype(f32) + got_ref[at[i], chip].astype(f32)
                    if with_extra:
                        total = total + extra_ref[at[i], chip]
                    out[i, j] = total.astype(out.dtype)


def core_sum(keep, got, extra):
    _, chips, rows, width = keep.shape
    shaped = functools.partial(jax.ShapeDtypeStruct, (2, chips // 2, rows, width))
    inputs = (keep, got) + (() if extra is None else (extra,))
    return pl.pallas_call(
        functools.partial(core_sum_kernel, extra is not None),
        out_shape=(shaped(jnp.float32), shaped(jnp.bfloat16)) * 2,
        in_specs=[VMEM] * len(inputs),
        out_specs=(VMEM,) * 4,
        name="core_sum",
    )(*inputs)


def reduce_dp(keep, send, extra, chips):
    got = swap(send, "expert", 1)
    parts = core_sum(keep, got, extra)
    result = []
    for parity in range(2):
        held, sent = parts[2 * parity : 2 * parity + 2]
        total = dp_finish(held, sent, parity)
        result += [total[k] for k in range(chips // 2)]
    return result


def reduce_chips(chip_blocks, core):
    arrived = [
        swap(bf(chip_blocks[k]), "expert", 2 * k) for k in range(1, len(chip_blocks))
    ]
    block = chip_blocks[0]
    for piece in arrived:
        block = block + piece.astype(jnp.float32)
    rows = block.shape[0] // 2
    mine = jnp.where(core == 0, block[:rows], block[rows:])
    theirs = jnp.where(core == 0, block[rows:], block[:rows])
    got = swap(bf(theirs), "expert", 1)
    return mine, got


def slot_positions(routes, experts):
    flat = routes.reshape(-1)
    expert_hot = (flat[:, None] == jnp.arange(experts, dtype=jnp.int32)[None, :]).astype(jnp.int32)
    earlier = jnp.cumsum(expert_hot, axis=0) - expert_hot
    return jnp.sum(earlier * expert_hot, axis=1).reshape(routes.shape)


def per_device(
    tokens,
    cotangent,
    buckets,
    routes,
    gain_attn,
    gain_moe,
    rel_bias,
    w_query,
    w_key,
    w_value,
    w_out,
    w_router,
    w_gate,
    w_up,
    w_down,
):
    f32 = jnp.float32
    groups = lax.axis_size("expert")
    chips = groups // 2
    replicas = lax.axis_size("dp")
    expert_index, dp_index = lax.axis_index("expert"), lax.axis_index("dp")
    core, chip_index = expert_index & 1, expert_index >> 1

    shard_rows = w_query.shape[0]
    experts = w_router.shape[1]
    n_bias = rel_bias.shape[0]
    model_width = tokens.shape[1]
    index = jnp.stack([dp_index, chip_index, jnp.int32(experts), core]).astype(jnp.int32)
    keep_a, keep_b, send_a, send_b = pack(
        index,
        (w_query, w_key, w_value, w_out),
        w_router,
        (gain_attn, gain_moe, rel_bias),
    )
    pieces = gather_pieces(keep_a, send_a, chips, core)
    pieces += gather_pieces(keep_b, send_b, chips, core)
    others = partner_pieces(pieces[:4]) + partner_pieces(pieces[4:])
    lane_ids = jnp.arange(model_width, dtype=jnp.int32)
    in_row = lane_ids % shard_rows
    flat_at = jnp.where(in_row < n_bias, lane_ids // shard_rows * n_bias + in_row, -1)
    head_of = jnp.where(flat_at >= 0, flat_at % H, -1)[None, :]
    bucket_of = jnp.where(flat_at >= 0, flat_at // H, -1)[:, None]
    hot = bf(bucket_of == jnp.arange(LANES, dtype=jnp.int32)[None, :])

    tok_count = tokens.shape[0]
    local_experts = w_gate.shape[0]
    capacity = max(2, 9 * tok_count // (4 * experts))
    unit = 2 * capacity
    chip_unit = local_experts * unit
    n_rows = chips * chip_unit
    group = routes // local_experts
    rel_core = (group & 1) ^ core
    rel_chip = (group >> 1) ^ chip_index
    targets = (
        rel_core * n_rows
        + rel_chip * chip_unit
        + (routes % local_experts) * unit
        + rel_core * capacity
        + slot_positions(routes, experts)
    )
    partner_targets = swap(targets, "expert", 1)
    partner_cot = swap(cotangent, "expert", 1)
    row_ids = jnp.arange(n_rows, dtype=jnp.int32)
    pick_own = [bf(row_ids[:, None] == targets[None, :, k]) for k in range(2)]
    pick_partner = [bf(row_ids[:, None] + n_rows == partner_targets[None, :, k]) for k in range(2)]

    forward = layer_forward(index, pieces, others, tokens, buckets, routes, head_of, hot, experts)
    hidden_one, normed_two, gate_lanes = forward[10:13]
    partner_normed = swap(normed_two, "expert", 1)
    partner_gates = swap(gate_lanes, "expert", 1)
    gates = gate_lanes[:, :2]

    def dispatch(rows, split):
        def piece(k, e):
            at = k * chip_unit + e * unit
            return rows[at : at + unit]

        found = []
        if split:
            for e in range(local_experts):
                found.append(
                    [piece(0, e)] + [swap(piece(k, e), "expert", 2 * k) for k in range(1, chips)]
                )
        else:
            whole = [
                swap(rows[k * chip_unit : (k + 1) * chip_unit], "expert", 2 * k)
                for k in range(1, chips)
            ]
            for e in range(local_experts):
                found.append([piece(0, e)] + [w[e * unit : (e + 1) * unit] for w in whole])
        result = []
        for e in range(local_experts):
            block = jnp.concatenate(found[e], 0)
            if split:
                middle = block.shape[0] // 2
                halves = [dp_gather(block[:middle], 0), dp_gather(block[middle:], 1)]
                result.append([part for pair in zip(*halves) for part in pair])
            else:
                result.append(dp_gather(block, e % 2))
        return result

    picks = jnp.concatenate([pick_own[0] + pick_own[1], pick_partner[0] + pick_partner[1]], 1)
    picked = bf(matmul(picks, jnp.concatenate([normed_two, partner_normed], 0)))
    rows = dispatch(picked, True)
    grad_picks = jnp.concatenate(pick_own + pick_partner, 1)
    gated = [bf(gates[:, k : k + 1] * cotangent) for k in range(2)]
    gated += [bf(partner_gates[:, k : k + 1] * partner_cot) for k in range(2)]
    picked = bf(matmul(grad_picks, jnp.concatenate(gated, 0)))
    grads = dispatch(picked, False)

    def reduce_rows(parts, e):
        split = parts.reshape(replicas, chips * unit, model_width)
        total = dp_reduce([split[k] for k in range(replicas)], e % 2)
        return bf(total)

    def send_home(totals):
        found = [
            jnp.concatenate([t[k * unit : (k + 1) * unit] for t in totals], 0)
            for k in range(chips)
        ]
        found = found[:1] + [swap(found[k], "expert", 2 * k) for k in range(1, chips)]
        if found[0].shape[0] % 16 != 0:
            found = [jnp.concatenate(found, 0)]
        return found + [swap(piece, "expert", 1) for piece in found]

    rows_e = [jnp.concatenate(rows[e], 0) for e in range(local_experts)]
    grads_e = [jnp.concatenate(grads[e], 0) for e in range(local_experts)]
    acts, saved, out_totals = [], [], []
    for e in range(local_experts):
        gate_pre = matmul(rows_e[e], w_gate[e])
        up_pre = matmul(rows_e[e], w_up[e])
        act = bf(geglu(gate_pre, up_pre))
        act, gate_pre, up_pre = lax.optimization_barrier((act, gate_pre, up_pre))
        acts.append(act)
        saved.append((gate_pre, up_pre))
        part = matmul_nt(act, w_down[e])
        out_totals.append(reduce_rows(part, e))
    back_totals, pres = [], []
    for e in range(local_experts):
        _, vjp = jax.vjp(geglu, *saved[e])
        gate_back_pre, up_back_pre = vjp(matmul(grads_e[e], w_down[e]))
        gate_back_pre, up_back_pre = bf(gate_back_pre), bf(up_back_pre)
        pres.append((gate_back_pre, up_back_pre))
        part = matmul_nt(gate_back_pre, w_gate[e]) + matmul_nt(up_back_pre, w_up[e])
        back_totals.append(reduce_rows(part, e))
    down_grad = jnp.stack([matmul_tn(grads_e[e], acts[e]) for e in range(local_experts)])
    gate_grad = jnp.stack([matmul_tn(rows_e[e], pres[e][0]) for e in range(local_experts)])
    up_grad = jnp.stack([matmul_tn(rows_e[e], pres[e][1]) for e in range(local_experts)])

    returned = send_home(out_totals)
    back_rows = send_home(back_totals)
    late_cot, *returned = lax.optimization_barrier((cotangent, *returned))
    layer_out, logit_back = combine(returned, targets, routes, gate_lanes, late_cot, hidden_one)
    *shared, tokens_grad, score_back = layer_backward(
        index, back_rows, targets, logit_back, late_cot, forward, tokens, chips, replicas
    )
    bucket_hot = bf(buckets[None] == jnp.arange(NB, dtype=jnp.int32)[:, None, None])
    bias_grad = lax.dot_general(
        bucket_hot, score_back, (((1, 2), (1, 2)), ((), ())), preferred_element_type=f32
    )
    bias_grad = jnp.pad(bias_grad, ((0, LANES - NB), (0, LANES - 2 * H)))
    extra = bias_blocks(
        index, bias_grad, swap(bias_grad, "expert", 1), hot, head_of, chips, replicas
    )
    keep_a, keep_b, keep_c, send_a, send_b, send_c = shared
    groups = reduce_chips(reduce_dp(keep_a, send_a, None, chips), core)
    blocks_b = reduce_dp(keep_b, send_b, None, chips)
    blocks_c = reduce_dp(keep_c, send_c, extra, chips)
    joined = [jnp.concatenate(pair, 1) for pair in zip(blocks_b, blocks_c)]
    groups += reduce_chips(joined, core)
    query_total, key_total, value_total, out_total, router_total, *vectors = finish(
        index, groups, experts, n_bias
    )
    return (
        layer_out,
        tokens_grad,
        vectors[0].reshape(-1),
        vectors[1].reshape(-1),
        vectors[2].reshape(-1),
        query_total,
        key_total,
        value_total,
        out_total,
        router_total.T,
        gate_grad,
        up_grad,
        down_grad,
    )


def solution(mesh):
    both = ("dp", "expert")
    row = P(both, None)

    return jax.shard_map(
        per_device,
        mesh=mesh,
        in_specs=(row, row, P(), row, P(both), P(both), P(both), row, row, row, row, row)
        + (P("expert", None, "dp"),) * 3,
        out_specs=(row, row, P(both), P(both), P(both), row, row, row, row, row)
        + (P("expert", None, "dp"),) * 3,
        check_vma=False,
    )
```
